32 devices in a mesh: fsdp: 8 (over y, x, core), tensor: 4 (over z).
Axes of the slice: x: 2, y: 2, z: 4, core: 2. Of those that a mesh axis runs over, the one named last changes fastest.
Arguments:
- tokens: bfloat16 [16384, 768], P(('fsdp', 'tensor')), may hold values from -6 to 6
- cotangent: bfloat16 [16384, 768], P(('fsdp', 'tensor')), may hold values from -6 to 6
- w_query: bfloat16 [768, 768], P('fsdp', 'tensor'), may hold values from -0.21875 to 0.21875
- w_key: bfloat16 [768, 768], P('fsdp', 'tensor'), may hold values from -0.21875 to 0.21875
- w_value: bfloat16 [768, 768], P('fsdp', 'tensor'), may hold values from -0.21875 to 0.21875
- w_out: bfloat16 [768, 768], P('tensor', 'fsdp'), may hold values from -6 to 6
- w_up: bfloat16 [768, 3072], P('fsdp', 'tensor'), may hold values from -0.21875 to 0.21875
- w_down: bfloat16 [3072, 768], P('tensor', 'fsdp'), may hold values from -0.109375 to 0.109375
- b_query: bfloat16 [768], P(('tensor', 'fsdp')), may hold values from -3 to 3
- b_value: bfloat16 [768], P(('tensor', 'fsdp')), may hold values from -0.1875 to 0.1875
- b_up: bfloat16 [3072], P(('tensor', 'fsdp')), may hold values from -3 to 3
- b_out: bfloat16 [768], P('fsdp'), may hold values from -1.25 to 1.25
- b_down: bfloat16 [768], P('fsdp'), may hold values from -1.25 to 1.25
- gain_attn: bfloat16 [768], P('fsdp'), may hold values from 0.5 to 1.5
- shift_attn: bfloat16 [768], P('fsdp'), may hold values from -1.25 to 1.25
- gain_ffn: bfloat16 [768], P('fsdp'), may hold values from 0.5 to 1.5
- shift_ffn: bfloat16 [768], P('fsdp'), may hold values from -1.25 to 1.25
Outputs:
- output: float32 [16384, 768], P(('fsdp', 'tensor'))
- grad_tokens: float32 [16384, 768], P(('fsdp', 'tensor'))
- grad_w_query: float32 [768, 768], P('fsdp', 'tensor')
- grad_w_key: float32 [768, 768], P('fsdp', 'tensor')
- grad_w_value: float32 [768, 768], P('fsdp', 'tensor')
- grad_w_out: float32 [768, 768], P('tensor', 'fsdp')
- grad_w_up: float32 [768, 3072], P('fsdp', 'tensor')
- grad_w_down: float32 [3072, 768], P('tensor', 'fsdp')
- grad_b_query: float32 [768], P(('tensor', 'fsdp'))
- grad_b_value: float32 [768], P(('tensor', 'fsdp'))
- grad_b_up: float32 [3072], P(('tensor', 'fsdp'))
- grad_b_out: float32 [768], P('fsdp')
- grad_b_down: float32 [768], P('fsdp')
- grad_gain_attn: float32 [768], P('fsdp')
- grad_shift_attn: float32 [768], P('fsdp')
- grad_gain_ffn: float32 [768], P('fsdp')
- grad_shift_ffn: float32 [768], P('fsdp')
The draws below stay inside these ranges and needn't reach their ends.
All inputs are finite; a program needn't handle non-finite values.
Results may differ from the reference program's by a relative error of at most 0.02.
Values may be sent and summed in bfloat16 or wider, within the bound.
A program may use at most 128 MiB of HBM per device.

```python
import jax
import jax.numpy as jnp
from jax import lax

D = 768
HEADS = 12
HEAD = 64
FF = 3072
LEN = 2048
TOKENS = 16384
N_FSDP = 8


def shard_levels(rng, shape, pieces, smallest, top_value):
    def one(dim, parts):
        steps = jax.random.uniform(jax.random.fold_in(jax.random.fold_in(rng, 6), dim), (parts,), jnp.float32, smallest / len(pieces), top_value / len(pieces))
        return jnp.repeat(jnp.exp(steps), shape[dim] // parts).reshape((-1,) + (1,) * (len(shape) - dim - 1))

    loudness = one(*pieces[0])
    for cut in pieces[1:]:
        loudness = loudness * one(*cut)
    return loudness


def scatter_about(stream_key, dims, width, limit, split=(), held_as=jnp.bfloat16):
    level = shard_levels(stream_key, dims, split, -0.22, 0.18) if split else 1.0
    array = jax.random.normal(stream_key, dims, jnp.float32) * width * level
    return jnp.minimum(jnp.maximum(array, -limit), limit).astype(held_as)


def setup_inputs(seed: int = 0) -> dict:
    splits = jax.random.split(jax.random.key(seed), 18)
    return {
        "tokens": scatter_about(splits[0], (TOKENS, D), 1.0, 6.0, ((0, 32),)),
        "cotangent": scatter_about(splits[1], (TOKENS, D), 1.0, 6.0, ((0, 32),)),
        "w_query": scatter_about(splits[2], (D, D), D ** -0.5, 0.21875, ((0, 8), (1, 4))),
        "w_key": scatter_about(splits[3], (D, D), D ** -0.5, 0.21875, ((0, 8), (1, 4))),
        "w_value": scatter_about(splits[4], (D, D), D ** -0.5, 0.21875, ((0, 8), (1, 4))),
        "w_out": scatter_about(splits[5], (D, D), (max(1, 3 * D // LEN)) ** -0.5, 6.0, ((0, 4), (1, 8))),
        "w_up": scatter_about(splits[6], (D, FF), D ** -0.5, 0.21875, ((0, 8), (1, 4))),
        "w_down": scatter_about(splits[7], (FF, D), FF ** -0.5, 0.109375, ((0, 4), (1, 8))),
        "b_query": scatter_about(splits[8], (D,), 0.5, 3.0, ((0, 32),)),
        "b_value": scatter_about(splits[9], (D,), 0.03, 0.1875, ((0, 32),)),
        "b_up": scatter_about(splits[10], (FF,), 0.5, 3.0, ((0, 32),)),
        "b_out": scatter_about(splits[11], (D,), 0.2, 1.25, ((0, 8),)),
        "b_down": scatter_about(splits[12], (D,), 0.2, 1.25, ((0, 8),)),
        "gain_attn": jnp.clip(1.0 + 0.1 * jax.random.normal(splits[13], (D,), jnp.float32), 0.5, 1.5).astype(jnp.bfloat16),
        "shift_attn": scatter_about(splits[14], (D,), 0.2, 1.25, ((0, 8),)),
        "gain_ffn": jnp.clip(1.0 + 0.1 * jax.random.normal(splits[15], (D,), jnp.float32), 0.5, 1.5).astype(jnp.bfloat16),
        "shift_ffn": scatter_about(splits[16], (D,), 0.2, 1.25, ((0, 8),)),
    }


@jax.custom_vjp
def low(v):
    return lax.optimization_barrier(v.astype(jnp.bfloat16)).astype(jnp.float32)

@jax.custom_vjp
def low_back(v):
    return v

def low_keep(v):
    return (low(v), None)

def low_pass(kept, grad):
    return (grad,)

def back_keep(v):
    return (v, None)

def back_low(kept, grad):
    return (low(grad),)
low.defvjp(low_keep, low_pass)
low_back.defvjp(back_keep, back_low)
EPSILON = 1e-12
PRECISE = lax.Precision.HIGHEST

def product(left, right):
    return jnp.dot(left, right, precision=PRECISE, preferred_element_type=jnp.float32)

def norm_rows(values, gain, shift):
    average = lax.optimization_barrier(jnp.mean(values, -1, keepdims=True))
    centered = values - average
    inverse = lax.rsqrt(lax.optimization_barrier(jnp.mean(centered * centered, -1, keepdims=True)) + EPSILON)
    return centered * inverse * gain + shift

def attend(query, keys, values):
    length = query.shape[0]
    span = min(512, length)
    blocks = query.reshape(length // span, span, HEADS, HEAD)

    def one_block(piece):
        scores = jnp.einsum('qhd,khd->hqk', piece, keys, precision=PRECISE) * HEAD ** (-0.5)
        attention = low(jax.nn.softmax(low_back(scores), axis=-1))
        return jnp.einsum('hqk,khd->qhd', attention, values, precision=PRECISE)
    return lax.map(jax.checkpoint(one_block), blocks).reshape(length, HEADS * HEAD)

def sequence(sequence_in, weights):
    w_query, w_key, w_value, w_out, w_up, w_down, b_query, b_value, b_up, b_out, b_down, gain_attn, shift_attn, gain_ffn, shift_ffn = weights
    query = low_back(low(product(sequence_in, w_query) + b_query))
    keys = low_back(low(product(sequence_in, w_key)))
    values = low_back(low(product(sequence_in, w_value) + b_value))
    heads_shape = (sequence_in.shape[0], HEADS, HEAD)
    attended = attend(query.reshape(heads_shape), keys.reshape(heads_shape), values.reshape(heads_shape))
    attended = low_back(low(attended))
    branch = low_back(product(attended, w_out) + b_out)
    hidden = norm_rows(sequence_in + branch, gain_attn, shift_attn)
    pre_act = low_back(product(low(hidden), w_up) + b_up)
    activ = low(jax.nn.gelu(pre_act, approximate=False))
    ffn = low_back(product(activ, w_down) + b_down)
    return norm_rows(hidden + ffn, gain_ffn, shift_ffn)

def reference(tokens, cotangent, w_query, w_key, w_value, w_out, w_up, w_down, b_query, b_value, b_up, b_out, b_down, gain_attn, shift_attn, gain_ffn, shift_ffn):
    params = tuple((item.astype(jnp.float32) for item in (w_query, w_key, w_value, w_out, w_up, w_down, b_query, b_value, b_up, b_out, b_down, gain_attn, shift_attn, gain_ffn, shift_ffn)))

    def layer(inputs, *weights):

        def run_sequence(sequence_in):
            return sequence(sequence_in, weights)
        stacked = inputs.reshape(N_FSDP, LEN, D)
        return lax.map(jax.checkpoint(run_sequence), stacked).reshape(TOKENS, D)
    result, backward = jax.vjp(layer, tokens.astype(jnp.float32), *params)
    gradients = backward(cotangent.astype(jnp.float32))
    return (result, gradients[0], gradients[1], gradients[2], gradients[3], gradients[4], gradients[5], gradients[6], gradients[7], gradients[8], gradients[9], gradients[10], gradients[11], gradients[12], gradients[13], gradients[14], gradients[15])
```

```python
import functools

import jax
import jax.numpy as jnp
import numpy as np
from jax import lax
from jax.experimental import pallas as pl
from jax.experimental.pallas import tpu as pltpu
from jax.sharding import PartitionSpec as P

F32, BF16 = jnp.float32, jnp.bfloat16
HEAD = 64
EPSILON = 1e-12
VMEM_LIMIT = 64000 * 1024


def dot(left, right, contract):
    return lax.dot_general(left, right, ((contract[:1], contract[1:]), ((), ())), preferred_element_type=F32)

NN, NT, TN = (1, 0), (1, 1), (0, 0)


def lanes_from(shape, low):
    return lax.broadcasted_iota(jnp.int32, shape, len(shape) - 1) % (2 * HEAD) >= HEAD if not low else \
        lax.broadcasted_iota(jnp.int32, shape, len(shape) - 1) % (2 * HEAD) < HEAD


def project_keys(x, w, bias):
    return (dot(x, w, NN) + bias).astype(BF16)


def project_query(x, w, bias):
    out = dot(x, w, NN) + bias
    return jnp.where(lanes_from(out.shape, True), out.astype(BF16) * BF16(HEAD ** -0.5), BF16(0))


def attend_kernel(heads, x_all, x_own, w_kv, w_qo, b_kv, b_q, kv_out, q_out, att_out, inv_out, exp_out, s_ref):
    kv_out[0] = project_keys(x_all[...], w_kv[0], b_kv[0])
    q_out[0] = project_query(x_own[...], w_qo[0], b_q[0])
    for h in range(heads):
        cols = slice(h * 128, h * 128 + 128)
        kv = kv_out[0, :, cols]
        s_ref[...] = dot(kv, q_out[0, :, cols], NT)
        top = jnp.max(s_ref[...], axis=0, keepdims=True)
        exps = jnp.exp(s_ref[...] - top)
        inv = 1.0 / jnp.sum(exps, axis=0, keepdims=True)
        exp_out[0, h] = exps.astype(BF16)
        out = dot(kv, exp_out[0, h], TN) * inv
        out = jnp.where(lax.broadcasted_iota(jnp.int32, out.shape, 0) >= HEAD, out, 0.0)
        att_out[0, :, cols] = out.T.astype(BF16)
        inv_out[0, h:h + 1] = inv


def attend(x_all, x_own, w_kv, w_qo, b_kv, b_q):
    groups, model, width = w_kv.shape
    heads = width // 128
    keys, rows = x_all.shape[0], x_own.shape[0]
    whole = lambda n: pl.BlockSpec((n, model), lambda g: (0, 0))
    lead = lambda *s: pl.BlockSpec((1, *s), lambda g: (g, *[0] * len(s)))
    return pl.pallas_call(
        functools.partial(attend_kernel, heads),
        grid=(groups,),
        in_specs=[whole(keys), whole(rows), lead(model, width), lead(model, width), lead(1, width), lead(1, width)],
        out_specs=[lead(keys, width), lead(rows, width), lead(rows, width), lead(8, rows), lead(heads, keys, rows)],
        out_shape=[jax.ShapeDtypeStruct(s, d) for s, d in [
            ((groups, keys, width), BF16), ((groups, rows, width), BF16), ((groups, rows, width), BF16),
            ((groups, 8, rows), F32), ((groups, heads, keys, rows), BF16)]],
        scratch_shapes=[pltpu.VMEM((keys, rows), F32)],
        compiler_params=pltpu.CompilerParams(vmem_limit_bytes=VMEM_LIMIT),
    )(x_all, x_own, w_kv, w_qo, b_kv, b_q)


def norm_forward(z):
    mean = jnp.mean(z, -1, keepdims=True)
    centered = z - mean
    inv = lax.rsqrt(jnp.mean(centered * centered, -1, keepdims=True) + EPSILON)
    return centered * inv, inv


def norm_backward(n, inv, dn):
    return inv * (dn - jnp.mean(dn, -1, keepdims=True) - n * jnp.mean(dn * n, -1, keepdims=True))


def colsum(x):
    return jnp.sum(x.astype(F32), axis=0, keepdims=True)


def ffn_kernel(groups, x_own, cot, att, w_qo, w_up0, w_up1, w_dn0, w_dn1, b_up, vecs,
               out_ref, resid_ref, datt_ref, g_o, g_up0, g_up1, g_dn0, g_dn1, g_bup, g_vecs,
               act_ref, slope_ref, hid_ref, n1_ref, acc_ref, low_ref, hl_ref):
    ups, downs, g_ups, g_dns = (w_up0, w_up1), (w_dn0, w_dn1), (g_up0, g_up1), (g_dn0, g_dn1)
    vec = lambda k: vecs[k:k + 1, :]
    width = w_up0.shape[2]
    acc_ref[...] = x_own[...].astype(F32) + vec(0)
    def branch(g, c):
        acc_ref[...] += dot(att[g], w_qo[g], NT)
        return c
    lax.fori_loop(0, groups, branch, 0)
    n1, inv1 = norm_forward(acc_ref[...])
    n1_ref[...] = n1
    hidden = n1 * vec(2) + vec(3)
    hid_ref[...] = hidden
    hl_ref[...] = hidden.astype(BF16)
    acc_ref[...] = hidden + vec(1)
    def forward(g, c):
        for k in range(2):
            pre = dot(hl_ref[...], ups[k][g], NN) + b_up[g, :, k * width:(k + 1) * width]
            phi = 0.5 + 0.5 * lax.erf(pre * np.float32(0.5 ** 0.5))
            slope_ref[g, k] = phi + pre * (jnp.exp(-0.5 * pre * pre) * np.float32((2 * np.pi) ** -0.5))
            act_ref[g, k] = (pre * phi).astype(BF16)
            acc_ref[...] += dot(act_ref[g, k], downs[k][g], NT)
        return c
    lax.fori_loop(0, groups, forward, 0)
    n2, inv2 = norm_forward(acc_ref[...])
    out_ref[...] = n2 * vec(4) + vec(5)
    cott = cot[...].astype(F32)
    g_vecs[4:5] = colsum(cott * n2)
    g_vecs[5:6] = colsum(cott)
    resid = norm_backward(n2, inv2, cott * vec(4))
    acc_ref[...] = resid
    low_ref[...] = resid.astype(BF16)
    g_vecs[1:2] = colsum(low_ref[...])
    def backward(g, c):
        for k in range(2):
            g_dns[k][g] = dot(low_ref[...], act_ref[g, k], TN).astype(BF16)
            gp = (dot(low_ref[...], downs[k][g], NN) * slope_ref[g, k]).astype(BF16)
            act_ref[g, k] = gp
            g_bup[g, :, k * width:(k + 1) * width] = colsum(gp)
            g_ups[k][g] = dot(hl_ref[...], gp, TN).astype(BF16)
            acc_ref[...] += dot(act_ref[g, k], ups[k][g], NT)
        return c
    lax.fori_loop(0, groups, backward, 0)
    gh = acc_ref[...]
    g_vecs[2:3] = colsum(gh * n1_ref[...])
    g_vecs[3:4] = colsum(gh)
    ga = norm_backward(n1_ref[...], inv1, gh * vec(2))
    resid_ref[...] = ga
    low_ref[...] = ga.astype(BF16)
    g_vecs[0:1] = colsum(low_ref[...])
    def last(g, c):
        da = dot(low_ref[...], w_qo[g], NN)
        datt_ref[g] = jnp.where(lanes_from(da.shape, False), da, 0.0).astype(BF16)
        g_o[g] = dot(low_ref[...], att[g], TN).astype(BF16)
        return c
    lax.fori_loop(0, groups, last, 0)


def feed_forward(x_own, cot, att, w_qo, ups, downs, b_up, vecs):
    groups, model, width = w_qo.shape
    rows = x_own.shape[0]
    vm = pl.BlockSpec(memory_space=pltpu.VMEM)
    wshape = ((groups, model, width), BF16)
    return pl.pallas_call(
        functools.partial(ffn_kernel, groups),
        in_specs=[vm] * 10, out_specs=[vm] * 10,
        out_shape=[jax.ShapeDtypeStruct(s, d) for s, d in [
            ((rows, model), F32), ((rows, model), F32), ((groups, rows, width), BF16),
            wshape, wshape, wshape, wshape, wshape, ((groups, 1, 2 * width), F32), ((8, model), F32)]],
        scratch_shapes=[pltpu.VMEM((groups, 2, rows, width), BF16), pltpu.VMEM((groups, 2, rows, width), F32),
                        pltpu.VMEM((rows, model), F32), pltpu.VMEM((rows, model), F32), pltpu.VMEM((rows, model), F32),
                        pltpu.VMEM((rows, model), BF16), pltpu.VMEM((rows, model), BF16)],
        compiler_params=pltpu.CompilerParams(vmem_limit_bytes=VMEM_LIMIT),
    )(x_own, cot, att, w_qo, *ups, *downs, b_up, vecs)


def backward_kernel(groups, heads, blocks, x_all, x_own, w_kv, w_qo, kv, q, att, inv, datt, g_o, e_ref,
                    dx_ref, dxo_ref, g_kv, g_qo, g_bkv, g_bq,
                    do_ref, r_ref, dqt_ref, dkv_ref, acc_ref, wacc_ref):
    b, g = pl.program_id(0), pl.program_id(1)
    rows = x_own.shape[0]
    @pl.when(b == 0)
    def _():
        for h in range(heads):
            cols = slice(h * 128, h * 128 + 128)
            da = datt[g, :, cols].astype(F32).T
            scale = inv[g, h:h + 1]
            prod = jnp.sum(da * att[g, :, cols].astype(F32).T, axis=0, keepdims=True)
            r_ref[g, h:h + 1] = prod * scale
            do_ref[g, :, cols] = (da * scale).T.astype(BF16)
            dqt_ref[g, h] = jnp.zeros_like(dqt_ref[g, h])
        wacc_ref[g] = jnp.zeros_like(wacc_ref[g])
        g_bkv[g] = jnp.zeros_like(g_bkv[g])
    @pl.when(g == 0)
    def _():
        acc_ref[...] = jnp.zeros_like(acc_ref)
    here = pl.ds(pl.multiple_of(b * rows, rows), rows)
    for h in range(heads):
        cols = slice(h * 128, h * 128 + 128)
        k = kv[g, here, cols]
        d = do_ref[g, :, cols]
        e = e_ref[0, h]
        ds = (e.astype(F32) * (dot(k, d, NT) - r_ref[g, h:h + 1])).astype(BF16)
        dkv_ref[:, cols] = (dot(ds, q[g, :, cols], NN) + dot(e, d, NN)).astype(BF16)
        dqt_ref[g, h] += dot(k, ds, TN)
    dk = dkv_ref[...]
    g_bkv[g] += colsum(dk)
    acc_ref[...] += dot(dk, w_kv[g], NT)
    wacc_ref[g] += dot(x_all[here, :], dk, TN)
    @pl.when(g == groups - 1)
    def _():
        dx_ref[0] = acc_ref[...].astype(BF16)
    @pl.when(b == blocks - 1)
    def _():
        g_kv[g] = wacc_ref[g].astype(BF16)
        for h in range(heads):
            cols = slice(h * 128, h * 128 + 128)
            dq = dqt_ref[g, h] * np.float32(HEAD ** -0.5)
            dq = jnp.where(lax.broadcasted_iota(jnp.int32, dq.shape, 0) < HEAD, dq, 0.0)
            dkv_ref[:, cols] = dq.T.astype(BF16)
        dq = dkv_ref[...]
        g_bq[g] = colsum(dq)
        @pl.when(g == 0)
        def _():
            dxo_ref[...] = jnp.zeros_like(dxo_ref)
        dxo_ref[...] += dot(dq, w_qo[g], NT)
        g_qo[g] = (dot(x_own[...], dq, TN) + g_o[g].astype(F32)).astype(BF16)


def backward(x_all, x_own, w_kv, w_qo, kv, q, att, inv, datt, g_o, e):
    groups, model, width = w_kv.shape
    heads, rows = width // 128, x_own.shape[0]
    blocks = x_all.shape[0] // rows
    vm = pl.BlockSpec(memory_space=pltpu.VMEM)
    wshape = ((groups, model, width), BF16)
    return pl.pallas_call(
        functools.partial(backward_kernel, groups, heads, blocks),
        grid=(blocks, groups),
        in_specs=[vm] * 10 + [pl.BlockSpec((1, heads, rows, rows), lambda b, g: (g, 0, b, 0))],
        out_specs=[pl.BlockSpec((1, rows, model), lambda b, g: (b, 0, 0))] + [vm] * 5,
        out_shape=[jax.ShapeDtypeStruct(s, d) for s, d in [
            ((blocks, rows, model), BF16), ((rows, model), F32), wshape, wshape,
            ((groups, 1, width), F32), ((groups, 1, width), F32)]],
        scratch_shapes=[pltpu.VMEM((groups, rows, width), BF16), pltpu.VMEM((groups, 8, rows), F32),
                        pltpu.VMEM((groups, heads, 128, rows), F32), pltpu.VMEM((rows, width), BF16),
                        pltpu.VMEM((rows, model), F32), pltpu.VMEM((groups, model, width), F32)],
        compiler_params=pltpu.CompilerParams(vmem_limit_bytes=VMEM_LIMIT),
    )(x_all, x_own, w_kv, w_qo, kv, q, att, inv, datt, g_o, e)


MESH = pl.DeviceIdType.MESH
ANY = pl.BlockSpec(memory_space=pl.ANY)
VM = pl.BlockSpec(memory_space=pltpu.VMEM)


def flip(index, bit):
    return index + bit - 2 * bit * lax.rem(index // bit, 2)


def flips(index, mask):
    bit = 1
    while bit <= mask:
        if mask & bit:
            index = flip(index, bit)
        bit *= 2
    return index


def span(bits):
    masks = [0]
    for bit in bits:
        masks += [m | bit for m in masks]
    return masks


def orders(fsdp):
    bits = [1 << k for k in range(fsdp.bit_length() - 1)]
    return bits[1:] + bits[:1], bits[:0:-1] + bits[:1]


class Place:
    def __init__(self, fsdp, tensor):
        self.fsdp, self.tensor = fsdp, tensor
        self.i, self.j = lax.axis_index("fsdp"), lax.axis_index("tensor")
        self.half = tensor // 2
        self.c = lax.rem(self.i, 2)
        self.h = self.j // self.half
        self.on = self.c == self.h
        self.off = self.c != self.h
        self.twin = flip(self.i, 1)
        self.swap = lax.rem(self.j + self.half, tensor)
        self.block = jnp.where(self.on, self.j, self.swap)
        self.edge = self.half - 1 + self.c
        self.end = self.c * (tensor - 1)
        self.mate = self.h * tensor + 1 - self.j
        self.is_edge = self.j == self.edge
        self.is_end = self.j == self.end

    def other(self, k):
        return (1 - self.c) * (self.half + k) + self.c * (self.half - 1 - k)

    def barrier(self):
        sem = pltpu.get_barrier_semaphore()
        others = [(self.i, lax.rem(self.j + k, self.tensor)) for k in range(1, self.tensor)]
        bit = 1
        while bit < self.fsdp:
            others.append((flip(self.i, bit), self.j))
            bit *= 2
        others.append((self.twin, self.swap))
        for i, j in others:
            pl.semaphore_signal(sem, inc=1, device_id=(i, j), device_id_type=MESH)
        pl.semaphore_wait(sem, len(others))


class Sends:
    def __init__(self, place, send, recv):
        self.place, self.send, self.recv, self.n, self.started = place, send, recv, 0, []

    def slot(self):
        self.n += 1
        return self.n - 1

    def copy(self, src, dst, slot, i, j):
        return pltpu.make_async_remote_copy(src_ref=src, dst_ref=dst, send_sem=self.send.at[slot], recv_sem=self.recv.at[slot],
                                            device_id=(i, j), device_id_type=MESH)

    def start(self, src, dst, slot, i, j, when=None):
        copy = self.copy(src, dst, slot, i, j)
        if when is None:
            copy.start()
        else:
            pl.when(when)(copy.start)
        self.started.append((copy, when))

    def arrive(self, dst, slot, when=None):
        copy = self.copy(dst, dst, slot, self.place.i, self.place.j)
        if when is None:
            copy.wait_recv()
        else:
            pl.when(when)(copy.wait_recv)

    def finish(self):
        for copy, when in self.started:
            if when is None:
                copy.wait_send()
            else:
                pl.when(when)(copy.wait_send)
        self.started = []


class Gather:
    def __init__(self, sends, array, order, own=None):
        self.s, self.p, self.a, self.order = sends, sends.place, array, order
        self.own = own
        self.right = [sends.slot() for _ in range(self.p.tensor - 1)]
        self.left = [sends.slot() for _ in range(self.p.tensor - 1)]
        self.stage = [[(m, sends.slot()) for m in span(order[:k])] for k in range(len(order))]

    def line(self, step):
        s, p, n = self.s, self.p, self.p.tensor
        for slots, way in ((self.right, 1), (self.left, -1)):
            owner = p.j - way * step
            exists = (owner >= 0) & (owner < n)
            there = p.j + way
            block = self.a.at[owner, p.i]
            if step > 0:
                s.arrive(block, slots[step - 1], exists)
            if step < n - 1:
                src = self.own if step == 0 and self.own is not None else block
                s.start(src, block, slots[step], p.i, there, exists & (there >= 0) & (there < n))

    def slab(self, mask):
        return self.a.at[:, flips(self.p.i, mask)]

    def go(self, k, masks=None):
        for m, slot in self.stage[k]:
            if masks is None or m in masks:
                self.s.start(self.slab(m), self.slab(m), slot, flip(self.p.i, self.order[k]), self.p.j)

    def come(self, k):
        for m, slot in self.stage[k]:
            self.s.arrive(self.slab(m | self.order[k]), slot)


def gather_kernel(fsdp, tensor, pack, small, tok, cot, w, sm, x, cotp, send, recv, local):
    p = Place(fsdp, tensor)
    s = Sends(p, send, recv)
    first, second = orders(fsdp)
    chunks = pack.shape[0]
    gathers = [Gather(s, w.at[k], (first, second)[k % 2], pack.at[k]) for k in range(chunks)]
    tiny = Gather(s, sm, first, small)
    xin = [s.slot() for _ in range(tensor)]
    xtwin = s.slot()
    cslot = s.slot()
    copies = [pltpu.make_async_copy(pack.at[k], w.at[k, p.j, p.i], local.at[k]) for k in range(chunks)]
    copies += [pltpu.make_async_copy(small, sm.at[p.j, p.i], local.at[chunks]),
               pltpu.make_async_copy(tok, x.at[p.j], local.at[chunks + 1])]
    for copy in copies[:-1]:
        copy.start()
    pl.when(p.on)(copies[-1].start)
    p.barrier()
    g0, g1, g2 = [tiny] + gathers[:2], gathers[2:4], gathers[4:]
    each = lambda group, call: [call(g) for g in group]
    xslot = lambda t: s_slot(xin, t)

    def x_start(src, t, i, j, when):
        copy = pltpu.make_async_remote_copy(src_ref=src, dst_ref=x.at[t], send_sem=xsend(t, i), recv_sem=recv.at[xin[0] + t],
                                            device_id=(i, j), device_id_type=MESH)
        pl.when(when)(copy.start)
        s.started.append((copy, when))

    def xsend(t, i):
        return send.at[xin[0] + t] if i is p.i else twin_send(t)

    def twin_send(t):
        return local.at[chunks + 2 + t]

    def x_arrive(t, when):
        pl.when(when)(pltpu.make_async_remote_copy(src_ref=x.at[t], dst_ref=x.at[t], send_sem=send.at[xin[0] + t], recv_sem=recv.at[xin[0] + t],
                                                   device_id=(p.i, p.j), device_id_type=MESH).wait_recv)

    each(g0, lambda g: g.line(0))
    x_start(tok, p.j, p.i, p.edge, p.off)
    if p.half > 1:
        x_start(tok, p.j, p.i, p.mate, p.on)
    x_start(tok, p.j, p.twin, p.j, p.on)
    for step in range(1, tensor):
        each(g0, lambda g: g.line(step))
    for copy in copies[:-1]:
        copy.wait()
    each(g0, lambda g: g.go(0))
    each(g1, lambda g: g.line(0))
    each(g0, lambda g: g.come(0))
    each(g0, lambda g: g.go(1))
    each(g0, lambda g: g.go(2, span(g.order[:1])))
    if p.half > 1:
        x_arrive(p.mate, p.on)
        x_start(x.at[p.mate], p.mate, p.twin, p.j, p.on)
    for k in range(p.half):
        t = p.other(k)
        x_arrive(t, p.on)
        if p.half > 1:
            x_start(x.at[t], t, p.i, p.end, p.on & p.is_edge)
        x_start(x.at[t], t, p.twin, p.j, p.on)
        if k == 0:
            each(g1, lambda g: g.line(1))
            each(g0, lambda g: g.come(1))
            each(g0, lambda g: g.go(2, [m for m in span(g.order[:2]) if m not in span(g.order[:1])]))
            each(g2, lambda g: g.line(0))
    for step in range(2, tensor):
        each(g1, lambda g: g.line(step))
    each(g1, lambda g: g.go(0))
    s.start(cot, cotp, cslot, p.twin, p.swap, p.off)
    each(g2, lambda g: g.line(1))
    each(g1, lambda g: g.come(0))
    each(g1, lambda g: g.go(1))
    each(g1, lambda g: g.go(2, span(g.order[:1])))
    for step in range(2, tensor):
        each(g2, lambda g: g.line(step))
    each(g2, lambda g: g.go(0))
    each(g1, lambda g: g.come(1))
    each(g1, lambda g: g.go(2, [m for m in span(g.order[:2]) if m not in span(g.order[:1])]))
    each(g2, lambda g: g.come(0))
    each(g2, lambda g: g.go(1))
    each(g2, lambda g: g.go(2, span(g.order[:1])))
    each(g2, lambda g: g.come(1))
    each(g2, lambda g: g.go(2, [m for m in span(g.order[:2]) if m not in span(g.order[:1])]))
    for group in (g0, g1, g2):
        each(group, lambda g: g.come(2))
    for t in range(tensor):
        x_arrive(t, p.off)
    s.arrive(cotp, cslot, p.off)
    pl.when(p.on)(copies[-1].wait)
    s.finish()


def gather_all(fsdp, tensor, pack, small, tok, cot):
    chunks, shard, width = pack.shape
    rows, model = tok.shape
    slots = (chunks + 1) * (2 * (tensor - 1) + fsdp - 1) + tensor + 2
    return pl.pallas_call(
        functools.partial(gather_kernel, fsdp, tensor),
        in_specs=[VM, VM, VM, ANY], out_specs=[ANY] * 4,
        out_shape=[jax.ShapeDtypeStruct(s, d) for s, d in [
            ((chunks, tensor, fsdp, shard, width), BF16), ((tensor, fsdp, *small.shape), F32),
            ((tensor, rows, model), BF16), ((rows, model), BF16)]],
        scratch_shapes=[pltpu.SemaphoreType.DMA((slots,)), pltpu.SemaphoreType.DMA((slots,)),
                        pltpu.SemaphoreType.DMA((chunks + 2 + tensor,))],
        compiler_params=pltpu.CompilerParams(collective_id=0, has_side_effects=True, vmem_limit_bytes=VMEM_LIMIT),
    )(pack, small, tok, cot)


class Scatter:
    def __init__(self, sends, parts, halves, from_left, from_right, order, out):
        self.s, self.p, self.a, self.order = sends, sends.place, parts, order[::-1]
        self.halves, self.left_in, self.right_in, self.out = halves, from_left, from_right, out
        n, self.n = len(order), self.p.tensor
        self.masks = [span(self.order[k + 1:]) for k in range(n)]
        self.slots = [[sends.slot() for _ in self.masks[k]] for k in range(n)]
        self.right = [sends.slot() for _ in range(self.n)]
        self.left = [sends.slot() for _ in range(self.n)]

    def part(self, k, mask):
        if k == 0:
            return self.a.at[:, flips(self.p.i, mask)]
        return self.halves[k - 1].at[self.masks[k - 1].index(mask)]

    def go(self, k):
        bit = self.order[k]
        for n, m in enumerate(self.masks[k]):
            self.s.start(self.part(k, m | bit), self.halves[k].at[n], self.slots[k][n], flip(self.p.i, bit), self.p.j)

    def come(self, k):
        for n, m in enumerate(self.masks[k]):
            here, mine = self.halves[k].at[n], self.part(k, m)
            self.s.arrive(here, self.slots[k][n])
            for t in range(self.n):
                here[t] = (here[t].astype(F32) + mine[t].astype(F32)).astype(BF16)

    def line(self, step):
        s, p, n = self.s, self.p, self.n
        total = self.halves[-1].at[0]
        for slots, way, inbox in ((self.right, 1, self.left_in), (self.left, -1, self.right_in)):
            far = n - 1 - step
            owner = p.j + way * far
            before = p.j - way
            exists = (owner >= 0) & (owner < n)
            has = exists & (before >= 0) & (before < n)
            if far < n - 1:
                s.arrive(inbox.at[owner], slots[far + 1], has)
            if far > 0:
                def add(owner=owner, inbox=inbox):
                    inbox[owner] = (inbox[owner].astype(F32) + total[owner].astype(F32)).astype(BF16)
                def plain(owner=owner, inbox=inbox):
                    inbox[owner] = total[owner]
                if far < n - 1:
                    pl.when(has)(add)
                    pl.when(exists & jnp.logical_not(has))(plain)
                else:
                    pl.when(exists)(plain)
                s.start(inbox.at[owner], inbox.at[owner], slots[far], p.i, p.j + way, exists)

    def result(self):
        p = self.p
        self.out[...] = self.halves[-1][0, p.j].astype(F32)
        for inbox, before in ((self.left_in, p.j > 0), (self.right_in, p.j < self.n - 1)):
            @pl.when(before)
            def _(inbox=inbox):
                self.out[...] += inbox[p.j].astype(F32)


def reduce_kernel(fsdp, tensor, chunks, *refs):
    grads, (dx, own, own2, result, tiny), refs = refs[:chunks], refs[chunks:chunks + 5], refs[chunks + 5:]
    g_out, dx_out, out_out, tiny_out = refs[:4]
    refs = refs[4:]
    bits = fsdp.bit_length() - 1
    halves, refs = refs[:bits], refs[bits:]
    inl, inr, twin_in, mate_in, fin_in, send_out, recv_out, send_own, tiny_in, send, recv = refs
    p = Place(fsdp, tensor)
    s = Sends(p, send, recv)
    first, second = orders(fsdp)
    sc = [Scatter(s, grads[k], [h.at[k] for h in halves], inl.at[k], inr.at[k], (first, second)[k % 2], g_out.at[k]) for k in range(chunks)]
    each = lambda group, call: [call(g) for g in group]
    g1, g2, g0 = sc[4:], sc[2:4], sc[:2]
    twin = [s.slot() for _ in range(tensor)]
    mate = [s.slot() for _ in range(tensor)]
    fin, swp = s.slot(), s.slot()
    tiny_out[...] = tiny[...]
    send_out[...] = result[...].astype(BF16)
    @pl.when(p.off)
    def _():
        send_own[...] = (dx[p.block].astype(F32) + (own[...] + own2[...])).astype(BF16)
    p.barrier()
    for t in range(tensor):
        s.start(dx.at[t], twin_in.at[t], twin[t], p.twin, p.j, p.off & (p.block != t))
        s.start(send_own, twin_in.at[t], twin[t], p.twin, p.j, p.off & (p.block == t))
    for g in (g1, g2, g0):
        each(g, lambda g: g.go(0))
    s.start(send_out, recv_out, swp, p.twin, p.swap, p.off)
    for t in range(tensor):
        @pl.when(p.on)
        def _(t=t):
            s.copy(twin_in.at[t], twin_in.at[t], twin[t], p.i, p.j).wait_recv()
            twin_in[t] = (twin_in[t].astype(F32) + dx[t].astype(F32)).astype(BF16)
    far = list(range(tensor // 2))[::-1]
    if p.half > 1:
        for k in far:
            t = p.other(k)
            s_copy = pltpu.make_async_remote_copy(src_ref=twin_in.at[t], dst_ref=mate_in.at[t], send_sem=send.at[mate[0] + t],
                                                  recv_sem=recv.at[mate[0] + t], device_id=(p.i, p.edge), device_id_type=MESH)
            when = p.on & p.is_end
            pl.when(when)(s_copy.start)
            s.started.append((s_copy, when))
        s_copy = pltpu.make_async_remote_copy(src_ref=twin_in.at[p.mate], dst_ref=mate_in.at[p.mate], send_sem=send.at[mate[0] + p.mate],
                                              recv_sem=recv.at[mate[0] + p.mate], device_id=(p.i, p.mate), device_id_type=MESH)
        pl.when(p.on)(s_copy.start)
        s.started.append((s_copy, p.on))
    def x_wait(t, when):
        pl.when(when)(pltpu.make_async_remote_copy(src_ref=mate_in.at[t], dst_ref=mate_in.at[t], send_sem=send.at[mate[0] + t],
                                                   recv_sem=recv.at[mate[0] + t], device_id=(p.i, p.j), device_id_type=MESH).wait_recv)
    each(g1, lambda g: g.come(0))
    each(g1, lambda g: g.go(1))
    for k in far:
        t = p.other(k)
        if p.half > 1:
            x_wait(t, p.on & p.is_edge)
            @pl.when(p.on & p.is_edge)
            def _(t=t):
                mate_in[t] = (mate_in[t].astype(F32) + twin_in[t].astype(F32)).astype(BF16)
        src = mate_in if p.half > 1 else twin_in
        copy = pltpu.make_async_remote_copy(src_ref=src.at[t], dst_ref=fin_in, send_sem=send.at[twin[0] + k], recv_sem=recv.at[fin],
                                            device_id=(p.i, t), device_id_type=MESH)
        when = p.on & p.is_edge
        pl.when(when)(copy.start)
        s.started.append((copy, when))
    each(g2, lambda g: g.come(0))
    each(g2, lambda g: g.go(1))
    each(g1, lambda g: g.come(1))
    each(g1, lambda g: g.go(2))
    each(g0, lambda g: g.come(0))
    each(g0, lambda g: g.go(1))
    each(g2, lambda g: g.come(1))
    each(g2, lambda g: g.go(2))
    each(g1, lambda g: g.come(2))
    each(g1, lambda g: g.line(0))
    each(g0, lambda g: g.come(1))
    each(g0, lambda g: g.go(2))
    each(g1, lambda g: g.line(1))
    each(g2, lambda g: g.come(2))
    each(g2, lambda g: g.line(0))
    for step in range(2, tensor):
        each(g1, lambda g: g.line(step))
    each(g1, lambda g: g.result())
    each(g0, lambda g: g.come(2))
    each(g0, lambda g: g.line(0))
    for step in range(1, tensor):
        each(g2, lambda g: g.line(step))
    each(g2, lambda g: g.result())
    for step in range(1, tensor):
        each(g0, lambda g: g.line(step))
    each(g0, lambda g: g.result())
    bit, n = 1, 0
    while bit < fsdp * tensor:
        i, j = (flip(p.i, bit), p.j) if bit < fsdp else (p.i, flip(p.j, bit // fsdp))
        slot = s.slot()
        s.start(tiny_out, tiny_in.at[n], slot, i, j)
        s.arrive(tiny_in.at[n], slot)
        s.started.pop()[0].wait_send()
        tiny_out[...] += tiny_in[n]
        bit, n = bit * 2, n + 1
    @pl.when(p.on)
    def _():
        dx_out[...] = own[...] + own2[...] + twin_in[p.j].astype(F32)
        out_out[...] = result[...]
    if p.half > 1:
        x_wait(p.j, p.on)
        @pl.when(p.on)
        def _():
            dx_out[...] += mate_in[p.j].astype(F32)
    s.arrive(fin_in, fin, p.off)
    s.arrive(recv_out, swp, p.off)
    @pl.when(p.off)
    def _():
        dx_out[...] = fin_in[...].astype(F32)
        out_out[...] = recv_out[...].astype(F32)
    s.finish()


def reduce_all(fsdp, tensor, grads, dx, own, own2, result, tiny):
    chunks = len(grads)
    shape = grads[0].shape
    shard, width = shape[2:]
    rows, model = own.shape
    bits = fsdp.bit_length() - 1
    slots = chunks * (fsdp - 1 + 2 * tensor) + 2 * tensor + 2 + 16
    steps = (fsdp * tensor).bit_length() - 1
    scratch = [pltpu.VMEM((chunks, fsdp >> (k + 1), tensor, shard, width), BF16) for k in range(bits)]
    scratch += [pltpu.VMEM((chunks, tensor, shard, width), BF16)] * 2
    scratch += [pltpu.VMEM((tensor, rows, model), BF16)] * 2 + [pltpu.VMEM((rows, model), BF16)] * 4
    scratch += [pltpu.VMEM((steps, *tiny.shape), F32), pltpu.SemaphoreType.DMA((slots,)), pltpu.SemaphoreType.DMA((slots,))]
    return pl.pallas_call(
        functools.partial(reduce_kernel, fsdp, tensor, chunks),
        in_specs=[VM] * (chunks + 5), out_specs=[VM] * 4,
        out_shape=[jax.ShapeDtypeStruct(s, d) for s, d in [
            ((chunks, shard, width), F32), ((rows, model), F32), ((rows, model), F32), (tiny.shape, F32)]],
        scratch_shapes=scratch,
        compiler_params=pltpu.CompilerParams(collective_id=1, has_side_effects=True, vmem_limit_bytes=VMEM_LIMIT),
    )(*grads, dx, own, own2, result, tiny)


def normalize(values, gain, shift):
    average = jnp.mean(values, -1, keepdims=True)
    centered = values - average
    inverse = lax.rsqrt(jnp.mean(centered * centered, -1, keepdims=True) + EPSILON)
    return centered * inverse * gain + shift


def exact_gelu(values):
    return jax.nn.gelu(values, approximate=False)


def outer_sum(left, right):
    return dot(left, right, TN)


def times_transposed(left, right):
    return dot(left, right, NT)


def plain(
    tokens,
    cotangent,
    w_query,
    w_key,
    w_value,
    w_out,
    w_up,
    w_down,
    b_query,
    b_value,
    b_up,
    b_out,
    b_down,
    gain_attn,
    shift_attn,
    gain_ffn,
    shift_ffn,
):
    gathered = (
        lax.all_gather(w_query, "fsdp", axis=0, tiled=True),
        lax.all_gather(w_key, "fsdp", axis=0, tiled=True),
        lax.all_gather(w_value, "fsdp", axis=0, tiled=True),
        lax.all_gather(w_out, "fsdp", axis=1, tiled=True),
        lax.all_gather(w_up, "fsdp", axis=0, tiled=True),
        lax.all_gather(w_down, "fsdp", axis=1, tiled=True),
        lax.all_gather(b_query, "fsdp", axis=0, tiled=True),
        lax.all_gather(b_value, "fsdp", axis=0, tiled=True),
        lax.all_gather(b_up, "fsdp", axis=0, tiled=True),
        lax.all_gather(b_out, "fsdp", axis=0, tiled=True),
        lax.all_gather(b_down, "fsdp", axis=0, tiled=True),
        lax.all_gather(gain_attn, "fsdp", axis=0, tiled=True),
        lax.all_gather(shift_attn, "fsdp", axis=0, tiled=True),
        lax.all_gather(gain_ffn, "fsdp", axis=0, tiled=True),
        lax.all_gather(shift_ffn, "fsdp", axis=0, tiled=True),
    )
    (
        query_weight,
        key_weight,
        value_weight,
        out_weight,
        up_weight,
        down_weight,
        query_bias,
        value_bias,
        up_bias,
        out_bias,
        down_bias,
        attn_gain,
        attn_shift,
        ffn_gain,
        ffn_shift,
    ) = gathered
    own_rows = tokens.shape[0]
    seq_len = own_rows * lax.axis_size("tensor")
    heads = query_weight.shape[1] // HEAD
    span = min(512, seq_len)
    blocks = seq_len // span
    scale = HEAD ** (-0.5)
    full_tokens = lax.all_gather(tokens, "tensor", axis=0, tiled=True)
    query = (
        jnp.dot(full_tokens, query_weight, preferred_element_type=jnp.float32)
        + query_bias.astype(jnp.float32)
    ).astype(jnp.bfloat16)
    keys = jnp.dot(full_tokens, key_weight, preferred_element_type=jnp.float32).astype(jnp.bfloat16)
    values = (
        jnp.dot(full_tokens, value_weight, preferred_element_type=jnp.float32)
        + value_bias.astype(jnp.float32)
    ).astype(jnp.bfloat16)
    query_blocks = query.reshape(blocks, span, heads, HEAD)
    key_heads = keys.reshape(seq_len, heads, HEAD)
    value_heads = values.reshape(seq_len, heads, HEAD)

    def scores_of(piece):
        return (
            jnp.einsum("qhd,khd->hqk", piece, key_heads, preferred_element_type=jnp.float32) * scale
        )

    def forward_block(piece):
        scores = scores_of(piece)
        largest = jnp.max(scores, -1, keepdims=True)
        exponent = jnp.exp(scores - largest)
        total = jnp.sum(exponent, -1, keepdims=True)
        soft_low = (exponent / total).astype(jnp.bfloat16)
        result = jnp.einsum(
            "hqk,khd->qhd", soft_low, value_heads, preferred_element_type=jnp.float32
        )
        return (result.astype(jnp.bfloat16), largest, total)

    attended, largest_all, total_all = lax.map(forward_block, query_blocks)
    attended = attended.reshape(seq_len, heads * HEAD)
    attn_part = lax.psum_scatter(
        jnp.dot(attended, out_weight, preferred_element_type=jnp.float32).astype(jnp.bfloat16),
        "tensor",
        scatter_dimension=0,
        tiled=True,
    ).astype(jnp.float32)
    resid_attn = tokens.astype(jnp.float32) + (attn_part + out_bias.astype(jnp.float32))
    hidden, attn_norm_back = jax.vjp(
        normalize, resid_attn, attn_gain.astype(jnp.float32), attn_shift.astype(jnp.float32)
    )
    full_hidden = lax.all_gather(hidden.astype(jnp.bfloat16), "tensor", axis=0, tiled=True)
    pre_act = jnp.dot(full_hidden, up_weight, preferred_element_type=jnp.float32) + up_bias.astype(
        jnp.float32
    )
    activ, gelu_back = jax.vjp(exact_gelu, pre_act)
    activ_low = activ.astype(jnp.bfloat16)
    ffn_part = lax.psum_scatter(
        jnp.dot(activ_low, down_weight, preferred_element_type=jnp.float32).astype(jnp.bfloat16),
        "tensor",
        scatter_dimension=0,
        tiled=True,
    ).astype(jnp.float32)
    resid_ffn = hidden + (ffn_part + down_bias.astype(jnp.float32))
    output, ffn_norm_back = jax.vjp(
        normalize, resid_ffn, ffn_gain.astype(jnp.float32), ffn_shift.astype(jnp.float32)
    )
    matrices = (
        lax.all_gather(w_query, "fsdp", axis=0, tiled=True),
        lax.all_gather(w_key, "fsdp", axis=0, tiled=True),
        lax.all_gather(w_value, "fsdp", axis=0, tiled=True),
        lax.all_gather(w_out, "fsdp", axis=1, tiled=True),
        lax.all_gather(w_up, "fsdp", axis=0, tiled=True),
        lax.all_gather(w_down, "fsdp", axis=1, tiled=True),
    )
    back_query, back_key, back_value, back_out, back_up, back_down = matrices
    grad_resid_ffn, grad_gain_ffn, grad_shift_ffn = ffn_norm_back(cotangent.astype(jnp.float32))
    grad_ffn_full = lax.all_gather(
        grad_resid_ffn.astype(jnp.bfloat16), "tensor", axis=0, tiled=True
    )
    grad_down_bias = jnp.sum(grad_ffn_full, 0, dtype=jnp.float32)
    grad_down_weight = outer_sum(activ_low, grad_ffn_full)
    grad_activ = times_transposed(grad_ffn_full, back_down)
    grad_pre = gelu_back(grad_activ)[0].astype(jnp.bfloat16)
    grad_up_bias = jnp.sum(grad_pre, 0, dtype=jnp.float32)
    grad_up_weight = outer_sum(full_hidden, grad_pre)
    grad_hidden = grad_resid_ffn + lax.psum_scatter(
        times_transposed(grad_pre, back_up).astype(jnp.bfloat16),
        "tensor",
        scatter_dimension=0,
        tiled=True,
    ).astype(jnp.float32)
    grad_resid_attn, grad_gain_attn, grad_shift_attn = attn_norm_back(grad_hidden)
    grad_attn_full = lax.all_gather(
        grad_resid_attn.astype(jnp.bfloat16), "tensor", axis=0, tiled=True
    )
    grad_out_bias = jnp.sum(grad_attn_full, 0, dtype=jnp.float32)
    grad_out_weight = outer_sum(attended, grad_attn_full)
    grad_attended = times_transposed(grad_attn_full, back_out).astype(jnp.bfloat16)
    grad_blocks = grad_attended.reshape(blocks, span, heads, HEAD)

    def backward_block(carry, item):
        piece, grad_piece, largest, total = item
        soft = jnp.exp(scores_of(piece) - largest) / total
        soft_low = soft.astype(jnp.bfloat16)
        grad_soft = jnp.einsum(
            "qhd,khd->hqk", grad_piece, value_heads, preferred_element_type=jnp.float32
        )
        inner = jnp.sum(soft * grad_soft, -1, keepdims=True)
        grad_scores = (soft * (grad_soft - inner)).astype(jnp.bfloat16)
        grad_query_block = (
            jnp.einsum("hqk,khd->qhd", grad_scores, key_heads, preferred_element_type=jnp.float32)
            * scale
        )
        grad_key_sum = (
            carry[0]
            + jnp.einsum("hqk,qhd->khd", grad_scores, piece, preferred_element_type=jnp.float32)
            * scale
        )
        grad_value_sum = carry[1] + jnp.einsum(
            "hqk,qhd->khd", soft_low, grad_piece, preferred_element_type=jnp.float32
        )
        return ((grad_key_sum, grad_value_sum), grad_query_block.astype(jnp.bfloat16))

    zeros = jnp.zeros((seq_len, heads, HEAD), jnp.float32)
    (grad_key_sum, grad_value_sum), grad_query = lax.scan(
        backward_block, (zeros, zeros), (query_blocks, grad_blocks, largest_all, total_all)
    )
    grad_query = grad_query.reshape(seq_len, heads * HEAD)
    grad_keys = grad_key_sum.reshape(seq_len, heads * HEAD).astype(jnp.bfloat16)
    grad_values = grad_value_sum.reshape(seq_len, heads * HEAD).astype(jnp.bfloat16)
    grad_query_bias = jnp.sum(grad_query, 0, dtype=jnp.float32)
    grad_value_bias = jnp.sum(grad_values, 0, dtype=jnp.float32)
    grad_query_weight = outer_sum(full_tokens, grad_query)
    grad_key_weight = outer_sum(full_tokens, grad_keys)
    grad_value_weight = outer_sum(full_tokens, grad_values)
    token_terms = (
        times_transposed(grad_query, back_query)
        + times_transposed(grad_keys, back_key)
        + times_transposed(grad_values, back_value)
    )
    norm_terms = jnp.tile(
        jnp.stack([grad_gain_attn, grad_shift_attn, grad_gain_ffn, grad_shift_ffn]),
        (lax.axis_size("tensor"), 1),
    )
    token_part, norm_sums = (
        lax.psum_scatter(
            token_terms.astype(jnp.bfloat16), "tensor", scatter_dimension=0, tiled=True
        ).astype(jnp.float32),
        lax.psum_scatter(
            norm_terms.astype(jnp.bfloat16), "tensor", scatter_dimension=0, tiled=True
        ).astype(jnp.float32),
    )
    grad_tokens = grad_resid_attn + token_part
    shards = (
        lax.psum_scatter(grad_query_weight, "fsdp", scatter_dimension=0, tiled=True),
        lax.psum_scatter(grad_key_weight, "fsdp", scatter_dimension=0, tiled=True),
        lax.psum_scatter(grad_value_weight, "fsdp", scatter_dimension=0, tiled=True),
        lax.psum_scatter(grad_out_weight, "fsdp", scatter_dimension=1, tiled=True),
        lax.psum_scatter(grad_up_weight, "fsdp", scatter_dimension=0, tiled=True),
        lax.psum_scatter(grad_down_weight, "fsdp", scatter_dimension=1, tiled=True),
        lax.psum_scatter(grad_query_bias, "fsdp", scatter_dimension=0, tiled=True),
        lax.psum_scatter(grad_value_bias, "fsdp", scatter_dimension=0, tiled=True),
        lax.psum_scatter(grad_up_bias, "fsdp", scatter_dimension=0, tiled=True),
        lax.psum_scatter(grad_out_bias, "fsdp", scatter_dimension=0, tiled=True),
        lax.psum_scatter(grad_down_bias, "fsdp", scatter_dimension=0, tiled=True),
        lax.psum_scatter(norm_sums[0], "fsdp", scatter_dimension=0, tiled=True),
        lax.psum_scatter(norm_sums[1], "fsdp", scatter_dimension=0, tiled=True),
        lax.psum_scatter(norm_sums[2], "fsdp", scatter_dimension=0, tiled=True),
        lax.psum_scatter(norm_sums[3], "fsdp", scatter_dimension=0, tiled=True),
    )
    return (
        output,
        grad_tokens,
        shards[0],
        shards[1],
        shards[2],
        shards[3],
        shards[4],
        shards[5],
        shards[6],
        shards[7],
        shards[8],
        shards[9],
        shards[10],
        shards[11],
        shards[12],
        shards[13],
        shards[14],
    )


def fits(tokens, w_query, w_up):
    fsdp, tensor = lax.axis_size("fsdp"), lax.axis_size("tensor")
    shard, columns = w_query.shape
    return (tensor in (2, 4) and fsdp >= 4 and fsdp & (fsdp - 1) == 0 and shard % 16 == 0 and columns % HEAD == 0
            and w_up.shape[1] == 4 * columns and tokens.shape[0] % 128 == 0)


def pairs(first, second):
    rows, columns = first.shape
    both = jnp.stack([first.reshape(rows, -1, HEAD), second.reshape(rows, -1, HEAD)], 2)
    return both.reshape(rows, 2 * columns)


def layer(tokens, cotangent, w_query, w_key, w_value, w_out, w_up, w_down, b_query, b_value, b_up, b_out, b_down,
          gain_attn, shift_attn, gain_ffn, shift_ffn):
    if not fits(tokens, w_query, w_up):
        return plain(tokens, cotangent, w_query, w_key, w_value, w_out, w_up, w_down, b_query, b_value, b_up, b_out, b_down,
                     gain_attn, shift_attn, gain_ffn, shift_ffn)
    fsdp, tensor = lax.axis_size("fsdp"), lax.axis_size("tensor")
    i, j = lax.axis_index("fsdp"), lax.axis_index("tensor")
    rows, model = tokens.shape
    shard, columns = w_query.shape
    width = 2 * columns
    down = w_down.T
    pack = jnp.stack([pairs(w_key, w_value), pairs(w_query, w_out.T), w_up[:, :width], w_up[:, width:], down[:, :width], down[:, width:]])

    def placed(vector):
        mine = jnp.tile(vector.astype(F32), fsdp).reshape(fsdp, -1)
        mine = jnp.where(lax.broadcasted_iota(jnp.int32, mine.shape, 0) == i, mine, 0.0)
        return mine.reshape(1, -1)

    def spread(vector, second):
        vector = placed(vector)
        zero = jnp.zeros_like(vector)
        return pairs(zero, vector) if second else pairs(vector, zero)

    small = jnp.concatenate([jnp.concatenate([spread(b_value, True), spread(b_query, False)], 1), placed(b_up),
                             *map(placed, (b_out, b_down, gain_attn, shift_attn, gain_ffn, shift_ffn))])
    weights, smalls, x, cot_in = gather_all(fsdp, tensor, pack, small, tokens, cotangent)
    weights = weights.reshape(6, tensor, model, width)
    w_kv, w_qo, up0, up1, dn0, dn1 = [weights[k] for k in range(6)]
    smalls = jnp.sum(smalls, 1)
    bias_kv, bias_q, bias_up = smalls[:, :1, :width], smalls[:, :1, width:], smalls[:, 1:2]
    vecs = jnp.concatenate([smalls[0, 2:8], jnp.zeros((2, model), F32)])
    half = tensor // 2
    on = i % 2 == j // half
    block = jnp.where(on, j, (j + half) % tensor)
    x_own = lax.dynamic_index_in_dim(x, block, 0, False)
    cot = jnp.where(on, cotangent, cot_in)
    x_all = x.reshape(tensor * rows, model)
    kv, q, att, inv, exps = attend(x_all, x_own, w_kv, w_qo, bias_kv, bias_q)
    out, resid, datt, g_o, g_up0, g_up1, g_dn0, g_dn1, g_bup, g_vecs = feed_forward(
        x_own, cot, att, w_qo, (up0, up1), (dn0, dn1), bias_up, vecs)
    dx, dx_own, g_kv, g_qo, g_bkv, g_bq = backward(x_all, x_own, w_kv, w_qo, kv, q, att, inv, datt, g_o, exps)
    tiny = jnp.concatenate([g_vecs, g_bup[:, 0], jnp.concatenate([g_bkv[:, 0], g_bq[:, 0]], 1)])
    grads = [g.reshape(tensor, fsdp, shard, width) for g in (g_kv, g_qo, g_up0, g_up1, g_dn0, g_dn1)]
    shards, grad_tokens, output, tiny = reduce_all(fsdp, tensor, grads, dx, resid, dx_own, out, tiny)

    def apart(shard_pair):
        both = shard_pair.reshape(shard, -1, 2, HEAD)
        return both[:, :, 0].reshape(shard, columns), both[:, :, 1].reshape(shard, columns)

    g_key, g_value = apart(shards[0])
    g_query, g_out = apart(shards[1])
    g_up = jnp.concatenate([shards[2], shards[3]], 1)
    g_down = jnp.concatenate([shards[4], shards[5]], 1).T
    mine = lambda vector, n: lax.dynamic_slice_in_dim(vector, i * n, n)
    pick = lambda first: lax.dynamic_index_in_dim(tiny, first + j, 0, False)
    both = pick(8 + tensor).reshape(2, -1, 2, HEAD)
    g_bq, g_bv = both[1, :, 0].reshape(-1), both[0, :, 1].reshape(-1)
    vectors = [mine(tiny[k], shard) for k in range(6)]
    return (output, grad_tokens, g_query, g_key, g_value, g_out.T, g_up, g_down,
            mine(g_bq, columns // fsdp), mine(g_bv, columns // fsdp), mine(pick(8), 2 * width // fsdp), *vectors)


def solution(mesh):
    return jax.shard_map(
        layer,
        mesh=mesh,
        in_specs=(
            P(("fsdp", "tensor"), None),
            P(("fsdp", "tensor"), None),
            P("fsdp", "tensor"),
            P("fsdp", "tensor"),
            P("fsdp", "tensor"),
            P("tensor", "fsdp"),
            P("fsdp", "tensor"),
            P("tensor", "fsdp"),
            P(("tensor", "fsdp")),
            P(("tensor", "fsdp")),
            P(("tensor", "fsdp")),
            P("fsdp"),
            P("fsdp"),
            P("fsdp"),
            P("fsdp"),
            P("fsdp"),
            P("fsdp"),
        ),
        out_specs=(
            P(("fsdp", "tensor"), None),
            P(("fsdp", "tensor"), None),
            P("fsdp", "tensor"),
            P("fsdp", "tensor"),
            P("fsdp", "tensor"),
            P("tensor", "fsdp"),
            P("fsdp", "tensor"),
            P("tensor", "fsdp"),
            P(("tensor", "fsdp")),
            P(("tensor", "fsdp")),
            P(("tensor", "fsdp")),
            P("fsdp"),
            P("fsdp"),
            P("fsdp"),
            P("fsdp"),
            P("fsdp"),
            P("fsdp"),
        ),
        check_vma=False,
    )
```

```python
import functools

import jax
import jax.numpy as jnp
import numpy as np
from jax import lax
from jax.experimental import pallas as pl
from jax.experimental.pallas import tpu as pltpu
from jax.sharding import PartitionSpec as P

F32, BF16 = jnp.float32, jnp.bfloat16
HEAD = 64
EPSILON = 1e-12
VMEM_LIMIT = 64000 * 1024


def dot(left, right, contract):
    return lax.dot_general(left, right, ((contract[:1], contract[1:]), ((), ())), preferred_element_type=F32)

NN, NT, TN = (1, 0), (1, 1), (0, 0)


def lanes_from(shape, low):
    return lax.broadcasted_iota(jnp.int32, shape, len(shape) - 1) % (2 * HEAD) >= HEAD if not low else \
        lax.broadcasted_iota(jnp.int32, shape, len(shape) - 1) % (2 * HEAD) < HEAD


def project_keys(x, w, bias):
    return (dot(x, w, NN) + bias).astype(BF16)


def project_query(x, w, bias):
    out = dot(x, w, NN) + bias
    return jnp.where(lanes_from(out.shape, True), out.astype(BF16) * BF16(HEAD ** -0.5), BF16(0))


def norm_forward(z):
    mean = jnp.mean(z, -1, keepdims=True)
    centered = z - mean
    inv = lax.rsqrt(jnp.mean(centered * centered, -1, keepdims=True) + EPSILON)
    return centered * inv, inv


def norm_backward(n, inv, dn):
    return inv * (dn - jnp.mean(dn, -1, keepdims=True) - n * jnp.mean(dn * n, -1, keepdims=True))


def colsum(x):
    return jnp.sum(x.astype(F32), axis=0, keepdims=True)


MESH = pl.DeviceIdType.MESH
ANY = pl.BlockSpec(memory_space=pl.ANY)
VM = pl.BlockSpec(memory_space=pltpu.VMEM)


def flip(index, bit):
    return index + bit - 2 * bit * lax.rem(index // bit, 2)


def flips(index, mask):
    bit = 1
    while bit <= mask:
        if mask & bit:
            index = flip(index, bit)
        bit *= 2
    return index


def span(bits):
    masks = [0]
    for bit in bits:
        masks += [m | bit for m in masks]
    return masks


def orders(fsdp):
    bits = [1 << k for k in range(fsdp.bit_length() - 1)]
    return bits[1:] + bits[:1], bits[:0:-1] + bits[:1]


class Place:
    def __init__(self, fsdp, tensor):
        self.fsdp, self.tensor = fsdp, tensor
        self.i, self.j = lax.axis_index("fsdp"), lax.axis_index("tensor")
        self.half = tensor // 2
        self.c = lax.rem(self.i, 2)
        self.h = self.j // self.half
        self.on = self.c == self.h
        self.off = self.c != self.h
        self.twin = flip(self.i, 1)
        self.swap = lax.rem(self.j + self.half, tensor)
        self.block = jnp.where(self.on, self.j, self.swap)
        self.edge = self.half - 1 + self.c
        self.end = self.c * (tensor - 1)
        self.mate = self.h * tensor + 1 - self.j
        self.is_edge = self.j == self.edge
        self.is_end = self.j == self.end

    def other(self, k):
        return (1 - self.c) * (self.half + k) + self.c * (self.half - 1 - k)

    def near(self, n):
        low = jnp.where(self.h == 0, self.j, self.tensor - 1 - self.j)
        if isinstance(n, int):
            place = low if n == 0 else 1 - low if n == 1 else n
        else:
            place = jnp.where(n == 0, low, jnp.where(n == 1, 1 - low, n))
        return jnp.where(self.h == 0, place, self.tensor - 1 - place)

    def barrier(self):
        sem = pltpu.get_barrier_semaphore()
        others = [(self.i, lax.rem(self.j + k, self.tensor)) for k in range(1, self.tensor)]
        bit = 1
        while bit < self.fsdp:
            others.append((flip(self.i, bit), self.j))
            bit *= 2
        others.append((self.twin, self.swap))
        for i, j in others:
            pl.semaphore_signal(sem, inc=1, device_id=(i, j), device_id_type=MESH)
        pl.semaphore_wait(sem, len(others))


class Sends:
    def __init__(self, place, send, recv):
        self.place, self.send, self.recv, self.n, self.started = place, send, recv, 0, []

    def slots(self, n):
        self.n += n
        return self.n - n

    def slot(self):
        return self.slots(1)

    def copy(self, src, dst, slot, i, j, back=None):
        return pltpu.make_async_remote_copy(src_ref=src, dst_ref=dst, send_sem=self.send.at[slot if back is None else back],
                                            recv_sem=self.recv.at[slot], device_id=(i, j), device_id_type=MESH)

    def start(self, src, dst, slot, i, j, when=None, back=None, note=True):
        copy = self.copy(src, dst, slot, i, j, back)
        copy.start() if when is None else pl.when(when)(copy.start)
        if note:
            self.started.append((copy, when))

    def arrive(self, dst, slot, when=None):
        copy = self.copy(dst, dst, slot, self.place.i, self.place.j)
        copy.wait_recv() if when is None else pl.when(when)(copy.wait_recv)

    def left(self, src, slot, when=None):
        copy = self.copy(src, src, slot, self.place.i, self.place.j)
        copy.wait_send() if when is None else pl.when(when)(copy.wait_send)

    def finish(self):
        for copy, when in self.started:
            copy.wait_send() if when is None else pl.when(when)(copy.wait_send)
        self.started = []


class Stream:
    def __init__(self, sends, array, lead, shard, order, own):
        self.s, self.p, self.a, self.lead, self.shard, self.order, self.own = sends, sends.place, array, lead, shard, order, own
        n = self.p.tensor
        self.z, self.back = sends.slots(n), sends.slots(1)
        self.hops = [{m: sends.slots(n) for m in span(order[:k])} for k in range(len(order))]

    def block(self, t, mask):
        rows = pl.ds(pl.multiple_of(flips(self.p.i, mask) * self.shard, self.shard), self.shard)
        return self.a.at[(*self.lead, t, rows)]

    def first_line(self):
        s, p = self.s, self.p
        there = self.block(p.j, 0)
        s.start(self.own, there, self.z + p.j, p.i, p.j + 1, p.j + 1 < p.tensor, note=False)
        s.start(self.own, there, self.z + p.j, p.i, p.j - 1, p.j > 0, self.back, note=False)

    def first_fan(self):
        self.fan(0, 0, self.p.j, self.own)

    def fan(self, mask, k, t, src=None):
        for n in range(k, len(self.order)):
            there = self.block(t, mask)
            self.s.start(there if src is None else src, there, self.hops[n][mask] + t, flip(self.p.i, self.order[n]), self.p.j, note=False)

    def line(self, n):
        s, p = self.s, self.p
        t = p.near(n)
        there = self.block(t, 0)
        s.arrive(there, self.z + t)
        ahead = p.j + jnp.where(t < p.j, 1, -1)
        s.start(there, there, self.z + t, p.i, ahead, (ahead >= 0) & (ahead < p.tensor), note=False)
        self.fan(0, 0, t)

    def finish(self):
        s, p = self.s, self.p
        here = self.block(p.j, 0)
        s.left(here, self.z + p.j, p.j + 1 < p.tensor)
        s.left(here, self.back, p.j > 0)
        for n in range(p.tensor):
            t = p.near(n)
            if n > 0:
                ahead = p.j + jnp.where(t < p.j, 1, -1)
                s.left(here, self.z + t, (ahead >= 0) & (ahead < p.tensor))
            for hops in self.hops:
                for slot in hops.values():
                    s.left(here, slot + t)

    def hop(self, k, n):
        t = self.p.near(n)
        for m in self.hops[k]:
            mask = m | self.order[k]
            self.s.arrive(self.block(t, mask), self.hops[k][m] + t)
            self.fan(mask, k + 1, t)


def attend_group(heads, g, x, own_rows, w_kv, w_qo, smalls, kv, q, att, inv, s_ref, exps, before, after):
    width = heads * 128
    kv[g] = project_keys(x[...], w_kv[g], smalls[g, 0:1, :width])
    q[g] = project_query(x[own_rows, :], w_qo[g], smalls[g, 0:1, width:])
    for h in range(heads):
        cols = slice(h * 128, h * 128 + 128)
        keys = kv[g, :, cols]
        s_ref[...] = dot(keys, q[g, :, cols], NT)
        top = jnp.max(s_ref[...], axis=0, keepdims=True)
        e = jnp.exp(s_ref[...] - top)
        scale = 1.0 / jnp.sum(e, axis=0, keepdims=True)
        before(h)
        exps[h] = e.astype(BF16)
        out = dot(keys, exps[h], TN) * scale
        out = jnp.where(lax.broadcasted_iota(jnp.int32, out.shape, 0) >= HEAD, out, 0.0)
        att[g, :, cols] = out.T.astype(BF16)
        inv[g, h:h + 1] = scale
        after(h)


def first_kernel(fsdp, tensor, pack, small, tok, cot, w0_out, w1, x_out, own_out, cot_out, kv_out, q_out, att_out, exp_out,
                 inv, smalls, w0, sm, x, kv, q, att, s_ref, exps, send, recv, local):
    p = Place(fsdp, tensor)
    s = Sends(p, send, recv)
    rows, model = tok.shape
    shard = pack.shape[1]
    heads = exps.shape[0]
    first, second = orders(fsdp)
    kvw = Stream(s, w0, (0,), shard, first, pack.at[0])
    qow = Stream(s, w0, (1,), shard, second, pack.at[1])
    tiny = Stream(s, sm, (), small.shape[0], first, small)
    upper = Stream(s, w1, (pl.ds(0, 2),), shard, first, pack.at[pl.ds(2, 2)])
    lower = Stream(s, w1, (pl.ds(2, 2),), shard, second, pack.at[pl.ds(4, 2)])
    now, later = (kvw, qow, tiny), (upper, lower)
    pieces = 4 if rows % 64 == 0 else 1
    part = rows // pieces
    xin, xtwin, cslot = s.slots(tensor * pieces), s.slots(tensor * pieces), s.slots(1)
    x_at = lambda t: x.at[pl.ds(pl.multiple_of(t * rows, rows), rows)]

    def piece(t, u):
        return x.at[pl.ds(pl.multiple_of(t * rows + u * part, part), part)]

    def send_rows(t, u, i, j, when, twin=False, src=None):
        slot = t * pieces + u
        there = piece(t, u)
        s.start(there if src is None else src.at[pl.ds(u * part, part)], there, xin + slot, i, j, when, xtwin + slot if twin else None)

    def pass_rows(u, n, when, forward):
        t = p.near(n)
        s.arrive(piece(t, u), xin + t * pieces + u, when)
        if forward:
            send_rows(t, u, p.i, p.end, when)
        send_rows(t, u, p.twin, p.j, when, True)

    def edge_rows(u):
        for n in [*range(2, tensor), 1]:
            pass_rows(u, n, p.on & p.is_edge, p.half > 1 and n > 1)

    def end_rows(u):
        for n in range(1, tensor):
            pass_rows(u, n, p.on & jnp.logical_not(p.is_edge), False)
    locals_ = []

    def keep(src, dst, when=None):
        copy = pltpu.make_async_copy(src, dst, local.at[len(locals_)])
        copy.start() if when is None else pl.when(when)(copy.start)
        locals_.append((copy, when))
        return len(locals_) - 1

    def kept(k):
        copy, when = locals_[k]
        copy.wait() if when is None else pl.when(when)(copy.wait)
        locals_[k] = None

    mine = pl.ds(pl.multiple_of(p.i * shard, shard), shard)
    own = [keep(pack.at[k], w0.at[k, p.j, mine]) for k in range(2)]
    own += [keep(pack.at[2 + k], w1.at[k, p.j, mine]) for k in range(4)]
    own += [keep(small, sm.at[p.j, pl.ds(pl.multiple_of(p.i * small.shape[0], small.shape[0]), small.shape[0])])]
    own += [keep(tok, x_at(p.j), p.on), keep(cot, cot_out, p.on)]
    p.barrier()
    for g in now:
        g.first_line()
    for g in now:
        g.first_fan()
    for u in range(pieces):
        send_rows(p.j, u, p.i, p.edge, p.off, src=tok)
        if p.half > 1:
            send_rows(p.j, u, p.i, p.mate, p.on, src=tok)
        send_rows(p.j, u, p.twin, p.j, p.on, True, tok)
    for g in later:
        g.first_fan()
    stages = len(first)
    for step in range(1, tensor + stages - 1):
        if step < tensor:
            for g in now:
                g.line(step)
        for k in range(stages - 1):
            if 0 <= step - 1 - k < tensor:
                for g in now:
                    g.hop(k, step - 1 - k)
        if step - 1 < pieces:
            edge_rows(step - 1)
    for u in range(tensor + stages - 2, pieces):
        edge_rows(u)
    for u in range(pieces):
        end_rows(u)
    for g in later:
        g.first_line()
    for k in range(stages - 1):
        for g in later:
            g.hop(k, 0)
    s.start(cot, cot_out, cslot, p.twin, p.swap, p.off)
    for n in range(tensor):
        for g in now:
            g.hop(stages - 1, n)
    for t in range(tensor):
        for u in range(pieces):
            s.arrive(piece(t, u), xin + t * pieces + u, p.off)
    for k in own[:8]:
        kept(k)
    for t in range(tensor):
        total = sm[t, :small.shape[0], :]
        for i in range(1, fsdp):
            total += sm[t, i * small.shape[0]:(i + 1) * small.shape[0], :]
        smalls[t] = total
    keep(x_at(p.block), own_out)
    for t in range(tensor):
        keep(x_at(t), x_out.at[pl.ds(t * rows, rows)])
    for k in range(2):
        keep(w0.at[k], w0_out.at[k])
    fixed = len(locals_)
    sem = lambda k: local.at[fixed + k]

    def group(g, carry):
        def exp_copy(h, g):
            return pltpu.make_async_copy(exps.at[h], exp_out.at[g, h], sem(h))

        def before(h):
            pl.when(g > 0)(lambda: exp_copy(h, g - 1).wait())

        def after(h):
            exp_copy(h, g).start()
            point = {0: 0, heads // 2: 1, heads - 1: 2}.get(h)
            if point == 0:
                @pl.when(g >= 2)
                def _():
                    for st in later:
                        for k in range(1, stages - 1):
                            st.hop(k, g - 1)
            if point == 1:
                @pl.when(g >= 1)
                def _():
                    for st in later:
                        st.hop(0, g)
            if point == 2:
                @pl.when(g < tensor - 1)
                def _():
                    for st in later:
                        st.line(g + 1)

        attend_group(heads, g, x, pl.ds(pl.multiple_of(p.block * rows, rows), rows), w0.at[0], w0.at[1], smalls, kv, q, att, inv,
                     s_ref, exps, before, after)
        for k, (src, dst) in enumerate(((kv, kv_out), (q, q_out), (att, att_out))):
            pltpu.make_async_copy(src.at[g], dst.at[g], sem(heads + k * tensor + g)).start()
        return carry

    lax.fori_loop(0, tensor, group, 0)
    for k in range(1, stages - 1):
        for st in later:
            st.hop(k, tensor - 1)
    for n in range(tensor):
        for st in later:
            st.hop(stages - 1, n)
    for h in range(heads):
        pltpu.make_async_copy(exps.at[h], exp_out.at[0, h], sem(h)).wait()
    for k, (src, dst) in enumerate(((kv, kv_out), (q, q_out), (att, att_out))):
        for g in range(tensor):
            pltpu.make_async_copy(src.at[g], dst.at[g], sem(heads + k * tensor + g)).wait()
    s.arrive(cot_out, cslot, p.off)
    for k in range(len(locals_)):
        if locals_[k] is not None:
            kept(k)
    s.finish()
    for st in now + later:
        st.finish()


def first_part(fsdp, tensor, pack, small, tok, cot):
    chunks, shard, width = pack.shape
    rows, model = tok.shape
    heads, keys = width // 128, tensor * rows
    slots = 5 * (tensor + 1 + (fsdp - 1) * tensor) + 8 * tensor + 1
    return pl.pallas_call(
        functools.partial(first_kernel, fsdp, tensor),
        in_specs=[VM] * 4, out_specs=[ANY] * 9 + [VM] * 2,
        out_shape=[jax.ShapeDtypeStruct(s, d) for s, d in [
            ((2, tensor, model, width), BF16), ((4, tensor, model, width), BF16), ((keys, model), BF16), ((rows, model), BF16),
            ((rows, model), BF16), ((tensor, keys, width), BF16), ((tensor, rows, width), BF16), ((tensor, rows, width), BF16),
            ((tensor, heads, keys, rows), BF16), ((tensor, 8, rows), F32), ((tensor, *small.shape), F32)]],
        scratch_shapes=[pltpu.VMEM(s, d) for s, d in [
            ((2, tensor, model, width), BF16), ((tensor, fsdp * small.shape[0], model), F32), ((keys, model), BF16),
            ((tensor, keys, width), BF16), ((tensor, rows, width), BF16), ((tensor, rows, width), BF16), ((keys, rows), F32),
            ((heads, keys, rows), BF16)]] + [pltpu.SemaphoreType.DMA((slots,)), pltpu.SemaphoreType.DMA((slots,)),
                                             pltpu.SemaphoreType.DMA((16 + 5 * tensor + heads,))],
        compiler_params=pltpu.CompilerParams(collective_id=0, has_side_effects=True, vmem_limit_bytes=VMEM_LIMIT),
    )(pack, small, tok, cot)


class Loads:
    def __init__(self, sems):
        self.sems, self.n = sems, 0

    def slots(self, n):
        self.n += n
        return self.n - n

    def load(self, src, dst):
        copy = pltpu.make_async_copy(src, dst, self.sems.at[self.slots(1)])
        copy.start()
        return copy

    def series(self, src, dst, n):
        first = self.slots(n)
        for k in range(n):
            pltpu.make_async_copy(src.at[k], dst.at[k], self.sems.at[first + k]).start()
        return lambda k: pltpu.make_async_copy(src.at[k], dst.at[k], self.sems.at[first + k]).wait()


def middle_kernel(groups, x_hbm, cot_hbm, att_hbm, w0_hbm, w1_hbm, smalls, inv,
                  out_ref, out_low, resid_ref, r_ref, datt_hbm, g_o_hbm, g_hbm, g_bup, g_vecs,
                  x_own, cot, att, w_qo, w1, datt, g_o, grads, act, slope, hid, n1_ref, acc, low, hl, sems):
    ld = Loads(sems)
    width = w_qo.shape[2]
    get_x = ld.load(x_hbm, x_own)
    get_att = ld.series(att_hbm, att, groups)
    get_qo = ld.series(w0_hbm.at[1], w_qo, groups)
    gets = [ld.series(w1_hbm.at[k], w1.at[k], groups) for k in range(4)]
    get_cot = ld.load(cot_hbm, cot)
    outs = [(grads.at[k], g_hbm.at[k], ld.slots(groups)) for k in range(4)]
    outs += [(datt, datt_hbm, ld.slots(groups)), (g_o, g_o_hbm, ld.slots(groups))]

    def put(k, g):
        src, dst, first = outs[k]
        return pltpu.make_async_copy(src.at[g], dst.at[g], sems.at[first + g])

    vec = lambda k: smalls[0, 2 + k:3 + k, :]
    get_x.wait()
    acc[...] = x_own[...].astype(F32) + vec(0)

    def branch(g, c):
        get_att(g)
        get_qo(g)
        acc[...] += dot(att[g], w_qo[g], NT)
        return c

    lax.fori_loop(0, groups, branch, 0)
    n1, inv1 = norm_forward(acc[...])
    n1_ref[...] = n1
    hidden = n1 * vec(2) + vec(3)
    hid[...] = hidden
    hl[...] = hidden.astype(BF16)
    acc[...] = hidden + vec(1)

    def forward(g, c):
        for k in range(2):
            gets[2 * k](g)
            gets[2 * k + 1](g)
            pre = dot(hl[...], w1[2 * k, g], NN) + smalls[g, 1:2, k * width:(k + 1) * width]
            phi = 0.5 + 0.5 * lax.erf(pre * np.float32(0.5 ** 0.5))
            slope[g, k] = phi + pre * (jnp.exp(-0.5 * pre * pre) * np.float32((2 * np.pi) ** -0.5))
            act[g, k] = (pre * phi).astype(BF16)
            acc[...] += dot(act[g, k], w1[2 * k + 1, g], NT)
        return c

    lax.fori_loop(0, groups, forward, 0)
    n2, inv2 = norm_forward(acc[...])
    out = n2 * vec(4) + vec(5)
    out_ref[...] = out
    out_low[...] = out.astype(BF16)
    get_cot.wait()
    cott = cot[...].astype(F32)
    g_vecs[4:5] = colsum(cott * n2)
    g_vecs[5:6] = colsum(cott)
    resid = norm_backward(n2, inv2, cott * vec(4))
    acc[...] = resid
    low[...] = resid.astype(BF16)
    g_vecs[1:2] = colsum(low[...])

    def back(g, c):
        for k in range(2):
            grads[2 * k + 1, g] = dot(low[...], act[g, k], TN).astype(BF16)
            put(2 * k + 1, g).start()
            gp = (dot(low[...], w1[2 * k + 1, g], NN) * slope[g, k]).astype(BF16)
            act[g, k] = gp
            g_bup[g, :, k * width:(k + 1) * width] = colsum(gp)
            grads[2 * k, g] = dot(hl[...], gp, TN).astype(BF16)
            put(2 * k, g).start()
            acc[...] += dot(act[g, k], w1[2 * k, g], NT)
        return c

    lax.fori_loop(0, groups, back, 0)
    gh = acc[...]
    g_vecs[2:3] = colsum(gh * n1_ref[...])
    g_vecs[3:4] = colsum(gh)
    ga = norm_backward(n1_ref[...], inv1, gh * vec(2))
    resid_ref[...] = ga
    low[...] = ga.astype(BF16)
    g_vecs[0:1] = colsum(low[...])
    g_vecs[6:8] = jnp.zeros_like(g_vecs[6:8])

    def last(g, c):
        da = dot(low[...], w_qo[g], NN)
        da = jnp.where(lanes_from(da.shape, False), da, 0.0).T.astype(BF16).astype(F32)
        prod = da * att[g].T.astype(F32)
        for h in range(width // 128):
            cols = slice(h * 128, h * 128 + 128)
            scale = inv[g, h:h + 1]
            r_ref[g, h:h + 1] = jnp.sum(prod[cols], axis=0, keepdims=True) * scale
            datt[g, :, cols] = (da[cols] * scale).T.astype(BF16)
        put(4, g).start()
        g_o[g] = dot(low[...], att[g], TN).astype(BF16)
        put(5, g).start()
        return c

    lax.fori_loop(0, groups, last, 0)
    for k in range(6):
        for g in range(groups):
            put(k, g).wait()


def middle_part(x_own, cot, att, w0, w1, smalls, inv):
    _, groups, model, width = w0.shape
    rows = x_own.shape[0]
    wide, deep = ((groups, rows, width), BF16), ((groups, model, width), BF16)
    flat, low = ((rows, model), F32), ((rows, model), BF16)
    return pl.pallas_call(
        functools.partial(middle_kernel, groups),
        in_specs=[ANY] * 5 + [VM] * 2, out_specs=[VM] * 4 + [ANY, ANY, ANY, VM, VM],
        out_shape=[jax.ShapeDtypeStruct(s, d) for s, d in [
            flat, low, flat, ((groups, 8, rows), F32), wide, deep, ((4, groups, model, width), BF16), ((groups, 1, 2 * width), F32), ((8, model), F32)]],
        scratch_shapes=[pltpu.VMEM(s, d) for s, d in [
            low, low, wide, deep, ((4, groups, model, width), BF16), wide, deep, ((4, groups, model, width), BF16),
            ((groups, 2, rows, width), BF16), ((groups, 2, rows, width), F32), flat, flat, flat, low, low]]
        + [pltpu.SemaphoreType.DMA((12 * groups + 2,))],
        compiler_params=pltpu.CompilerParams(vmem_limit_bytes=VMEM_LIMIT),
    )(x_own, cot, att, w0, w1, smalls, inv)


class Fold:
    def __init__(self, sends, give, keep, lead, halves, inbox, order, out):
        self.s, self.p, self.give, self.keep, self.lead = sends, sends.place, give, keep, lead
        self.halves, self.inbox, self.order, self.out = halves, inbox, order[::-1], out
        n = self.p.tensor
        self.masks = [span(self.order[k + 1:]) for k in range(len(order))]
        self.slot = [[sends.slots(n) for _ in masks] for masks in self.masks]
        self.z = sends.slots(2 * n)

    def half(self, k, mask, t):
        return self.halves[k].at[(self.lead, self.masks[k].index(mask), t)]

    def first(self, n):
        t, bit = self.p.near(n), self.order[0]
        for k, m in enumerate(self.masks[0]):
            self.s.start(self.give(t, m | bit), self.half(0, m, t), self.slot[0][k] + t, flip(self.p.i, bit), self.p.j, note=False)

    def add(self, k, n):
        t = self.p.near(n)
        for at, m in enumerate(self.masks[k]):
            here = self.half(k, m, t)
            self.s.arrive(here, self.slot[k][at] + t)
            mine = self.keep(t, at) if k == 0 else self.half(k - 1, m, t)
            here[...] = (here[...].astype(F32) + mine[...].astype(F32)).astype(BF16)
        if k + 1 < len(self.order):
            bit = self.order[k + 1]
            for at, m in enumerate(self.masks[k + 1]):
                self.s.start(self.half(k, m | bit, t), self.half(k + 1, m, t), self.slot[k + 1][at] + t,
                             flip(self.p.i, bit), self.p.j, note=False)

    def total(self, t):
        return self.half(len(self.order) - 1, 0, t)

    def way(self, n):
        t = self.p.near(n)
        right = t > self.p.j
        there = self.p.j + jnp.where(right, 1, -1)
        before = self.p.j - jnp.where(right, 1, -1)
        side = jnp.where(right, 0, 1)
        has = (before >= 0) & (before < self.p.tensor)
        return t, there, has, self.inbox.at[(self.lead, side, t)], self.z + side * self.p.tensor + t

    def line_first(self, n):
        t, there, has, box, slot = self.way(n)
        self.s.start(self.total(t), box, slot, self.p.i, there, jnp.logical_not(has), note=False)

    def line_next(self, n):
        t, there, has, box, slot = self.way(n)
        total = self.total(t)

        @pl.when(has)
        def _():
            self.s.arrive(box, slot)
            box[...] = (box[...].astype(F32) + total[...].astype(F32)).astype(BF16)
            self.s.start(box, box, slot, self.p.i, there, note=False)

    def result(self):
        p = self.p
        self.out[...] = self.total(p.j)[...].astype(F32)
        for side, there in ((0, p.j > 0), (1, p.j < p.tensor - 1)):
            box = self.inbox.at[(self.lead, side, p.j)]

            @pl.when(there)
            def _(box=box, side=side):
                self.s.arrive(box, self.z + side * p.tensor + p.j)
                self.out[...] += box[...].astype(F32)

    def finish(self):
        here = self.half(0, self.masks[0][0], 0)
        for n in range(self.p.tensor):
            t = self.p.near(n)
            for slots in self.slot:
                for slot in slots:
                    self.s.left(here, slot + t)
            if n > 0:
                self.s.left(here, self.way(n)[4])


def last_kernel(fsdp, tensor, x_hbm, w0_hbm, kv_hbm, q_hbm, do_hbm, g_o_hbm, g_hbm, e_hbm, resid_hbm, low_hbm, r, g_bup, g_vecs,
                shards, dx, tiny, swapped, *scratch):
    bits = fsdp.bit_length() - 1
    halves, scratch = scratch[:bits], scratch[bits:]
    (inbox, own_g, x, w0, kv, q, do, dqt, wacc, exps, gw, dkv, dxb, own, twin_in, mate_in, fin_in, tiny_in, send, recv, local) = scratch
    p = Place(fsdp, tensor)
    s, ld = Sends(p, send, recv), Loads(local)
    _, heads, rows, _ = exps.shape
    model, width = gw.shape[2:]
    shard = model // fsdp
    first, second = orders(fsdp)
    block_rows = lambda mask: pl.ds(pl.multiple_of(flips(p.i, mask) * shard, shard), shard)
    pair = lambda k: pl.ds(2 * k, 2)
    stay = [m for m in span(first[::-1][1:])]
    folds = []
    for k, order in enumerate((first, second)):
        masks = span(order[::-1][1:])
        folds.append(Fold(s, lambda t, m, k=k: g_hbm.at[pair(k), t, block_rows(m)],
                          lambda t, at, k=k, masks=masks: own_g.at[pair(k), t, stay.index(masks[at])],
                          pair(k + 1), halves, inbox, order, shards.at[pair(k + 1)]))
    tails = []
    for k, order in enumerate((first, second)):
        masks = span(order[::-1][1:])
        tails.append(Fold(s, lambda t, m, k=k: gw.at[pl.ds(k, 1), t, block_rows(m)],
                          lambda t, at, k=k, masks=masks: gw.at[pl.ds(k, 1), t, block_rows(masks[at])],
                          pl.ds(k, 1), halves, inbox, order, shards.at[pl.ds(k, 1)]))
    stages = bits

    steps = tensor * tensor
    step_sem, x_sem = ld.slots(4), ld.slots(2)

    def step_copies(step, slot):
        t, g = p.near(tensor - 1 - step // tensor), p.near(tensor - 1 - lax.rem(step, tensor))
        here = pl.ds(pl.multiple_of(t * rows, rows), rows)
        return (pltpu.make_async_copy(e_hbm.at[g, :, here], exps.at[slot], local.at[step_sem + slot]),
                pltpu.make_async_copy(kv_hbm.at[g, here], kv.at[slot], local.at[step_sem + 2 + slot]))

    def x_copy(it, slot):
        t = p.near(tensor - 1 - it)
        return pltpu.make_async_copy(x_hbm.at[pl.ds(pl.multiple_of(t * rows, rows), rows)], x.at[slot], local.at[x_sem + slot])

    for copy in step_copies(0, 0):
        copy.start()
    gets = [ld.load(do_hbm, do), ld.load(q_hbm, q)]
    x_copy(0, 0).start()
    gets.append(ld.load(w0_hbm, w0))
    own_gets = [ld.load(g_hbm.at[:, :, block_rows(m)], own_g.at[:, :, at]) for at, m in enumerate(stay)]
    gets.append(ld.load(g_o_hbm, gw.at[1]))
    gets.append(ld.load(resid_hbm, own))
    own_sem = ld.slots(1)
    tiny[:8] = g_vecs[...]
    for t in range(tensor):
        tiny[8 + t:9 + t] = g_bup[t]
    tiny[8 + tensor:] = jnp.zeros_like(tiny[8 + tensor:])
    p.barrier()
    for n in range(tensor)[::-1]:
        for f in folds:
            f.first(n)
    swap_slot = s.slots(1)
    s.start(low_hbm, swapped, swap_slot, p.twin, p.swap, p.off)
    twin, mate, fin = s.slots(tensor), s.slots(tensor), s.slots(1)
    fin_send, own_slot = s.slots(tensor), s.slots(1)
    tiny_slots = s.slots((fsdp * tensor).bit_length() - 1)
    wacc[...] = jnp.zeros_like(wacc)
    dqt[...] = jnp.zeros_like(dqt)
    for copy in gets + own_gets:
        copy.wait()

    def rows_to_twin(n, slot):
        t = p.near(n)
        s.start(dxb.at[slot], twin_in.at[t], twin + t, p.twin, p.j, p.off, note=False)

    def rows_from_twin(n, slot):
        t = p.near(n)

        @pl.when(p.on)
        def _():
            s.arrive(twin_in.at[t], twin + t)
            twin_in[t] = (twin_in[t].astype(F32) + dxb[slot].astype(F32)).astype(BF16)
        if p.half > 1:
            to_mate = p.on & ((n == 1) | ((n > 1) & p.is_end))
            s.start(twin_in.at[t], mate_in.at[t], mate + t, p.i, p.mate, to_mate, note=False)
        else:
            s.start(twin_in.at[t], fin_in, fin, p.i, t, p.on, fin_send + t, note=False)

    def rows_from_mate(n):
        t = p.near(n)
        here = p.on & p.is_edge

        @pl.when(here)
        def _():
            s.arrive(mate_in.at[t], mate + t)
            mate_in[t] = (mate_in[t].astype(F32) + twin_in[t].astype(F32)).astype(BF16)
        s.start(mate_in.at[t], fin_in, fin, p.i, t, here, fin_send + t, note=False)

    def one(it, gi):
        n = tensor - 1 - it
        t, g = p.near(n), p.near(tensor - 1 - gi)
        step = it * tensor + gi
        slot, x_slot = lax.rem(step, 2), lax.rem(it, 2)
        for copy in step_copies(step, slot):
            copy.wait()

        @pl.when(step + 1 < steps)
        def _():
            for copy in step_copies(step + 1, 1 - slot):
                copy.start()

        @pl.when(gi == 0)
        def _():
            x_copy(it, x_slot).wait()

            pl.when(it + 1 < tensor)(x_copy(it + 1, 1 - x_slot).start)
            dx[...] = jnp.zeros_like(dx)

            @pl.when(it + 1 == tensor)
            def _():
                copy = pltpu.make_async_copy(x_hbm.at[pl.ds(pl.multiple_of(p.block * rows, rows), rows)], x.at[1 - x_slot], local.at[own_sem])
                copy.start()
                copy.wait()

        for h in range(heads):
            cols = slice(h * 128, h * 128 + 128)
            k = kv[slot, :, cols]
            d = do[g, :, cols]
            e = exps[slot, h]
            ds = (e.astype(F32) * (dot(k, d, NT) - r[g, h:h + 1])).astype(BF16)
            dkv[:, cols] = (dot(ds, q[g, :, cols], NN) + dot(e, d, NN)).astype(BF16)
            dqt[g, h] += dot(k, ds, TN)
        dk = dkv[...]
        bias = pl.ds(8 + tensor + g, 1)
        tiny[bias, :width] += colsum(dk)
        dx[...] += dot(dk, w0[0, g], NT)
        wacc[g] += dot(x[x_slot], dk, TN)

        @pl.when(it == tensor - 1)
        def _():
            for h in range(heads):
                cols = slice(h * 128, h * 128 + 128)
                dq = dqt[g, h] * np.float32(HEAD ** -0.5)
                dq = jnp.where(lax.broadcasted_iota(jnp.int32, dq.shape, 0) < HEAD, dq, 0.0)
                dkv[:, cols] = dq.T.astype(BF16)
            dq = dkv[...]
            tiny[bias, width:] = colsum(dq)
            own[...] += dot(dq, w0[1, g], NT)
            gw[1, g] = (dot(x[1 - x_slot], dq, TN) + gw[1, g].astype(F32)).astype(BF16)
            gw[0, g] = wacc[g].astype(BF16)
            for f in tails:
                f.first(tensor - 1 - gi)

        @pl.when((gi == 0) & (it >= 1))
        def _():
            for f in folds:
                for k in range(2, stages):
                    f.add(k, n + 1)
                f.line_first(n + 1)

        @pl.when((gi == 0) & (it >= 2))
        def _():
            if p.half > 1:
                rows_from_mate(n + 2)

        @pl.when(gi == 0)
        def _():
            for f in folds:
                f.add(0, n)

        @pl.when((gi == min(1, tensor - 1)) & (it >= 1))
        def _():
            rows_from_twin(n + 1, 1 - x_slot)

        @pl.when(gi == min(2, tensor - 1))
        def _():
            for f in folds:
                f.add(1, n)

        @pl.when((gi == tensor - 1) & (it >= 1))
        def _():
            for f in folds:
                f.line_next(n + 1)

        @pl.when((it == tensor - 1) & (gi >= 1))
        def _():
            for f in tails:
                f.add(0, tensor - gi)

        @pl.when((gi == tensor - 1) & (it < tensor - 1))
        def _():
            pl.when((it >= 2) & p.off)(lambda: s.left(dxb.at[x_slot], twin + p.near(n + 2)))
            dxb[x_slot] = dx[...].astype(BF16)
            rows_to_twin(n, x_slot)

    def body(step, carry):
        one(step // tensor, lax.rem(step, tensor))
        return carry

    lax.fori_loop(0, steps, body, 0)
    last_slot = (tensor - 1) % 2

    @pl.when(p.off)
    def _():
        if tensor > 2:
            s.left(dxb.at[last_slot], twin + p.near(2))
        dxb[last_slot] = dx[...].astype(BF16)
        mate_in[1] = own[...].astype(BF16)
    rows_to_twin(0, last_slot)
    s.start(mate_in.at[1], mate_in.at[0], own_slot, p.twin, p.swap, p.off)

    tiny_at = [0]

    def tiny_step(begin, end):
        k = tiny_at[0]
        if k == len(range((fsdp * tensor).bit_length() - 1)):
            return
        bit = 1 << k
        i, j = (flip(p.i, bit), p.j) if bit < fsdp else (p.i, flip(p.j, bit // fsdp))
        copy = s.copy(tiny, tiny_in.at[k], tiny_slots + k, i, j)
        if begin:
            copy.start()
        if end:
            copy.wait_recv()
            copy.wait_send()
            tiny[...] += tiny_in[k]
            tiny_at[0] += 1

    tiny_step(True, False)
    for f in folds:
        for k in range(2, stages):
            f.add(k, 0)
    for f in tails:
        f.add(0, 0)
    for n in range(tensor)[::-1]:
        for f in tails:
            f.add(1, n)
        if n < tensor - 1:
            for f in tails:
                for k in range(2, stages):
                    f.add(k, n + 1)
                f.line_first(n + 1)
        tiny_step(False, True)
        tiny_step(True, False)
    for f in folds:
        f.result()
    for f in tails:
        for k in range(2, stages):
            f.add(k, 0)
    for n in range(1, tensor)[::-1]:
        for f in tails:
            f.line_next(n)
        tiny_step(False, True)
        tiny_step(True, False)
    while tiny_at[0] < (fsdp * tensor).bit_length() - 1:
        tiny_step(False, True)
        tiny_step(True, False)

    @pl.when(p.on)
    def _():
        s.arrive(twin_in.at[p.j], twin + p.j)
        dx[...] += own[...] + twin_in[p.j].astype(F32)
        if p.half > 1:
            s.arrive(mate_in.at[p.j], mate + p.j)
            dx[...] += mate_in[p.j].astype(F32)

    @pl.when(p.off)
    def _():
        s.arrive(fin_in, fin)
        s.arrive(mate_in.at[0], own_slot)
        dx[...] = fin_in[...].astype(F32) + mate_in[0].astype(F32)
    s.arrive(swapped, swap_slot, p.off)
    for f in tails:
        f.result()
    for n in range(tensor):
        t = p.near(n)
        if n < 2:
            s.left(dxb.at[0], twin + t, p.off)
        if n > 0:
            if p.half > 1:
                s.left(dxb.at[0], mate + t, p.on & ((n == 1) | p.is_end))
                if n > 1:
                    s.left(dxb.at[0], fin_send + t, p.on & p.is_edge)
            else:
                s.left(dxb.at[0], fin_send + t, p.on)
    for f in folds + tails:
        f.finish()
    s.finish()


def last_part(fsdp, tensor, x, w0, kv, q, do, g_o, g, e, resid, low, r, g_bup, g_vecs):
    groups, heads, _, rows = e.shape
    model, width = w0.shape[2:]
    shard = model // fsdp
    bits = fsdp.bit_length() - 1
    vm = lambda d, *shape: pltpu.VMEM(shape, d)
    slots = 4 * ((fsdp - 1) * tensor + 2 * tensor) + 3 * tensor + 16
    scratch = [vm(BF16, 6, fsdp >> (k + 1), tensor, shard, width) for k in range(bits)]
    scratch += [vm(BF16, 6, 2, tensor, shard, width), vm(BF16, 4, tensor, fsdp // 2, shard, width), vm(BF16, 2, rows, model),
                vm(BF16, 2, tensor, model, width), vm(BF16, 2, rows, width), vm(BF16, tensor, rows, width), vm(BF16, tensor, rows, width),
                vm(F32, tensor, heads, 128, rows), vm(F32, tensor, model, width), vm(BF16, 2, heads, rows, rows),
                vm(BF16, 2, tensor, model, width), vm(BF16, rows, width), vm(BF16, 2, rows, model), vm(F32, rows, model), vm(BF16, tensor, rows, model),
                vm(BF16, tensor, rows, model), vm(BF16, rows, model), vm(F32, (fsdp * tensor).bit_length() - 1, 8 + 2 * tensor, model),
                pltpu.SemaphoreType.DMA((slots,)), pltpu.SemaphoreType.DMA((slots,)), pltpu.SemaphoreType.DMA((16 + fsdp,))]
    return pl.pallas_call(
        functools.partial(last_kernel, fsdp, tensor),
        in_specs=[ANY] * 10 + [VM] * 3, out_specs=[VM] * 3 + [ANY],
        out_shape=[jax.ShapeDtypeStruct(s, d) for s, d in [
            ((6, shard, width), F32), ((rows, model), F32), ((8 + 2 * tensor, model), F32), ((rows, model), BF16)]],
        scratch_shapes=scratch,
        compiler_params=pltpu.CompilerParams(collective_id=1, has_side_effects=True, vmem_limit_bytes=65400 * 1024),
    )(x, w0, kv, q, do, g_o, g, e, resid, low, r, g_bup, g_vecs)


def normalize(values, gain, shift):
    average = jnp.mean(values, -1, keepdims=True)
    centered = values - average
    inverse = lax.rsqrt(jnp.mean(centered * centered, -1, keepdims=True) + EPSILON)
    return centered * inverse * gain + shift


def exact_gelu(values):
    return jax.nn.gelu(values, approximate=False)


def outer_sum(left, right):
    return dot(left, right, TN)


def times_transposed(left, right):
    return dot(left, right, NT)


def plain(
    tokens,
    cotangent,
    w_query,
    w_key,
    w_value,
    w_out,
    w_up,
    w_down,
    b_query,
    b_value,
    b_up,
    b_out,
    b_down,
    gain_attn,
    shift_attn,
    gain_ffn,
    shift_ffn,
):
    gathered = (
        lax.all_gather(w_query, "fsdp", axis=0, tiled=True),
        lax.all_gather(w_key, "fsdp", axis=0, tiled=True),
        lax.all_gather(w_value, "fsdp", axis=0, tiled=True),
        lax.all_gather(w_out, "fsdp", axis=1, tiled=True),
        lax.all_gather(w_up, "fsdp", axis=0, tiled=True),
        lax.all_gather(w_down, "fsdp", axis=1, tiled=True),
        lax.all_gather(b_query, "fsdp", axis=0, tiled=True),
        lax.all_gather(b_value, "fsdp", axis=0, tiled=True),
        lax.all_gather(b_up, "fsdp", axis=0, tiled=True),
        lax.all_gather(b_out, "fsdp", axis=0, tiled=True),
        lax.all_gather(b_down, "fsdp", axis=0, tiled=True),
        lax.all_gather(gain_attn, "fsdp", axis=0, tiled=True),
        lax.all_gather(shift_attn, "fsdp", axis=0, tiled=True),
        lax.all_gather(gain_ffn, "fsdp", axis=0, tiled=True),
        lax.all_gather(shift_ffn, "fsdp", axis=0, tiled=True),
    )
    (
        query_weight,
        key_weight,
        value_weight,
        out_weight,
        up_weight,
        down_weight,
        query_bias,
        value_bias,
        up_bias,
        out_bias,
        down_bias,
        attn_gain,
        attn_shift,
        ffn_gain,
        ffn_shift,
    ) = gathered
    own_rows = tokens.shape[0]
    seq_len = own_rows * lax.axis_size("tensor")
    heads = query_weight.shape[1] // HEAD
    span = min(512, seq_len)
    blocks = seq_len // span
    scale = HEAD ** (-0.5)
    full_tokens = lax.all_gather(tokens, "tensor", axis=0, tiled=True)
    query = (
        jnp.dot(full_tokens, query_weight, preferred_element_type=jnp.float32)
        + query_bias.astype(jnp.float32)
    ).astype(jnp.bfloat16)
    keys = jnp.dot(full_tokens, key_weight, preferred_element_type=jnp.float32).astype(jnp.bfloat16)
    values = (
        jnp.dot(full_tokens, value_weight, preferred_element_type=jnp.float32)
        + value_bias.astype(jnp.float32)
    ).astype(jnp.bfloat16)
    query_blocks = query.reshape(blocks, span, heads, HEAD)
    key_heads = keys.reshape(seq_len, heads, HEAD)
    value_heads = values.reshape(seq_len, heads, HEAD)

    def scores_of(piece):
        return (
            jnp.einsum("qhd,khd->hqk", piece, key_heads, preferred_element_type=jnp.float32) * scale
        )

    def forward_block(piece):
        scores = scores_of(piece)
        largest = jnp.max(scores, -1, keepdims=True)
        exponent = jnp.exp(scores - largest)
        total = jnp.sum(exponent, -1, keepdims=True)
        soft_low = (exponent / total).astype(jnp.bfloat16)
        result = jnp.einsum(
            "hqk,khd->qhd", soft_low, value_heads, preferred_element_type=jnp.float32
        )
        return (result.astype(jnp.bfloat16), largest, total)

    attended, largest_all, total_all = lax.map(forward_block, query_blocks)
    attended = attended.reshape(seq_len, heads * HEAD)
    attn_part = lax.psum_scatter(
        jnp.dot(attended, out_weight, preferred_element_type=jnp.float32).astype(jnp.bfloat16),
        "tensor",
        scatter_dimension=0,
        tiled=True,
    ).astype(jnp.float32)
    resid_attn = tokens.astype(jnp.float32) + (attn_part + out_bias.astype(jnp.float32))
    hidden, attn_norm_back = jax.vjp(
        normalize, resid_attn, attn_gain.astype(jnp.float32), attn_shift.astype(jnp.float32)
    )
    full_hidden = lax.all_gather(hidden.astype(jnp.bfloat16), "tensor", axis=0, tiled=True)
    pre_act = jnp.dot(full_hidden, up_weight, preferred_element_type=jnp.float32) + up_bias.astype(
        jnp.float32
    )
    activ, gelu_back = jax.vjp(exact_gelu, pre_act)
    activ_low = activ.astype(jnp.bfloat16)
    ffn_part = lax.psum_scatter(
        jnp.dot(activ_low, down_weight, preferred_element_type=jnp.float32).astype(jnp.bfloat16),
        "tensor",
        scatter_dimension=0,
        tiled=True,
    ).astype(jnp.float32)
    resid_ffn = hidden + (ffn_part + down_bias.astype(jnp.float32))
    output, ffn_norm_back = jax.vjp(
        normalize, resid_ffn, ffn_gain.astype(jnp.float32), ffn_shift.astype(jnp.float32)
    )
    matrices = (
        lax.all_gather(w_query, "fsdp", axis=0, tiled=True),
        lax.all_gather(w_key, "fsdp", axis=0, tiled=True),
        lax.all_gather(w_value, "fsdp", axis=0, tiled=True),
        lax.all_gather(w_out, "fsdp", axis=1, tiled=True),
        lax.all_gather(w_up, "fsdp", axis=0, tiled=True),
        lax.all_gather(w_down, "fsdp", axis=1, tiled=True),
    )
    back_query, back_key, back_value, back_out, back_up, back_down = matrices
    grad_resid_ffn, grad_gain_ffn, grad_shift_ffn = ffn_norm_back(cotangent.astype(jnp.float32))
    grad_ffn_full = lax.all_gather(
        grad_resid_ffn.astype(jnp.bfloat16), "tensor", axis=0, tiled=True
    )
    grad_down_bias = jnp.sum(grad_ffn_full, 0, dtype=jnp.float32)
    grad_down_weight = outer_sum(activ_low, grad_ffn_full)
    grad_activ = times_transposed(grad_ffn_full, back_down)
    grad_pre = gelu_back(grad_activ)[0].astype(jnp.bfloat16)
    grad_up_bias = jnp.sum(grad_pre, 0, dtype=jnp.float32)
    grad_up_weight = outer_sum(full_hidden, grad_pre)
    grad_hidden = grad_resid_ffn + lax.psum_scatter(
        times_transposed(grad_pre, back_up).astype(jnp.bfloat16),
        "tensor",
        scatter_dimension=0,
        tiled=True,
    ).astype(jnp.float32)
    grad_resid_attn, grad_gain_attn, grad_shift_attn = attn_norm_back(grad_hidden)
    grad_attn_full = lax.all_gather(
        grad_resid_attn.astype(jnp.bfloat16), "tensor", axis=0, tiled=True
    )
    grad_out_bias = jnp.sum(grad_attn_full, 0, dtype=jnp.float32)
    grad_out_weight = outer_sum(attended, grad_attn_full)
    grad_attended = times_transposed(grad_attn_full, back_out).astype(jnp.bfloat16)
    grad_blocks = grad_attended.reshape(blocks, span, heads, HEAD)

    def backward_block(carry, item):
        piece, grad_piece, largest, total = item
        soft = jnp.exp(scores_of(piece) - largest) / total
        soft_low = soft.astype(jnp.bfloat16)
        grad_soft = jnp.einsum(
            "qhd,khd->hqk", grad_piece, value_heads, preferred_element_type=jnp.float32
        )
        inner = jnp.sum(soft * grad_soft, -1, keepdims=True)
        grad_scores = (soft * (grad_soft - inner)).astype(jnp.bfloat16)
        grad_query_block = (
            jnp.einsum("hqk,khd->qhd", grad_scores, key_heads, preferred_element_type=jnp.float32)
            * scale
        )
        grad_key_sum = (
            carry[0]
            + jnp.einsum("hqk,qhd->khd", grad_scores, piece, preferred_element_type=jnp.float32)
            * scale
        )
        grad_value_sum = carry[1] + jnp.einsum(
            "hqk,qhd->khd", soft_low, grad_piece, preferred_element_type=jnp.float32
        )
        return ((grad_key_sum, grad_value_sum), grad_query_block.astype(jnp.bfloat16))

    zeros = jnp.zeros((seq_len, heads, HEAD), jnp.float32)
    (grad_key_sum, grad_value_sum), grad_query = lax.scan(
        backward_block, (zeros, zeros), (query_blocks, grad_blocks, largest_all, total_all)
    )
    grad_query = grad_query.reshape(seq_len, heads * HEAD)
    grad_keys = grad_key_sum.reshape(seq_len, heads * HEAD).astype(jnp.bfloat16)
    grad_values = grad_value_sum.reshape(seq_len, heads * HEAD).astype(jnp.bfloat16)
    grad_query_bias = jnp.sum(grad_query, 0, dtype=jnp.float32)
    grad_value_bias = jnp.sum(grad_values, 0, dtype=jnp.float32)
    grad_query_weight = outer_sum(full_tokens, grad_query)
    grad_key_weight = outer_sum(full_tokens, grad_keys)
    grad_value_weight = outer_sum(full_tokens, grad_values)
    token_terms = (
        times_transposed(grad_query, back_query)
        + times_transposed(grad_keys, back_key)
        + times_transposed(grad_values, back_value)
    )
    norm_terms = jnp.tile(
        jnp.stack([grad_gain_attn, grad_shift_attn, grad_gain_ffn, grad_shift_ffn]),
        (lax.axis_size("tensor"), 1),
    )
    token_part, norm_sums = (
        lax.psum_scatter(
            token_terms.astype(jnp.bfloat16), "tensor", scatter_dimension=0, tiled=True
        ).astype(jnp.float32),
        lax.psum_scatter(
            norm_terms.astype(jnp.bfloat16), "tensor", scatter_dimension=0, tiled=True
        ).astype(jnp.float32),
    )
    grad_tokens = grad_resid_attn + token_part
    shards = (
        lax.psum_scatter(grad_query_weight, "fsdp", scatter_dimension=0, tiled=True),
        lax.psum_scatter(grad_key_weight, "fsdp", scatter_dimension=0, tiled=True),
        lax.psum_scatter(grad_value_weight, "fsdp", scatter_dimension=0, tiled=True),
        lax.psum_scatter(grad_out_weight, "fsdp", scatter_dimension=1, tiled=True),
        lax.psum_scatter(grad_up_weight, "fsdp", scatter_dimension=0, tiled=True),
        lax.psum_scatter(grad_down_weight, "fsdp", scatter_dimension=1, tiled=True),
        lax.psum_scatter(grad_query_bias, "fsdp", scatter_dimension=0, tiled=True),
        lax.psum_scatter(grad_value_bias, "fsdp", scatter_dimension=0, tiled=True),
        lax.psum_scatter(grad_up_bias, "fsdp", scatter_dimension=0, tiled=True),
        lax.psum_scatter(grad_out_bias, "fsdp", scatter_dimension=0, tiled=True),
        lax.psum_scatter(grad_down_bias, "fsdp", scatter_dimension=0, tiled=True),
        lax.psum_scatter(norm_sums[0], "fsdp", scatter_dimension=0, tiled=True),
        lax.psum_scatter(norm_sums[1], "fsdp", scatter_dimension=0, tiled=True),
        lax.psum_scatter(norm_sums[2], "fsdp", scatter_dimension=0, tiled=True),
        lax.psum_scatter(norm_sums[3], "fsdp", scatter_dimension=0, tiled=True),
    )
    return (
        output,
        grad_tokens,
        shards[0],
        shards[1],
        shards[2],
        shards[3],
        shards[4],
        shards[5],
        shards[6],
        shards[7],
        shards[8],
        shards[9],
        shards[10],
        shards[11],
        shards[12],
        shards[13],
        shards[14],
    )


def fits(tokens, w_query, w_up):
    fsdp, tensor = lax.axis_size("fsdp"), lax.axis_size("tensor")
    shard, columns = w_query.shape
    return (tensor in (2, 4) and fsdp >= 4 and fsdp & (fsdp - 1) == 0 and shard % 16 == 0 and columns >= 3 * HEAD and columns % HEAD == 0
            and w_up.shape[1] == 4 * columns and tokens.shape[0] % 128 == 0)


def pairs(first, second):
    rows, columns = first.shape
    both = jnp.stack([first.reshape(rows, -1, HEAD), second.reshape(rows, -1, HEAD)], 2)
    return both.reshape(rows, 2 * columns)


def layer(tokens, cotangent, w_query, w_key, w_value, w_out, w_up, w_down, b_query, b_value, b_up, b_out, b_down,
          gain_attn, shift_attn, gain_ffn, shift_ffn):
    if not fits(tokens, w_query, w_up):
        return plain(tokens, cotangent, w_query, w_key, w_value, w_out, w_up, w_down, b_query, b_value, b_up, b_out, b_down,
                     gain_attn, shift_attn, gain_ffn, shift_ffn)
    fsdp, tensor = lax.axis_size("fsdp"), lax.axis_size("tensor")
    i, j = lax.axis_index("fsdp"), lax.axis_index("tensor")
    rows, model = tokens.shape
    shard, columns = w_query.shape
    width = 2 * columns
    down = w_down.T
    pack = jnp.stack([pairs(w_key, w_value), pairs(w_query, w_out.T), w_up[:, :width], down[:, :width], w_up[:, width:], down[:, width:]])

    def placed(vector):
        mine = jnp.tile(vector.astype(F32), fsdp).reshape(fsdp, -1)
        mine = jnp.where(lax.broadcasted_iota(jnp.int32, mine.shape, 0) == i, mine, 0.0)
        return mine.reshape(1, -1)

    def spread(vector, second):
        vector = placed(vector)
        zero = jnp.zeros_like(vector)
        return pairs(zero, vector) if second else pairs(vector, zero)

    small = jnp.concatenate([jnp.concatenate([spread(b_value, True), spread(b_query, False)], 1), placed(b_up),
                             *map(placed, (b_out, b_down, gain_attn, shift_attn, gain_ffn, shift_ffn))])
    w0, w1, x, x_own, cot, kv, q, att, exps, inv, smalls = first_part(fsdp, tensor, pack, small, tokens, cotangent)
    out, low, resid, r, do, g_o, g, g_bup, g_vecs = middle_part(x_own, cot, att, w0, w1, smalls, inv)
    shards, grad_tokens, tiny, swapped = last_part(fsdp, tensor, x, w0, kv, q, do, g_o, g, exps, resid, low, r, g_bup, g_vecs)
    output = jnp.where(i % 2 == j // (tensor // 2), out, swapped.astype(F32))

    def apart(shard_pair):
        both = shard_pair.reshape(shard, -1, 2, HEAD)
        return both[:, :, 0].reshape(shard, columns), both[:, :, 1].reshape(shard, columns)

    g_key, g_value = apart(shards[0])
    g_query, g_out = apart(shards[1])
    g_up = jnp.concatenate([shards[2], shards[4]], 1)
    g_down = jnp.concatenate([shards[3], shards[5]], 1).T
    mine = lambda vector, n: lax.dynamic_slice_in_dim(vector, i * n, n)
    pick = lambda first: lax.dynamic_index_in_dim(tiny, first + j, 0, False)
    both = pick(8 + tensor).reshape(2, -1, 2, HEAD)
    g_bq, g_bv = both[1, :, 0].reshape(-1), both[0, :, 1].reshape(-1)
    vectors = [mine(tiny[k], shard) for k in range(6)]
    return (output, grad_tokens, g_query, g_key, g_value, g_out.T, g_up, g_down,
            mine(g_bq, columns // fsdp), mine(g_bv, columns // fsdp), mine(pick(8), 2 * width // fsdp), *vectors)


def solution(mesh):
    return jax.shard_map(
        layer,
        mesh=mesh,
        in_specs=(
            P(("fsdp", "tensor"), None),
            P(("fsdp", "tensor"), None),
            P("fsdp", "tensor"),
            P("fsdp", "tensor"),
            P("fsdp", "tensor"),
            P("tensor", "fsdp"),
            P("fsdp", "tensor"),
            P("tensor", "fsdp"),
            P(("tensor", "fsdp")),
            P(("tensor", "fsdp")),
            P(("tensor", "fsdp")),
            P("fsdp"),
            P("fsdp"),
            P("fsdp"),
            P("fsdp"),
            P("fsdp"),
            P("fsdp"),
        ),
        out_specs=(
            P(("fsdp", "tensor"), None),
            P(("fsdp", "tensor"), None),
            P("fsdp", "tensor"),
            P("fsdp", "tensor"),
            P("fsdp", "tensor"),
            P("tensor", "fsdp"),
            P("fsdp", "tensor"),
            P("tensor", "fsdp"),
            P(("tensor", "fsdp")),
            P(("tensor", "fsdp")),
            P(("tensor", "fsdp")),
            P("fsdp"),
            P("fsdp"),
            P("fsdp"),
            P("fsdp"),
            P("fsdp"),
            P("fsdp"),
        ),
        check_vma=False,
    )
```

```python
import functools

import jax
import jax.numpy as jnp
import numpy as np
from jax import lax
from jax.experimental import pallas as pl
from jax.experimental.pallas import tpu as pltpu
from jax.sharding import PartitionSpec as P

F32, BF16 = jnp.float32, jnp.bfloat16
HEAD = 64
EPSILON = 1e-12
VMEM_LIMIT = 64000 * 1024


def dot(left, right, contract):
    return lax.dot_general(left, right, ((contract[:1], contract[1:]), ((), ())), preferred_element_type=F32)

NN, NT, TN = (1, 0), (1, 1), (0, 0)


def lanes_from(shape, low):
    return lax.broadcasted_iota(jnp.int32, shape, len(shape) - 1) % (2 * HEAD) >= HEAD if not low else \
        lax.broadcasted_iota(jnp.int32, shape, len(shape) - 1) % (2 * HEAD) < HEAD


def project_keys(x, w, bias):
    return (dot(x, w, NN) + bias).astype(BF16)


def project_query(x, w, bias):
    out = dot(x, w, NN) + bias
    return jnp.where(lanes_from(out.shape, True), out.astype(BF16) * BF16(HEAD ** -0.5), BF16(0))


def norm_forward(z):
    mean = jnp.mean(z, -1, keepdims=True)
    centered = z - mean
    inv = lax.rsqrt(jnp.mean(centered * centered, -1, keepdims=True) + EPSILON)
    return centered * inv, inv


def norm_backward(n, inv, dn):
    return inv * (dn - jnp.mean(dn, -1, keepdims=True) - n * jnp.mean(dn * n, -1, keepdims=True))


def colsum(x):
    return jnp.sum(x.astype(F32), axis=0, keepdims=True)


MESH = pl.DeviceIdType.MESH
ANY = pl.BlockSpec(memory_space=pl.ANY)
VM = pl.BlockSpec(memory_space=pltpu.VMEM)


def flip(index, bit):
    return index + bit - 2 * bit * lax.rem(index // bit, 2)


def flips(index, mask):
    bit = 1
    while bit <= mask:
        if mask & bit:
            index = flip(index, bit)
        bit *= 2
    return index


def span(bits):
    masks = [0]
    for bit in bits:
        masks += [m | bit for m in masks]
    return masks


def orders(fsdp):
    bits = [1 << k for k in range(fsdp.bit_length() - 1)]
    return bits[1:] + bits[:1], bits[:0:-1] + bits[:1]


class Place:
    def __init__(self, fsdp, tensor):
        self.fsdp, self.tensor = fsdp, tensor
        self.i, self.j = lax.axis_index("fsdp"), lax.axis_index("tensor")
        self.half = tensor // 2
        self.c = lax.rem(self.i, 2)
        self.h = self.j // self.half
        self.on = self.c == self.h
        self.off = self.c != self.h
        self.twin = flip(self.i, 1)
        self.swap = lax.rem(self.j + self.half, tensor)
        self.block = jnp.where(self.on, self.j, self.swap)
        self.edge = self.half - 1 + self.c
        self.end = self.c * (tensor - 1)
        self.mate = self.h * tensor + 1 - self.j
        self.is_edge = self.j == self.edge
        self.is_end = self.j == self.end

    def other(self, k):
        return (1 - self.c) * (self.half + k) + self.c * (self.half - 1 - k)

    def near(self, n):
        low = jnp.where(self.h == 0, self.j, self.tensor - 1 - self.j)
        if isinstance(n, int):
            place = low if n == 0 else 1 - low if n == 1 else n
        else:
            place = jnp.where(n == 0, low, jnp.where(n == 1, 1 - low, n))
        return jnp.where(self.h == 0, place, self.tensor - 1 - place)

    def barrier(self):
        self.greet()
        self.met()

    def met(self):
        pl.semaphore_wait(pltpu.get_barrier_semaphore(), self.tensor + self.fsdp.bit_length() - 1)

    def greet(self):
        sem = pltpu.get_barrier_semaphore()
        others = [(self.i, lax.rem(self.j + k, self.tensor)) for k in range(1, self.tensor)]
        bit = 1
        while bit < self.fsdp:
            others.append((flip(self.i, bit), self.j))
            bit *= 2
        others.append((self.twin, self.swap))
        for i, j in others:
            pl.semaphore_signal(sem, inc=1, device_id=(i, j), device_id_type=MESH)


class Sends:
    def __init__(self, place, send, recv):
        self.place, self.send, self.recv, self.n, self.started = place, send, recv, 0, []

    def slots(self, n):
        self.n += n
        return self.n - n

    def slot(self):
        return self.slots(1)

    def copy(self, src, dst, slot, i, j, back=None):
        return pltpu.make_async_remote_copy(src_ref=src, dst_ref=dst, send_sem=self.send.at[slot if back is None else back],
                                            recv_sem=self.recv.at[slot], device_id=(i, j), device_id_type=MESH)

    def start(self, src, dst, slot, i, j, when=None, back=None, note=True):
        copy = self.copy(src, dst, slot, i, j, back)
        copy.start() if when is None else pl.when(when)(copy.start)
        if note:
            self.started.append((copy, when))

    def arrive(self, dst, slot, when=None):
        copy = self.copy(dst, dst, slot, self.place.i, self.place.j)
        copy.wait_recv() if when is None else pl.when(when)(copy.wait_recv)

    def left(self, src, slot, when=None):
        copy = self.copy(src, src, slot, self.place.i, self.place.j)
        copy.wait_send() if when is None else pl.when(when)(copy.wait_send)

    def finish(self):
        for copy, when in self.started:
            copy.wait_send() if when is None else pl.when(when)(copy.wait_send)
        self.started = []


def transposed(value):
    return value.astype(F32).T.astype(value.dtype)


def spread(lanes, n, place, first, width):
    at = lanes(lax.broadcasted_iota(jnp.int32, (n, width), 1))
    return jnp.where(at == lax.broadcasted_iota(jnp.int32, (n, width), 0) + place * n, 1.0, 0.0)


def head_lanes(second):
    def lanes(lane):
        inside = lane % 128
        if second:
            return jnp.where(inside >= HEAD, lane // 128 * HEAD + inside - HEAD, -1)
        return jnp.where(inside < HEAD, lane // 128 * HEAD + inside, -1)
    return lanes


def pack_own(p, w_query, w_key, w_value, w_out, w_up, w_down, vectors, pack, small):
    shard, columns = w_query.shape
    width = 2 * columns
    out = transposed(w_out[...])
    for k, (first, second) in enumerate(((w_key[...], w_value[...]), (w_query[...], out))):
        for h in range(columns // HEAD):
            cols = slice(h * HEAD, h * HEAD + HEAD)
            pack[k, :, 2 * h * HEAD:2 * h * HEAD + 2 * HEAD] = jnp.concatenate([first[:, cols], second[:, cols]], 1)
    for k in range(2):
        cols = slice(k * width, k * width + width)
        pack[2 + 2 * k] = w_up[:, cols]
        pack[3 + 2 * k] = w_down[:, cols]
    few, many = columns // p.fsdp, 2 * width // p.fsdp
    take = lambda at, n: vectors[:, at:at + n].astype(BF16)
    put = lambda value, ones: dot(value, ones.astype(BF16), NN)
    small[0:1, width:] = put(take(0, few), spread(head_lanes(False), few, p.i, 0, width))
    small[0:1, :width] = put(take(few, few), spread(head_lanes(True), few, p.i, 0, width))
    small[1:2] = put(take(2 * few, many), spread(lambda lane: lane, many, p.i, 0, 2 * width))
    ones = spread(lambda lane: lane, shard, p.i, 0, shard * p.fsdp)
    for k in range(6):
        small[2 + k:3 + k] = put(take(2 * few + many + k * shard, shard), ones)


class Stream:
    def __init__(self, sends, array, lead, shard, order, own):
        self.s, self.p, self.a, self.lead, self.shard, self.order, self.own = sends, sends.place, array, lead, shard, order, own
        n = self.p.tensor
        self.z, self.back = sends.slots(n), sends.slots(1)
        self.hops = [{m: sends.slots(n) for m in span(order[:k])} for k in range(len(order))]

    def block(self, t, mask):
        rows = pl.ds(pl.multiple_of(flips(self.p.i, mask) * self.shard, self.shard), self.shard)
        return self.a.at[(*self.lead, t, rows)]

    def first_line(self):
        s, p = self.s, self.p
        there = self.block(p.j, 0)
        s.start(self.own, there, self.z + p.j, p.i, p.j + 1, p.j + 1 < p.tensor, note=False)
        s.start(self.own, there, self.z + p.j, p.i, p.j - 1, p.j > 0, self.back, note=False)

    def first_fan(self):
        self.fan(0, 0, self.p.j, self.own)

    def fan(self, mask, k, t, src=None):
        for n in range(k, len(self.order)):
            there = self.block(t, mask)
            self.s.start(there if src is None else src, there, self.hops[n][mask] + t, flip(self.p.i, self.order[n]), self.p.j, note=False)

    def line(self, n):
        s, p = self.s, self.p
        t = p.near(n)
        there = self.block(t, 0)
        s.arrive(there, self.z + t)
        ahead = p.j + jnp.where(t < p.j, 1, -1)
        s.start(there, there, self.z + t, p.i, ahead, (ahead >= 0) & (ahead < p.tensor), note=False)
        self.fan(0, 0, t)

    def finish(self):
        s, p = self.s, self.p
        here = self.block(p.j, 0)
        s.left(here, self.z + p.j, p.j + 1 < p.tensor)
        s.left(here, self.back, p.j > 0)
        for n in range(p.tensor):
            t = p.near(n)
            if n > 0:
                ahead = p.j + jnp.where(t < p.j, 1, -1)
                s.left(here, self.z + t, (ahead >= 0) & (ahead < p.tensor))
            for hops in self.hops:
                for slot in hops.values():
                    s.left(here, slot + t)

    def hop(self, k, n):
        t = self.p.near(n)
        for m in self.hops[k]:
            mask = m | self.order[k]
            self.s.arrive(self.block(t, mask), self.hops[k][m] + t)
            self.fan(mask, k + 1, t)


def attend_group(heads, g, x, own_rows, w_kv, w_qo, smalls, kv, q, att, inv, s_ref, exps, before, after):
    width = heads * 128
    kv[g] = project_keys(x[...], w_kv[g], smalls[g, 0:1, :width])
    q[g] = project_query(x[own_rows, :], w_qo[g], smalls[g, 0:1, width:])
    for h in range(heads):
        cols = slice(h * 128, h * 128 + 128)
        keys = kv[g, :, cols]
        s_ref[...] = dot(keys, q[g, :, cols], NT)
        top = jnp.max(s_ref[...], axis=0, keepdims=True)
        e = jnp.exp(s_ref[...] - top)
        scale = 1.0 / jnp.sum(e, axis=0, keepdims=True)
        before(h)
        exps[h] = e.astype(BF16)
        out = dot(keys, exps[h], TN) * scale
        out = jnp.where(lax.broadcasted_iota(jnp.int32, out.shape, 0) >= HEAD, out, 0.0)
        att[g, :, cols] = out.T.astype(BF16)
        inv[g, h:h + 1] = scale
        after(h)


def first_kernel(fsdp, tensor, w_query, w_key, w_value, w_out, w_up, w_down, vectors, tok, cot, w0_out, w1, x_out, own_out, cot_out, kv_out, q_out, att_out, exp_out,
                 inv, smalls, pack, small, w0, sm, x, kv, q, att, s_ref, exps, send, recv, local):
    p = Place(fsdp, tensor)
    s = Sends(p, send, recv)
    p.greet()
    pack_own(p, w_query, w_key, w_value, w_out, w_up, w_down, vectors, pack, small)
    rows, model = tok.shape
    shard = pack.shape[1]
    heads = exps.shape[0]
    first, second = orders(fsdp)
    kvw = Stream(s, w0, (0,), shard, first, pack.at[0])
    qow = Stream(s, w0, (1,), shard, second, pack.at[1])
    tiny = Stream(s, sm, (), small.shape[0], first, small)
    upper = Stream(s, w1, (pl.ds(0, 2),), shard, first, pack.at[pl.ds(2, 2)])
    lower = Stream(s, w1, (pl.ds(2, 2),), shard, second, pack.at[pl.ds(4, 2)])
    now, later = (kvw, qow, tiny), (upper, lower)
    pieces = 4 if rows % 64 == 0 else 1
    part = rows // pieces
    xin, xtwin, cslot = s.slots(tensor * pieces), s.slots(tensor * pieces), s.slots(1)
    x_at = lambda t: x.at[pl.ds(pl.multiple_of(t * rows, rows), rows)]

    def piece(t, u):
        return x.at[pl.ds(pl.multiple_of(t * rows + u * part, part), part)]

    def send_rows(t, u, i, j, when, twin=False, src=None):
        slot = t * pieces + u
        there = piece(t, u)
        s.start(there if src is None else src.at[pl.ds(u * part, part)], there, xin + slot, i, j, when, xtwin + slot if twin else None)

    def pass_rows(u, n, when, forward):
        t = p.near(n)
        s.arrive(piece(t, u), xin + t * pieces + u, when)
        if forward:
            send_rows(t, u, p.i, p.end, when)
        send_rows(t, u, p.twin, p.j, when, True)

    def edge_rows(u):
        for n in [*range(2, tensor), 1]:
            pass_rows(u, n, p.on & p.is_edge, p.half > 1 and n > 1)

    def end_rows(u):
        for n in range(1, tensor):
            pass_rows(u, n, p.on & jnp.logical_not(p.is_edge), False)
    locals_ = []

    def keep(src, dst, when=None):
        copy = pltpu.make_async_copy(src, dst, local.at[len(locals_)])
        copy.start() if when is None else pl.when(when)(copy.start)
        locals_.append((copy, when))
        return len(locals_) - 1

    def kept(k):
        copy, when = locals_[k]
        copy.wait() if when is None else pl.when(when)(copy.wait)
        locals_[k] = None

    mine = pl.ds(pl.multiple_of(p.i * shard, shard), shard)
    own = [keep(pack.at[k], w0.at[k, p.j, mine]) for k in range(2)]
    own += [keep(pack.at[2 + k], w1.at[k, p.j, mine]) for k in range(4)]
    own += [keep(small, sm.at[p.j, pl.ds(pl.multiple_of(p.i * small.shape[0], small.shape[0]), small.shape[0])])]
    own += [keep(tok, x_at(p.j), p.on), keep(cot, cot_out, p.on)]
    p.met()
    for g in now:
        g.first_line()
    for g in now:
        g.first_fan()
    for u in range(pieces):
        send_rows(p.j, u, p.i, p.edge, p.off, src=tok)
        if p.half > 1:
            send_rows(p.j, u, p.i, p.mate, p.on, src=tok)
        send_rows(p.j, u, p.twin, p.j, p.on, True, tok)
    for g in later:
        g.first_fan()
    stages = len(first)
    for step in range(1, tensor + stages - 1):
        if step < tensor:
            for g in now:
                g.line(step)
        for k in range(stages - 1):
            if 0 <= step - 1 - k < tensor:
                for g in now:
                    g.hop(k, step - 1 - k)
        if step - 1 < pieces:
            edge_rows(step - 1)
    for u in range(tensor + stages - 2, pieces):
        edge_rows(u)
    for u in range(pieces):
        end_rows(u)
    for g in later:
        g.first_line()
    for k in range(stages - 1):
        for g in later:
            g.hop(k, 0)
    s.start(cot, cot_out, cslot, p.twin, p.swap, p.off)
    for n in range(tensor):
        for g in now:
            g.hop(stages - 1, n)
    for t in range(tensor):
        for u in range(pieces):
            s.arrive(piece(t, u), xin + t * pieces + u, p.off)
    for k in own[:8]:
        kept(k)
    for t in range(tensor):
        total = sm[t, :small.shape[0], :]
        for i in range(1, fsdp):
            total += sm[t, i * small.shape[0]:(i + 1) * small.shape[0], :]
        smalls[t] = total
    keep(x_at(p.block), own_out)
    for t in range(tensor):
        keep(x_at(t), x_out.at[pl.ds(t * rows, rows)])
    for k in range(2):
        keep(w0.at[k], w0_out.at[k])
    fixed = len(locals_)
    sem = lambda k: local.at[fixed + k]

    def group(g, carry):
        def exp_copy(h, g):
            return pltpu.make_async_copy(exps.at[h], exp_out.at[g, h], sem(h))

        def before(h):
            pl.when(g > 0)(lambda: exp_copy(h, g - 1).wait())

        def after(h):
            exp_copy(h, g).start()
            point = {0: 0, heads // 2: 1, heads - 1: 2}.get(h)
            if point == 0:
                @pl.when(g >= 2)
                def _():
                    for st in later:
                        for k in range(1, stages - 1):
                            st.hop(k, g - 1)
            if point == 1:
                @pl.when(g >= 1)
                def _():
                    for st in later:
                        st.hop(0, g)
            if point == 2:
                @pl.when(g < tensor - 1)
                def _():
                    for st in later:
                        st.line(g + 1)

        attend_group(heads, g, x, pl.ds(pl.multiple_of(p.block * rows, rows), rows), w0.at[0], w0.at[1], smalls, kv, q, att, inv,
                     s_ref, exps, before, after)
        for k, (src, dst) in enumerate(((kv, kv_out), (q, q_out), (att, att_out))):
            pltpu.make_async_copy(src.at[g], dst.at[g], sem(heads + k * tensor + g)).start()
        return carry

    lax.fori_loop(0, tensor, group, 0)
    for k in range(1, stages - 1):
        for st in later:
            st.hop(k, tensor - 1)
    for n in range(tensor):
        for st in later:
            st.hop(stages - 1, n)
    for h in range(heads):
        pltpu.make_async_copy(exps.at[h], exp_out.at[0, h], sem(h)).wait()
    for k, (src, dst) in enumerate(((kv, kv_out), (q, q_out), (att, att_out))):
        for g in range(tensor):
            pltpu.make_async_copy(src.at[g], dst.at[g], sem(heads + k * tensor + g)).wait()
    s.arrive(cot_out, cslot, p.off)
    for k in range(len(locals_)):
        if locals_[k] is not None:
            kept(k)
    s.finish()
    for st in now + later:
        st.finish()


def first_part(fsdp, tensor, w_query, w_key, w_value, w_out, w_up, w_down, vectors, tok, cot):
    shard, width = w_query.shape[0], 2 * w_query.shape[1]
    rows, model = tok.shape
    heads, keys = width // 128, tensor * rows
    slots = 5 * (tensor + 1 + (fsdp - 1) * tensor) + 8 * tensor + 1
    return pl.pallas_call(
        functools.partial(first_kernel, fsdp, tensor),
        in_specs=[VM] * 9, out_specs=[ANY] * 9 + [VM] * 2,
        out_shape=[jax.ShapeDtypeStruct(s, d) for s, d in [
            ((2, tensor, model, width), BF16), ((4, tensor, model, width), BF16), ((keys, model), BF16), ((rows, model), BF16),
            ((rows, model), BF16), ((tensor, keys, width), BF16), ((tensor, rows, width), BF16), ((tensor, rows, width), BF16),
            ((tensor, heads, keys, rows), BF16), ((tensor, 8, rows), F32), ((tensor, 8, model), F32)]],
        scratch_shapes=[pltpu.VMEM(s, d) for s, d in [
            ((6, shard, width), BF16), ((8, model), F32),
            ((2, tensor, model, width), BF16), ((tensor, fsdp * 8, model), F32), ((keys, model), BF16),
            ((tensor, keys, width), BF16), ((tensor, rows, width), BF16), ((tensor, rows, width), BF16), ((keys, rows), F32),
            ((heads, keys, rows), BF16)]] + [pltpu.SemaphoreType.DMA((slots,)), pltpu.SemaphoreType.DMA((slots,)),
                                             pltpu.SemaphoreType.DMA((16 + 5 * tensor + heads,))],
        compiler_params=pltpu.CompilerParams(collective_id=0, has_side_effects=True, vmem_limit_bytes=VMEM_LIMIT),
    )(w_query, w_key, w_value, w_out, w_up, w_down, vectors, tok, cot)


class Fold:
    def __init__(self, sends, give, keep, lead, halves, inbox, order, out):
        self.s, self.p, self.give, self.keep, self.lead = sends, sends.place, give, keep, lead
        self.halves, self.inbox, self.order, self.out = halves, inbox, order[::-1], out
        n = self.p.tensor
        self.masks = [span(self.order[k + 1:]) for k in range(len(order))]
        self.slot = [[sends.slots(n) for _ in masks] for masks in self.masks]
        self.z = sends.slots(2 * n)

    def half(self, k, mask, t):
        return self.halves[k].at[(self.lead, self.masks[k].index(mask), t)]

    def first(self, n):
        t, bit = self.p.near(n), self.order[0]
        for k, m in enumerate(self.masks[0]):
            self.s.start(self.give(t, m | bit), self.half(0, m, t), self.slot[0][k] + t, flip(self.p.i, bit), self.p.j, note=False)

    def add(self, k, n):
        t = self.p.near(n)
        for at, m in enumerate(self.masks[k]):
            here = self.half(k, m, t)
            self.s.arrive(here, self.slot[k][at] + t)
            mine = self.keep(t, at) if k == 0 else self.half(k - 1, m, t)
            here[...] = (here[...].astype(F32) + mine[...].astype(F32)).astype(BF16)
        if k + 1 < len(self.order):
            bit = self.order[k + 1]
            for at, m in enumerate(self.masks[k + 1]):
                self.s.start(self.half(k, m | bit, t), self.half(k + 1, m, t), self.slot[k + 1][at] + t,
                             flip(self.p.i, bit), self.p.j, note=False)

    def total(self, t):
        return self.half(len(self.order) - 1, 0, t)

    def way(self, n):
        t = self.p.near(n)
        right = t > self.p.j
        there = self.p.j + jnp.where(right, 1, -1)
        before = self.p.j - jnp.where(right, 1, -1)
        side = jnp.where(right, 0, 1)
        has = (before >= 0) & (before < self.p.tensor)
        return t, there, has, self.inbox.at[(self.lead, side, t)], self.z + side * self.p.tensor + t

    def line_first(self, n):
        t, there, has, box, slot = self.way(n)
        self.s.start(self.total(t), box, slot, self.p.i, there, jnp.logical_not(has), note=False)

    def line_next(self, n):
        t, there, has, box, slot = self.way(n)
        total = self.total(t)

        @pl.when(has)
        def _():
            self.s.arrive(box, slot)
            box[...] = (box[...].astype(F32) + total[...].astype(F32)).astype(BF16)
            self.s.start(box, box, slot, self.p.i, there, note=False)

    def result(self):
        p = self.p
        self.out[...] = self.total(p.j)[...].astype(F32)
        for side, there in ((0, p.j > 0), (1, p.j < p.tensor - 1)):
            box = self.inbox.at[(self.lead, side, p.j)]

            @pl.when(there)
            def _(box=box, side=side):
                self.s.arrive(box, self.z + side * p.tensor + p.j)
                self.out[...] += box[...].astype(F32)

    def finish(self):
        here = self.half(0, self.masks[0][0], 0)
        for n in range(self.p.tensor):
            t = self.p.near(n)
            for slots in self.slot:
                for slot in slots:
                    self.s.left(here, slot + t)
            if n > 0:
                self.s.left(here, self.way(n)[4])

class Loads:
    def __init__(self, sems):
        self.sems, self.n = sems, 0

    def slots(self, n):
        self.n += n
        return self.n - n

    def load(self, src, dst):
        copy = pltpu.make_async_copy(src, dst, self.sems.at[self.slots(1)])
        copy.start()
        return copy

    def series(self, src, dst, n):
        first = self.slots(n)
        for k in range(n):
            pltpu.make_async_copy(src.at[k], dst.at[k], self.sems.at[first + k]).start()
        return lambda k: pltpu.make_async_copy(src.at[k], dst.at[k], self.sems.at[first + k]).wait()


def middle_kernel(groups, x_hbm, cot_hbm, att_hbm, w0_hbm, w1_hbm, smalls, inv,
                  out_ref, out_low, resid_ref, r_ref, datt_hbm, g_o_hbm, g_hbm, g_bup, g_vecs,
                  x_own, cot, att, w_qo, w1, datt, g_o, grads, act, slope, hid, n1_ref, acc, low, hl, sems):
    ld = Loads(sems)
    width = w_qo.shape[2]
    get_x = ld.load(x_hbm, x_own)
    get_att = ld.series(att_hbm, att, groups)
    get_qo = ld.series(w0_hbm.at[1], w_qo, groups)
    gets = [ld.series(w1_hbm.at[k], w1.at[k], groups) for k in range(4)]
    get_cot = ld.load(cot_hbm, cot)
    outs = [(grads.at[k], g_hbm.at[k], ld.slots(groups)) for k in range(4)]
    outs += [(datt, datt_hbm, ld.slots(groups)), (g_o, g_o_hbm, ld.slots(groups))]

    def put(k, g):
        src, dst, first = outs[k]
        return pltpu.make_async_copy(src.at[g], dst.at[g], sems.at[first + g])

    vec = lambda k: smalls[0, 2 + k:3 + k, :]
    get_x.wait()
    acc[...] = x_own[...].astype(F32) + vec(0)

    def branch(g, c):
        get_att(g)
        get_qo(g)
        acc[...] += dot(att[g], w_qo[g], NT)
        return c

    lax.fori_loop(0, groups, branch, 0)
    n1, inv1 = norm_forward(acc[...])
    n1_ref[...] = n1
    hidden = n1 * vec(2) + vec(3)
    hid[...] = hidden
    hl[...] = hidden.astype(BF16)
    acc[...] = hidden + vec(1)

    def forward(g, c):
        for k in range(2):
            gets[2 * k](g)
            gets[2 * k + 1](g)
            pre = dot(hl[...], w1[2 * k, g], NN) + smalls[g, 1:2, k * width:(k + 1) * width]
            phi = 0.5 + 0.5 * lax.erf(pre * np.float32(0.5 ** 0.5))
            slope[g, k] = phi + pre * (jnp.exp(-0.5 * pre * pre) * np.float32((2 * np.pi) ** -0.5))
            act[g, k] = (pre * phi).astype(BF16)
            acc[...] += dot(act[g, k], w1[2 * k + 1, g], NT)
        return c

    lax.fori_loop(0, groups, forward, 0)
    n2, inv2 = norm_forward(acc[...])
    out = n2 * vec(4) + vec(5)
    out_ref[...] = out
    out_low[...] = out.astype(BF16)
    get_cot.wait()
    cott = cot[...].astype(F32)
    g_vecs[4:5] = colsum(cott * n2)
    g_vecs[5:6] = colsum(cott)
    resid = norm_backward(n2, inv2, cott * vec(4))
    acc[...] = resid
    low[...] = resid.astype(BF16)
    g_vecs[1:2] = colsum(low[...])

    def back(g, c):
        for k in range(2):
            grads[2 * k + 1, g] = dot(low[...], act[g, k], TN).astype(BF16)
            put(2 * k + 1, g).start()
            gp = (dot(low[...], w1[2 * k + 1, g], NN) * slope[g, k]).astype(BF16)
            act[g, k] = gp
            g_bup[g, :, k * width:(k + 1) * width] = colsum(gp)
            grads[2 * k, g] = dot(hl[...], gp, TN).astype(BF16)
            put(2 * k, g).start()
            acc[...] += dot(act[g, k], w1[2 * k, g], NT)
        return c

    lax.fori_loop(0, groups, back, 0)
    gh = acc[...]
    g_vecs[2:3] = colsum(gh * n1_ref[...])
    g_vecs[3:4] = colsum(gh)
    ga = norm_backward(n1_ref[...], inv1, gh * vec(2))
    resid_ref[...] = ga
    low[...] = ga.astype(BF16)
    g_vecs[0:1] = colsum(low[...])
    g_vecs[6:8] = jnp.zeros_like(g_vecs[6:8])

    def last(g, c):
        da = dot(low[...], w_qo[g], NN)
        da = jnp.where(lanes_from(da.shape, False), da, 0.0).T.astype(BF16).astype(F32)
        prod = da * att[g].T.astype(F32)
        for h in range(width // 128):
            cols = slice(h * 128, h * 128 + 128)
            scale = inv[g, h:h + 1]
            r_ref[g, h:h + 1] = jnp.sum(prod[cols], axis=0, keepdims=True) * scale
            datt[g, :, cols] = (da[cols] * scale).T.astype(BF16)
        put(4, g).start()
        g_o[g] = dot(low[...], att[g], TN).astype(BF16)
        put(5, g).start()
        return c

    lax.fori_loop(0, groups, last, 0)
    for k in range(6):
        for g in range(groups):
            put(k, g).wait()


def middle_part(x_own, cot, att, w0, w1, smalls, inv):
    _, groups, model, width = w0.shape
    rows = x_own.shape[0]
    wide, deep = ((groups, rows, width), BF16), ((groups, model, width), BF16)
    flat, low = ((rows, model), F32), ((rows, model), BF16)
    return pl.pallas_call(
        functools.partial(middle_kernel, groups),
        in_specs=[ANY] * 5 + [VM] * 2, out_specs=[VM] * 4 + [ANY, ANY, ANY, VM, VM],
        out_shape=[jax.ShapeDtypeStruct(s, d) for s, d in [
            flat, low, flat, ((groups, 8, rows), F32), wide, deep, ((4, groups, model, width), BF16), ((groups, 1, 2 * width), F32), ((8, model), F32)]],
        scratch_shapes=[pltpu.VMEM(s, d) for s, d in [
            low, low, wide, deep, ((4, groups, model, width), BF16), wide, deep, ((4, groups, model, width), BF16),
            ((groups, 2, rows, width), BF16), ((groups, 2, rows, width), F32), flat, flat, flat, low, low]]
        + [pltpu.SemaphoreType.DMA((12 * groups + 2,))],
        compiler_params=pltpu.CompilerParams(vmem_limit_bytes=VMEM_LIMIT),
    )(x_own, cot, att, w0, w1, smalls, inv)


def last_kernel(fsdp, tensor, x_hbm, w0_hbm, kv_hbm, q_hbm, do_hbm, g_o_hbm, g_hbm, e_hbm, resid_hbm, low_hbm, r, g_bup, g_vecs,
                shards, dx, tiny, swapped, *scratch):
    bits = fsdp.bit_length() - 1
    halves, scratch = scratch[:bits], scratch[bits:]
    (inbox, own_g, x, w0, kv, q, do, dqt, wacc, exps, gw, dkv, dxb, own, twin_in, mate_in, fin_in, tiny_in, send, recv, local) = scratch
    p = Place(fsdp, tensor)
    s, ld = Sends(p, send, recv), Loads(local)
    _, heads, rows, _ = exps.shape
    model, width = gw.shape[2:]
    shard = model // fsdp
    first, second = orders(fsdp)
    block_rows = lambda mask: pl.ds(pl.multiple_of(flips(p.i, mask) * shard, shard), shard)
    pair = lambda k: pl.ds(2 * k, 2)
    stay = [m for m in span(first[::-1][1:])]
    folds = []
    for k, order in enumerate((first, second)):
        masks = span(order[::-1][1:])
        folds.append(Fold(s, lambda t, m, k=k: g_hbm.at[pair(k), t, block_rows(m)],
                          lambda t, at, k=k, masks=masks: own_g.at[pair(k), t, stay.index(masks[at])],
                          pair(k + 1), halves, inbox, order, shards.at[pair(k + 1)]))
    tails = []
    for k, order in enumerate((first, second)):
        masks = span(order[::-1][1:])
        tails.append(Fold(s, lambda t, m, k=k: gw.at[pl.ds(k, 1), t, block_rows(m)],
                          lambda t, at, k=k, masks=masks: gw.at[pl.ds(k, 1), t, block_rows(masks[at])],
                          pl.ds(k, 1), halves, inbox, order, shards.at[pl.ds(k, 1)]))
    stages = bits

    steps = tensor * tensor
    step_sem, x_sem = ld.slots(4), ld.slots(2)

    def step_copies(step, slot):
        t, g = p.near(tensor - 1 - step // tensor), p.near(tensor - 1 - lax.rem(step, tensor))
        here = pl.ds(pl.multiple_of(t * rows, rows), rows)
        return (pltpu.make_async_copy(e_hbm.at[g, :, here], exps.at[slot], local.at[step_sem + slot]),
                pltpu.make_async_copy(kv_hbm.at[g, here], kv.at[slot], local.at[step_sem + 2 + slot]))

    def x_copy(it, slot):
        t = p.near(tensor - 1 - it)
        return pltpu.make_async_copy(x_hbm.at[pl.ds(pl.multiple_of(t * rows, rows), rows)], x.at[slot], local.at[x_sem + slot])

    for copy in step_copies(0, 0):
        copy.start()
    gets = [ld.load(do_hbm, do), ld.load(q_hbm, q)]
    x_copy(0, 0).start()
    gets.append(ld.load(w0_hbm.at[0], w0.at[0]))
    late = [ld.load(w0_hbm.at[1], w0.at[1])]
    own_gets = [ld.load(g_hbm.at[:, :, block_rows(m)], own_g.at[:, :, at]) for at, m in enumerate(stay)]
    late += [ld.load(g_o_hbm, gw.at[1]), ld.load(resid_hbm, own)]
    own_sem = ld.slots(1)
    tiny[:8] = g_vecs[...]
    for t in range(tensor):
        tiny[8 + t:9 + t] = g_bup[t]
    tiny[8 + tensor:] = jnp.zeros_like(tiny[8 + tensor:])
    p.greet()
    wacc[...] = jnp.zeros_like(wacc)
    dqt[...] = jnp.zeros_like(dqt)
    p.met()
    for n in range(tensor)[::-1]:
        for f in folds:
            f.first(n)
    swap_slot = s.slots(1)
    s.start(low_hbm, swapped, swap_slot, p.twin, p.swap, p.off)
    twin, mate, fin = s.slots(tensor), s.slots(tensor), s.slots(1)
    fin_send, own_slot = s.slots(tensor), s.slots(1)
    tiny_slots = s.slots((fsdp * tensor).bit_length() - 1)
    for copy in gets:
        copy.wait()

    def rows_to_twin(n, slot):
        t = p.near(n)
        s.start(dxb.at[slot], twin_in.at[t], twin + t, p.twin, p.j, p.off, note=False)

    def rows_from_twin(n, slot):
        t = p.near(n)

        @pl.when(p.on)
        def _():
            s.arrive(twin_in.at[t], twin + t)
            twin_in[t] = (twin_in[t].astype(F32) + dxb[slot].astype(F32)).astype(BF16)
        if p.half > 1:
            to_mate = p.on & ((n == 1) | ((n > 1) & p.is_end))
            s.start(twin_in.at[t], mate_in.at[t], mate + t, p.i, p.mate, to_mate, note=False)
        else:
            s.start(twin_in.at[t], fin_in, fin, p.i, t, p.on, fin_send + t, note=False)

    def rows_from_mate(n):
        t = p.near(n)
        here = p.on & p.is_edge

        @pl.when(here)
        def _():
            s.arrive(mate_in.at[t], mate + t)
            mate_in[t] = (mate_in[t].astype(F32) + twin_in[t].astype(F32)).astype(BF16)
        s.start(mate_in.at[t], fin_in, fin, p.i, t, here, fin_send + t, note=False)

    def one(it, gi):
        n = tensor - 1 - it
        t, g = p.near(n), p.near(tensor - 1 - gi)
        step = it * tensor + gi
        slot, x_slot = lax.rem(step, 2), lax.rem(it, 2)
        for copy in step_copies(step, slot):
            copy.wait()

        @pl.when(step + 1 < steps)
        def _():
            for copy in step_copies(step + 1, 1 - slot):
                copy.start()

        @pl.when(gi == 0)
        def _():
            x_copy(it, x_slot).wait()

            pl.when(it + 1 < tensor)(x_copy(it + 1, 1 - x_slot).start)
            dx[...] = jnp.zeros_like(dx)

            @pl.when(it + 1 == tensor)
            def _():
                copy = pltpu.make_async_copy(x_hbm.at[pl.ds(pl.multiple_of(p.block * rows, rows), rows)], x.at[1 - x_slot], local.at[own_sem])
                copy.start()
                copy.wait()

        for h in range(heads):
            cols = slice(h * 128, h * 128 + 128)
            k = kv[slot, :, cols]
            d = do[g, :, cols]
            e = exps[slot, h]
            ds = (e.astype(F32) * (dot(k, d, NT) - r[g, h:h + 1])).astype(BF16)
            dkv[:, cols] = (dot(ds, q[g, :, cols], NN) + dot(e, d, NN)).astype(BF16)
            dqt[g, h] += dot(k, ds, TN)
        dk = dkv[...]
        bias = pl.ds(8 + tensor + g, 1)
        tiny[bias, :width] += colsum(dk)
        dx[...] += dot(dk, w0[0, g], NT)
        wacc[g] += dot(x[x_slot], dk, TN)

        @pl.when(it == tensor - 1)
        def _():
            for h in range(heads):
                cols = slice(h * 128, h * 128 + 128)
                dq = dqt[g, h] * np.float32(HEAD ** -0.5)
                dq = jnp.where(lax.broadcasted_iota(jnp.int32, dq.shape, 0) < HEAD, dq, 0.0)
                dkv[:, cols] = dq.T.astype(BF16)
            dq = dkv[...]
            tiny[bias, width:] = colsum(dq)
            own[...] += dot(dq, w0[1, g], NT)
            gw[1, g] = (dot(x[1 - x_slot], dq, TN) + gw[1, g].astype(F32)).astype(BF16)
            gw[0, g] = wacc[g].astype(BF16)
            for f in tails:
                f.first(tensor - 1 - gi)

        @pl.when(step == 0)
        def _():
            for copy in own_gets + late:
                copy.wait()

        @pl.when((gi == 0) & (it >= 1))
        def _():
            for f in folds:
                for k in range(2, stages):
                    f.add(k, n + 1)
                f.line_first(n + 1)

        @pl.when((gi == 0) & (it >= 2))
        def _():
            if p.half > 1:
                rows_from_mate(n + 2)

        @pl.when(gi == 0)
        def _():
            for f in folds:
                f.add(0, n)

        @pl.when((gi == min(1, tensor - 1)) & (it >= 1))
        def _():
            rows_from_twin(n + 1, 1 - x_slot)

        @pl.when(gi == min(2, tensor - 1))
        def _():
            for f in folds:
                f.add(1, n)

        @pl.when((gi == tensor - 1) & (it >= 1))
        def _():
            for f in folds:
                f.line_next(n + 1)

        @pl.when((it == tensor - 1) & (gi >= 1))
        def _():
            for f in tails:
                f.add(0, tensor - gi)

        @pl.when((gi == tensor - 1) & (it < tensor - 1))
        def _():
            pl.when((it >= 2) & p.off)(lambda: s.left(dxb.at[x_slot], twin + p.near(n + 2)))
            dxb[x_slot] = dx[...].astype(BF16)
            rows_to_twin(n, x_slot)

    def body(step, carry):
        one(step // tensor, lax.rem(step, tensor))
        return carry

    lax.fori_loop(0, steps, body, 0)
    last_slot = (tensor - 1) % 2

    @pl.when(p.off)
    def _():
        if tensor > 2:
            s.left(dxb.at[last_slot], twin + p.near(2))
        dxb[last_slot] = dx[...].astype(BF16)
        mate_in[1] = own[...].astype(BF16)
    rows_to_twin(0, last_slot)
    s.start(mate_in.at[1], mate_in.at[0], own_slot, p.twin, p.swap, p.off)

    tiny_at = [0]

    def tiny_step(begin, end):
        k = tiny_at[0]
        if k == len(range((fsdp * tensor).bit_length() - 1)):
            return
        bit = 1 << k
        i, j = (flip(p.i, bit), p.j) if bit < fsdp else (p.i, flip(p.j, bit // fsdp))
        copy = s.copy(tiny, tiny_in.at[k], tiny_slots + k, i, j)
        if begin:
            copy.start()
        if end:
            copy.wait_recv()
            copy.wait_send()
            tiny[...] += tiny_in[k]
            tiny_at[0] += 1

    tiny_step(True, False)
    for f in folds:
        for k in range(2, stages):
            f.add(k, 0)
    for f in tails:
        f.add(0, 0)
    for n in range(tensor)[::-1]:
        for f in tails:
            f.add(1, n)
        if n < tensor - 1:
            for f in tails:
                for k in range(2, stages):
                    f.add(k, n + 1)
                f.line_first(n + 1)
        tiny_step(False, True)
        tiny_step(True, False)
    for f in folds:
        f.result()
    for f in tails:
        for k in range(2, stages):
            f.add(k, 0)
    for n in range(1, tensor)[::-1]:
        for f in tails:
            f.line_next(n)
        tiny_step(False, True)
        tiny_step(True, False)
    while tiny_at[0] < (fsdp * tensor).bit_length() - 1:
        tiny_step(False, True)
        tiny_step(True, False)

    @pl.when(p.on)
    def _():
        s.arrive(twin_in.at[p.j], twin + p.j)
        dx[...] += own[...] + twin_in[p.j].astype(F32)
        if p.half > 1:
            s.arrive(mate_in.at[p.j], mate + p.j)
            dx[...] += mate_in[p.j].astype(F32)

    @pl.when(p.off)
    def _():
        s.arrive(fin_in, fin)
        s.arrive(mate_in.at[0], own_slot)
        dx[...] = fin_in[...].astype(F32) + mate_in[0].astype(F32)
    s.arrive(swapped, swap_slot, p.off)
    for f in tails:
        f.result()
    for n in range(tensor):
        t = p.near(n)
        if n < 2:
            s.left(dxb.at[0], twin + t, p.off)
        if n > 0:
            if p.half > 1:
                s.left(dxb.at[0], mate + t, p.on & ((n == 1) | p.is_end))
                if n > 1:
                    s.left(dxb.at[0], fin_send + t, p.on & p.is_edge)
            else:
                s.left(dxb.at[0], fin_send + t, p.on)
    for f in folds + tails:
        f.finish()
    s.finish()


def last_part(fsdp, tensor, x, w0, kv, q, do, g_o, g, e, resid, low, r, g_bup, g_vecs):
    groups, heads, _, rows = e.shape
    model, width = w0.shape[2:]
    shard = model // fsdp
    bits = fsdp.bit_length() - 1
    vm = lambda d, *shape: pltpu.VMEM(shape, d)
    slots = 4 * ((fsdp - 1) * tensor + 2 * tensor) + 3 * tensor + 16
    scratch = [vm(BF16, 6, fsdp >> (k + 1), tensor, shard, width) for k in range(bits)]
    scratch += [vm(BF16, 6, 2, tensor, shard, width), vm(BF16, 4, tensor, fsdp // 2, shard, width), vm(BF16, 2, rows, model),
                vm(BF16, 2, tensor, model, width), vm(BF16, 2, rows, width), vm(BF16, tensor, rows, width), vm(BF16, tensor, rows, width),
                vm(F32, tensor, heads, 128, rows), vm(F32, tensor, model, width), vm(BF16, 2, heads, rows, rows),
                vm(BF16, 2, tensor, model, width), vm(BF16, rows, width), vm(BF16, 2, rows, model), vm(F32, rows, model), vm(BF16, tensor, rows, model),
                vm(BF16, tensor, rows, model), vm(BF16, rows, model), vm(F32, (fsdp * tensor).bit_length() - 1, 8 + 2 * tensor, model),
                pltpu.SemaphoreType.DMA((slots,)), pltpu.SemaphoreType.DMA((slots,)), pltpu.SemaphoreType.DMA((16 + fsdp,))]
    return pl.pallas_call(
        functools.partial(last_kernel, fsdp, tensor),
        in_specs=[ANY] * 10 + [VM] * 3, out_specs=[VM] * 3 + [ANY],
        out_shape=[jax.ShapeDtypeStruct(s, d) for s, d in [
            ((6, shard, width), F32), ((rows, model), F32), ((8 + 2 * tensor, model), F32), ((rows, model), BF16)]],
        scratch_shapes=scratch,
        compiler_params=pltpu.CompilerParams(collective_id=1, has_side_effects=True, vmem_limit_bytes=65400 * 1024),
    )(x, w0, kv, q, do, g_o, g, e, resid, low, r, g_bup, g_vecs)


def final_kernel(fsdp, tensor, shards, dx, tiny, out, swapped,
                 output, grad_tokens, g_query, g_key, g_value, g_out, g_up, g_down, b_query, b_value, b_up, *vectors):
    p = Place(fsdp, tensor)
    columns, width = g_query.shape[1], shards.shape[2]
    shard = shards.shape[1]
    grad_tokens[...] = dx[...]

    @pl.when(p.on)
    def _():
        output[...] = out[...]

    @pl.when(p.off)
    def _():
        output[...] = swapped[...].astype(F32)
    heads = [(h, slice(h * HEAD, h * HEAD + HEAD), slice(2 * h * HEAD, 2 * h * HEAD + 2 * HEAD)) for h in range(columns // HEAD)]
    out_rows = []
    for h, cols, both in heads:
        keys, query = shards[0, :, both], shards[1, :, both]
        g_key[:, cols], g_value[:, cols] = keys[:, :HEAD], keys[:, HEAD:]
        g_query[:, cols] = query[:, :HEAD]
        out_rows.append(query[:, HEAD:])
    g_out[...] = jnp.concatenate(out_rows, 1).T
    for k in range(2):
        cols = slice(k * width, k * width + width)
        g_up[:, cols] = shards[2 + 2 * k]
        g_down[:, cols] = shards[3 + 2 * k]

    def take(row, ones):
        return lax.dot_general(row, ones, ((NT[:1], NT[1:]), ((), ())), precision=lax.Precision.HIGHEST, preferred_element_type=F32)

    few, many = columns // fsdp, 2 * width // fsdp
    both = tiny[pl.ds(8 + tensor + p.j, 1), :]
    b_query[...] = take(both[:, width:], spread(head_lanes(False), few, p.i, 0, width))
    b_value[...] = take(both[:, :width], spread(head_lanes(True), few, p.i, 0, width))
    b_up[...] = take(tiny[pl.ds(8 + p.j, 1), :], spread(lambda lane: lane, many, p.i, 0, 2 * width))
    rows = take(tiny[:8], spread(lambda lane: lane, shard, p.i, 0, shard * fsdp))
    for k, vector in enumerate(vectors):
        vector[...] = rows[k:k + 1]


def final_part(fsdp, tensor, shards, dx, tiny, out, swapped):
    _, shard, width = shards.shape
    rows, model = dx.shape
    columns = width // 2
    flat, square = (rows, model), (shard, columns)
    results = pl.pallas_call(
        functools.partial(final_kernel, fsdp, tensor),
        in_specs=[VM] * 5, out_specs=[VM] * 17,
        out_shape=[jax.ShapeDtypeStruct(s, F32) for s in [
            flat, flat, square, square, square, (columns, shard), (shard, 2 * width), (shard, 2 * width),
            (1, columns // fsdp), (1, columns // fsdp), (1, 2 * width // fsdp)] + [(1, shard)] * 6],
        compiler_params=pltpu.CompilerParams(vmem_limit_bytes=VMEM_LIMIT),
    )(shards, dx, tiny, out, swapped)
    return (*results[:7], results[7].T, *[r.reshape(-1) for r in results[8:]])


def normalize(values, gain, shift):
    average = jnp.mean(values, -1, keepdims=True)
    centered = values - average
    inverse = lax.rsqrt(jnp.mean(centered * centered, -1, keepdims=True) + EPSILON)
    return centered * inverse * gain + shift


def exact_gelu(values):
    return jax.nn.gelu(values, approximate=False)


def outer_sum(left, right):
    return dot(left, right, TN)


def times_transposed(left, right):
    return dot(left, right, NT)


def plain(
    tokens,
    cotangent,
    w_query,
    w_key,
    w_value,
    w_out,
    w_up,
    w_down,
    b_query,
    b_value,
    b_up,
    b_out,
    b_down,
    gain_attn,
    shift_attn,
    gain_ffn,
    shift_ffn,
):
    gathered = (
        lax.all_gather(w_query, "fsdp", axis=0, tiled=True),
        lax.all_gather(w_key, "fsdp", axis=0, tiled=True),
        lax.all_gather(w_value, "fsdp", axis=0, tiled=True),
        lax.all_gather(w_out, "fsdp", axis=1, tiled=True),
        lax.all_gather(w_up, "fsdp", axis=0, tiled=True),
        lax.all_gather(w_down, "fsdp", axis=1, tiled=True),
        lax.all_gather(b_query, "fsdp", axis=0, tiled=True),
        lax.all_gather(b_value, "fsdp", axis=0, tiled=True),
        lax.all_gather(b_up, "fsdp", axis=0, tiled=True),
        lax.all_gather(b_out, "fsdp", axis=0, tiled=True),
        lax.all_gather(b_down, "fsdp", axis=0, tiled=True),
        lax.all_gather(gain_attn, "fsdp", axis=0, tiled=True),
        lax.all_gather(shift_attn, "fsdp", axis=0, tiled=True),
        lax.all_gather(gain_ffn, "fsdp", axis=0, tiled=True),
        lax.all_gather(shift_ffn, "fsdp", axis=0, tiled=True),
    )
    (
        query_weight,
        key_weight,
        value_weight,
        out_weight,
        up_weight,
        down_weight,
        query_bias,
        value_bias,
        up_bias,
        out_bias,
        down_bias,
        attn_gain,
        attn_shift,
        ffn_gain,
        ffn_shift,
    ) = gathered
    own_rows = tokens.shape[0]
    seq_len = own_rows * lax.axis_size("tensor")
    heads = query_weight.shape[1] // HEAD
    span = min(512, seq_len)
    blocks = seq_len // span
    scale = HEAD ** (-0.5)
    full_tokens = lax.all_gather(tokens, "tensor", axis=0, tiled=True)
    query = (
        jnp.dot(full_tokens, query_weight, preferred_element_type=jnp.float32)
        + query_bias.astype(jnp.float32)
    ).astype(jnp.bfloat16)
    keys = jnp.dot(full_tokens, key_weight, preferred_element_type=jnp.float32).astype(jnp.bfloat16)
    values = (
        jnp.dot(full_tokens, value_weight, preferred_element_type=jnp.float32)
        + value_bias.astype(jnp.float32)
    ).astype(jnp.bfloat16)
    query_blocks = query.reshape(blocks, span, heads, HEAD)
    key_heads = keys.reshape(seq_len, heads, HEAD)
    value_heads = values.reshape(seq_len, heads, HEAD)

    def scores_of(piece):
        return (
            jnp.einsum("qhd,khd->hqk", piece, key_heads, preferred_element_type=jnp.float32) * scale
        )

    def forward_block(piece):
        scores = scores_of(piece)
        largest = jnp.max(scores, -1, keepdims=True)
        exponent = jnp.exp(scores - largest)
        total = jnp.sum(exponent, -1, keepdims=True)
        soft_low = (exponent / total).astype(jnp.bfloat16)
        result = jnp.einsum(
            "hqk,khd->qhd", soft_low, value_heads, preferred_element_type=jnp.float32
        )
        return (result.astype(jnp.bfloat16), largest, total)

    attended, largest_all, total_all = lax.map(forward_block, query_blocks)
    attended = attended.reshape(seq_len, heads * HEAD)
    attn_part = lax.psum_scatter(
        jnp.dot(attended, out_weight, preferred_element_type=jnp.float32).astype(jnp.bfloat16),
        "tensor",
        scatter_dimension=0,
        tiled=True,
    ).astype(jnp.float32)
    resid_attn = tokens.astype(jnp.float32) + (attn_part + out_bias.astype(jnp.float32))
    hidden, attn_norm_back = jax.vjp(
        normalize, resid_attn, attn_gain.astype(jnp.float32), attn_shift.astype(jnp.float32)
    )
    full_hidden = lax.all_gather(hidden.astype(jnp.bfloat16), "tensor", axis=0, tiled=True)
    pre_act = jnp.dot(full_hidden, up_weight, preferred_element_type=jnp.float32) + up_bias.astype(
        jnp.float32
    )
    activ, gelu_back = jax.vjp(exact_gelu, pre_act)
    activ_low = activ.astype(jnp.bfloat16)
    ffn_part = lax.psum_scatter(
        jnp.dot(activ_low, down_weight, preferred_element_type=jnp.float32).astype(jnp.bfloat16),
        "tensor",
        scatter_dimension=0,
        tiled=True,
    ).astype(jnp.float32)
    resid_ffn = hidden + (ffn_part + down_bias.astype(jnp.float32))
    output, ffn_norm_back = jax.vjp(
        normalize, resid_ffn, ffn_gain.astype(jnp.float32), ffn_shift.astype(jnp.float32)
    )
    matrices = (
        lax.all_gather(w_query, "fsdp", axis=0, tiled=True),
        lax.all_gather(w_key, "fsdp", axis=0, tiled=True),
        lax.all_gather(w_value, "fsdp", axis=0, tiled=True),
        lax.all_gather(w_out, "fsdp", axis=1, tiled=True),
        lax.all_gather(w_up, "fsdp", axis=0, tiled=True),
        lax.all_gather(w_down, "fsdp", axis=1, tiled=True),
    )
    back_query, back_key, back_value, back_out, back_up, back_down = matrices
    grad_resid_ffn, grad_gain_ffn, grad_shift_ffn = ffn_norm_back(cotangent.astype(jnp.float32))
    grad_ffn_full = lax.all_gather(
        grad_resid_ffn.astype(jnp.bfloat16), "tensor", axis=0, tiled=True
    )
    grad_down_bias = jnp.sum(grad_ffn_full, 0, dtype=jnp.float32)
    grad_down_weight = outer_sum(activ_low, grad_ffn_full)
    grad_activ = times_transposed(grad_ffn_full, back_down)
    grad_pre = gelu_back(grad_activ)[0].astype(jnp.bfloat16)
    grad_up_bias = jnp.sum(grad_pre, 0, dtype=jnp.float32)
    grad_up_weight = outer_sum(full_hidden, grad_pre)
    grad_hidden = grad_resid_ffn + lax.psum_scatter(
        times_transposed(grad_pre, back_up).astype(jnp.bfloat16),
        "tensor",
        scatter_dimension=0,
        tiled=True,
    ).astype(jnp.float32)
    grad_resid_attn, grad_gain_attn, grad_shift_attn = attn_norm_back(grad_hidden)
    grad_attn_full = lax.all_gather(
        grad_resid_attn.astype(jnp.bfloat16), "tensor", axis=0, tiled=True
    )
    grad_out_bias = jnp.sum(grad_attn_full, 0, dtype=jnp.float32)
    grad_out_weight = outer_sum(attended, grad_attn_full)
    grad_attended = times_transposed(grad_attn_full, back_out).astype(jnp.bfloat16)
    grad_blocks = grad_attended.reshape(blocks, span, heads, HEAD)

    def backward_block(carry, item):
        piece, grad_piece, largest, total = item
        soft = jnp.exp(scores_of(piece) - largest) / total
        soft_low = soft.astype(jnp.bfloat16)
        grad_soft = jnp.einsum(
            "qhd,khd->hqk", grad_piece, value_heads, preferred_element_type=jnp.float32
        )
        inner = jnp.sum(soft * grad_soft, -1, keepdims=True)
        grad_scores = (soft * (grad_soft - inner)).astype(jnp.bfloat16)
        grad_query_block = (
            jnp.einsum("hqk,khd->qhd", grad_scores, key_heads, preferred_element_type=jnp.float32)
            * scale
        )
        grad_key_sum = (
            carry[0]
            + jnp.einsum("hqk,qhd->khd", grad_scores, piece, preferred_element_type=jnp.float32)
            * scale
        )
        grad_value_sum = carry[1] + jnp.einsum(
            "hqk,qhd->khd", soft_low, grad_piece, preferred_element_type=jnp.float32
        )
        return ((grad_key_sum, grad_value_sum), grad_query_block.astype(jnp.bfloat16))

    zeros = jnp.zeros((seq_len, heads, HEAD), jnp.float32)
    (grad_key_sum, grad_value_sum), grad_query = lax.scan(
        backward_block, (zeros, zeros), (query_blocks, grad_blocks, largest_all, total_all)
    )
    grad_query = grad_query.reshape(seq_len, heads * HEAD)
    grad_keys = grad_key_sum.reshape(seq_len, heads * HEAD).astype(jnp.bfloat16)
    grad_values = grad_value_sum.reshape(seq_len, heads * HEAD).astype(jnp.bfloat16)
    grad_query_bias = jnp.sum(grad_query, 0, dtype=jnp.float32)
    grad_value_bias = jnp.sum(grad_values, 0, dtype=jnp.float32)
    grad_query_weight = outer_sum(full_tokens, grad_query)
    grad_key_weight = outer_sum(full_tokens, grad_keys)
    grad_value_weight = outer_sum(full_tokens, grad_values)
    token_terms = (
        times_transposed(grad_query, back_query)
        + times_transposed(grad_keys, back_key)
        + times_transposed(grad_values, back_value)
    )
    norm_terms = jnp.tile(
        jnp.stack([grad_gain_attn, grad_shift_attn, grad_gain_ffn, grad_shift_ffn]),
        (lax.axis_size("tensor"), 1),
    )
    token_part, norm_sums = (
        lax.psum_scatter(
            token_terms.astype(jnp.bfloat16), "tensor", scatter_dimension=0, tiled=True
        ).astype(jnp.float32),
        lax.psum_scatter(
            norm_terms.astype(jnp.bfloat16), "tensor", scatter_dimension=0, tiled=True
        ).astype(jnp.float32),
    )
    grad_tokens = grad_resid_attn + token_part
    shards = (
        lax.psum_scatter(grad_query_weight, "fsdp", scatter_dimension=0, tiled=True),
        lax.psum_scatter(grad_key_weight, "fsdp", scatter_dimension=0, tiled=True),
        lax.psum_scatter(grad_value_weight, "fsdp", scatter_dimension=0, tiled=True),
        lax.psum_scatter(grad_out_weight, "fsdp", scatter_dimension=1, tiled=True),
        lax.psum_scatter(grad_up_weight, "fsdp", scatter_dimension=0, tiled=True),
        lax.psum_scatter(grad_down_weight, "fsdp", scatter_dimension=1, tiled=True),
        lax.psum_scatter(grad_query_bias, "fsdp", scatter_dimension=0, tiled=True),
        lax.psum_scatter(grad_value_bias, "fsdp", scatter_dimension=0, tiled=True),
        lax.psum_scatter(grad_up_bias, "fsdp", scatter_dimension=0, tiled=True),
        lax.psum_scatter(grad_out_bias, "fsdp", scatter_dimension=0, tiled=True),
        lax.psum_scatter(grad_down_bias, "fsdp", scatter_dimension=0, tiled=True),
        lax.psum_scatter(norm_sums[0], "fsdp", scatter_dimension=0, tiled=True),
        lax.psum_scatter(norm_sums[1], "fsdp", scatter_dimension=0, tiled=True),
        lax.psum_scatter(norm_sums[2], "fsdp", scatter_dimension=0, tiled=True),
        lax.psum_scatter(norm_sums[3], "fsdp", scatter_dimension=0, tiled=True),
    )
    return (
        output,
        grad_tokens,
        shards[0],
        shards[1],
        shards[2],
        shards[3],
        shards[4],
        shards[5],
        shards[6],
        shards[7],
        shards[8],
        shards[9],
        shards[10],
        shards[11],
        shards[12],
        shards[13],
        shards[14],
    )


def fits(tokens, w_query, w_up):
    fsdp, tensor = lax.axis_size("fsdp"), lax.axis_size("tensor")
    shard, columns = w_query.shape
    return (tensor == 4 and fsdp >= 4 and fsdp & (fsdp - 1) == 0 and shard % 16 == 0 and 4 * columns == tokens.shape[1] and columns >= 3 * HEAD and columns % HEAD == 0
            and w_up.shape[1] == 4 * columns and tokens.shape[0] % 128 == 0)


def layer(tokens, cotangent, w_query, w_key, w_value, w_out, w_up, w_down, b_query, b_value, b_up, b_out, b_down,
          gain_attn, shift_attn, gain_ffn, shift_ffn):
    if not fits(tokens, w_query, w_up):
        return plain(tokens, cotangent, w_query, w_key, w_value, w_out, w_up, w_down, b_query, b_value, b_up, b_out, b_down,
                     gain_attn, shift_attn, gain_ffn, shift_ffn)
    fsdp, tensor = lax.axis_size("fsdp"), lax.axis_size("tensor")
    pieces = (b_query, b_value, b_up, b_out, b_down, gain_attn, shift_attn, gain_ffn, shift_ffn)
    total, at, vectors = sum(piece.size for piece in pieces), 0, 0.0
    for piece in pieces:
        vectors += jnp.pad(piece.reshape(1, -1), ((0, 0), (at, total - at - piece.size)))
        at += piece.size
    w0, w1, x, x_own, cot, kv, q, att, exps, inv, smalls = first_part(
        fsdp, tensor, w_query, w_key, w_value, w_out, w_up, w_down.T, vectors, tokens, cotangent)
    out, low, resid, r, do, g_o, g, g_bup, g_vecs = middle_part(x_own, cot, att, w0, w1, smalls, inv)
    shards, grad_tokens, tiny, swapped = last_part(fsdp, tensor, x, w0, kv, q, do, g_o, g, exps, resid, low, r, g_bup, g_vecs)
    return final_part(fsdp, tensor, shards, grad_tokens, tiny, out, swapped)


def solution(mesh):
    return jax.shard_map(
        layer,
        mesh=mesh,
        in_specs=(
            P(("fsdp", "tensor"), None),
            P(("fsdp", "tensor"), None),
            P("fsdp", "tensor"),
            P("fsdp", "tensor"),
            P("fsdp", "tensor"),
            P("tensor", "fsdp"),
            P("fsdp", "tensor"),
            P("tensor", "fsdp"),
            P(("tensor", "fsdp")),
            P(("tensor", "fsdp")),
            P(("tensor", "fsdp")),
            P("fsdp"),
            P("fsdp"),
            P("fsdp"),
            P("fsdp"),
            P("fsdp"),
            P("fsdp"),
        ),
        out_specs=(
            P(("fsdp", "tensor"), None),
            P(("fsdp", "tensor"), None),
            P("fsdp", "tensor"),
            P("fsdp", "tensor"),
            P("fsdp", "tensor"),
            P("tensor", "fsdp"),
            P("fsdp", "tensor"),
            P("tensor", "fsdp"),
            P(("tensor", "fsdp")),
            P(("tensor", "fsdp")),
            P(("tensor", "fsdp")),
            P("fsdp"),
            P("fsdp"),
            P("fsdp"),
            P("fsdp"),
            P("fsdp"),
            P("fsdp"),
        ),
        check_vma=False,
    )
```

```python
import functools

import jax
import jax.numpy as jnp
import numpy as np
from jax import lax
from jax.experimental import pallas as pl
from jax.experimental.pallas import tpu as pltpu
from jax.sharding import PartitionSpec as P

F32, BF16 = jnp.float32, jnp.bfloat16
HEAD = 64
EPSILON = 1e-12
VMEM_LIMIT = 64000 * 1024


def dot(left, right, contract):
    return lax.dot_general(left, right, ((contract[:1], contract[1:]), ((), ())), preferred_element_type=F32)

NN, NT, TN = (1, 0), (1, 1), (0, 0)


def lanes_from(shape, low):
    return lax.broadcasted_iota(jnp.int32, shape, len(shape) - 1) % (2 * HEAD) >= HEAD if not low else \
        lax.broadcasted_iota(jnp.int32, shape, len(shape) - 1) % (2 * HEAD) < HEAD


def project_keys(x, w, bias):
    return (dot(x, w, NN) + bias).astype(BF16)


def project_query(x, w, bias):
    out = dot(x, w, NN) + bias
    return jnp.where(lanes_from(out.shape, True), out.astype(BF16) * BF16(HEAD ** -0.5), BF16(0))


def norm_forward(z):
    mean = jnp.mean(z, -1, keepdims=True)
    centered = z - mean
    inv = lax.rsqrt(jnp.mean(centered * centered, -1, keepdims=True) + EPSILON)
    return centered * inv, inv


def norm_backward(n, inv, dn):
    return inv * (dn - jnp.mean(dn, -1, keepdims=True) - n * jnp.mean(dn * n, -1, keepdims=True))


def colsum(x):
    return jnp.sum(x.astype(F32), axis=0, keepdims=True)


MESH = pl.DeviceIdType.MESH
ANY = pl.BlockSpec(memory_space=pl.ANY)
VM = pl.BlockSpec(memory_space=pltpu.VMEM)


def flip(index, bit):
    return index + bit - 2 * bit * lax.rem(index // bit, 2)


def flips(index, mask):
    bit = 1
    while bit <= mask:
        if mask & bit:
            index = flip(index, bit)
        bit *= 2
    return index


def span(bits):
    masks = [0]
    for bit in bits:
        masks += [m | bit for m in masks]
    return masks


def orders(fsdp):
    bits = [1 << k for k in range(fsdp.bit_length() - 1)]
    return bits[1:] + bits[:1], bits[:0:-1] + bits[:1]


class Place:
    def __init__(self, fsdp, tensor):
        self.fsdp, self.tensor = fsdp, tensor
        self.i, self.j = lax.axis_index("fsdp"), lax.axis_index("tensor")
        self.half = tensor // 2
        self.c = lax.rem(self.i, 2)
        self.h = self.j // self.half
        self.on = self.c == self.h
        self.off = self.c != self.h
        self.twin = flip(self.i, 1)
        self.swap = lax.rem(self.j + self.half, tensor)
        self.block = jnp.where(self.on, self.j, self.swap)
        self.edge = self.half - 1 + self.c
        self.end = self.c * (tensor - 1)
        self.mate = self.h * tensor + 1 - self.j
        self.is_edge = self.j == self.edge
        self.is_end = self.j == self.end

    def other(self, k):
        return (1 - self.c) * (self.half + k) + self.c * (self.half - 1 - k)

    def near(self, n):
        low = jnp.where(self.h == 0, self.j, self.tensor - 1 - self.j)
        if isinstance(n, int):
            place = low if n == 0 else 1 - low if n == 1 else n
        else:
            place = jnp.where(n == 0, low, jnp.where(n == 1, 1 - low, n))
        return jnp.where(self.h == 0, place, self.tensor - 1 - place)

    def barrier(self):
        self.greet()
        self.met()

    def met(self):
        pl.semaphore_wait(pltpu.get_barrier_semaphore(), self.tensor + self.fsdp.bit_length() - 1)

    def greet(self):
        sem = pltpu.get_barrier_semaphore()
        others = [(self.i, lax.rem(self.j + k, self.tensor)) for k in range(1, self.tensor)]
        bit = 1
        while bit < self.fsdp:
            others.append((flip(self.i, bit), self.j))
            bit *= 2
        others.append((self.twin, self.swap))
        for i, j in others:
            pl.semaphore_signal(sem, inc=1, device_id=(i, j), device_id_type=MESH)


class Sends:
    def __init__(self, place, send, recv):
        self.place, self.send, self.recv, self.n, self.started = place, send, recv, 0, []

    def slots(self, n):
        self.n += n
        return self.n - n

    def slot(self):
        return self.slots(1)

    def copy(self, src, dst, slot, i, j, back=None):
        return pltpu.make_async_remote_copy(src_ref=src, dst_ref=dst, send_sem=self.send.at[slot if back is None else back],
                                            recv_sem=self.recv.at[slot], device_id=(i, j), device_id_type=MESH)

    def start(self, src, dst, slot, i, j, when=None, back=None, note=True):
        copy = self.copy(src, dst, slot, i, j, back)
        copy.start() if when is None else pl.when(when)(copy.start)
        if note:
            self.started.append((copy, when))

    def arrive(self, dst, slot, when=None):
        copy = self.copy(dst, dst, slot, self.place.i, self.place.j)
        copy.wait_recv() if when is None else pl.when(when)(copy.wait_recv)

    def left(self, src, slot, when=None):
        copy = self.copy(src, src, slot, self.place.i, self.place.j)
        copy.wait_send() if when is None else pl.when(when)(copy.wait_send)

    def finish(self):
        for copy, when in self.started:
            copy.wait_send() if when is None else pl.when(when)(copy.wait_send)
        self.started = []


def transposed(value):
    return value.astype(F32).T.astype(value.dtype)


def spread(lanes, n, place, first, width):
    at = lanes(lax.broadcasted_iota(jnp.int32, (n, width), 1))
    return jnp.where(at == lax.broadcasted_iota(jnp.int32, (n, width), 0) + place * n, 1.0, 0.0)


def head_lanes(second):
    def lanes(lane):
        inside = lane % 128
        if second:
            return jnp.where(inside >= HEAD, lane // 128 * HEAD + inside - HEAD, -1)
        return jnp.where(inside < HEAD, lane // 128 * HEAD + inside, -1)
    return lanes


def pack_own(p, w_query, w_key, w_value, w_out, w_up, w_down, vectors, pack, small):
    shard, columns = w_query.shape
    width = 2 * columns
    out = transposed(w_out[...])
    for k, (first, second) in enumerate(((w_key[...], w_value[...]), (w_query[...], out))):
        for h in range(columns // HEAD):
            cols = slice(h * HEAD, h * HEAD + HEAD)
            pack[k, :, 2 * h * HEAD:2 * h * HEAD + 2 * HEAD] = jnp.concatenate([first[:, cols], second[:, cols]], 1)
    for k in range(2):
        cols = slice(k * width, k * width + width)
        pack[2 + 2 * k] = w_up[:, cols]
        pack[3 + 2 * k] = w_down[:, cols]
    few, many = columns // p.fsdp, 2 * width // p.fsdp
    take = lambda at, n: vectors[:, at:at + n].astype(BF16)
    put = lambda value, ones: dot(value, ones.astype(BF16), NN)
    small[0:1, width:] = put(take(0, few), spread(head_lanes(False), few, p.i, 0, width))
    small[0:1, :width] = put(take(few, few), spread(head_lanes(True), few, p.i, 0, width))
    small[1:2] = put(take(2 * few, many), spread(lambda lane: lane, many, p.i, 0, 2 * width))
    ones = spread(lambda lane: lane, shard, p.i, 0, shard * p.fsdp)
    for k in range(6):
        small[2 + k:3 + k] = put(take(2 * few + many + k * shard, shard), ones)


class Stream:
    def __init__(self, sends, array, lead, shard, order, own):
        self.s, self.p, self.a, self.lead, self.shard, self.order, self.own = sends, sends.place, array, lead, shard, order, own
        n = self.p.tensor
        self.z, self.back = sends.slots(n), sends.slots(1)
        self.hops = [{m: sends.slots(n) for m in span(order[:k])} for k in range(len(order))]

    def block(self, t, mask):
        rows = pl.ds(pl.multiple_of(flips(self.p.i, mask) * self.shard, self.shard), self.shard)
        return self.a.at[(*self.lead, t, rows)]

    def first_line(self):
        s, p = self.s, self.p
        there = self.block(p.j, 0)
        s.start(self.own, there, self.z + p.j, p.i, p.j + 1, p.j + 1 < p.tensor, note=False)
        s.start(self.own, there, self.z + p.j, p.i, p.j - 1, p.j > 0, self.back, note=False)

    def first_fan(self):
        self.fan(0, 0, self.p.j, self.own)

    def fan(self, mask, k, t, src=None):
        for n in range(k, len(self.order)):
            there = self.block(t, mask)
            self.s.start(there if src is None else src, there, self.hops[n][mask] + t, flip(self.p.i, self.order[n]), self.p.j, note=False)

    def line(self, n):
        s, p = self.s, self.p
        t = p.near(n)
        there = self.block(t, 0)
        s.arrive(there, self.z + t)
        ahead = p.j + jnp.where(t < p.j, 1, -1)
        s.start(there, there, self.z + t, p.i, ahead, (ahead >= 0) & (ahead < p.tensor), note=False)
        self.fan(0, 0, t)

    def finish(self):
        s, p = self.s, self.p
        here = self.block(p.j, 0)
        s.left(here, self.z + p.j, p.j + 1 < p.tensor)
        s.left(here, self.back, p.j > 0)
        for n in range(p.tensor):
            t = p.near(n)
            if n > 0:
                ahead = p.j + jnp.where(t < p.j, 1, -1)
                s.left(here, self.z + t, (ahead >= 0) & (ahead < p.tensor))
            for hops in self.hops:
                for slot in hops.values():
                    s.left(here, slot + t)

    def hop(self, k, n):
        t = self.p.near(n)
        for m in self.hops[k]:
            mask = m | self.order[k]
            self.s.arrive(self.block(t, mask), self.hops[k][m] + t)
            self.fan(mask, k + 1, t)


def attend_group(heads, g, x, own_rows, w_kv, w_qo, smalls, kv, q, att, inv, s_ref, exps, before, after):
    width = heads * 128
    kv[g] = project_keys(x[...], w_kv[g], smalls[g, 0:1, :width])
    q[g] = project_query(x[own_rows, :], w_qo[g], smalls[g, 0:1, width:])
    for h in range(heads):
        cols = slice(h * 128, h * 128 + 128)
        keys = kv[g, :, cols]
        s_ref[...] = dot(keys, q[g, :, cols], NT)
        top = jnp.max(s_ref[...], axis=0, keepdims=True)
        e = jnp.exp(s_ref[...] - top)
        scale = 1.0 / jnp.sum(e, axis=0, keepdims=True)
        before(h)
        exps[h] = e.astype(BF16)
        out = dot(keys, exps[h], TN) * scale
        out = jnp.where(lax.broadcasted_iota(jnp.int32, out.shape, 0) >= HEAD, out, 0.0)
        att[g, :, cols] = out.T.astype(BF16)
        inv[g, h:h + 1] = scale
        after(h)


def first_kernel(fsdp, tensor, w_query, w_key, w_value, w_out, w_up, w_down, vectors, tok, cot, w0_out, w1, x_out, own_out, cot_out, kv_out, q_out, att_out, exp_out,
                 inv, smalls, pack, small, w0, sm, x, kv, q, att, s_ref, exps, send, recv, local):
    p = Place(fsdp, tensor)
    s = Sends(p, send, recv)
    p.greet()
    pack_own(p, w_query, w_key, w_value, w_out, w_up, w_down, vectors, pack, small)
    rows, model = tok.shape
    shard = pack.shape[1]
    heads = exps.shape[0]
    first, second = orders(fsdp)
    kvw = Stream(s, w0, (0,), shard, first, pack.at[0])
    qow = Stream(s, w0, (1,), shard, second, pack.at[1])
    tiny = Stream(s, sm, (), small.shape[0], first, small)
    upper = Stream(s, w1, (pl.ds(0, 2),), shard, first, pack.at[pl.ds(2, 2)])
    lower = Stream(s, w1, (pl.ds(2, 2),), shard, second, pack.at[pl.ds(4, 2)])
    now, later = (kvw, qow, tiny), (upper, lower)
    pieces = 4 if rows % 64 == 0 else 1
    part = rows // pieces
    xin, xtwin, cslot = s.slots(tensor * pieces), s.slots(tensor * pieces), s.slots(1)
    x_at = lambda t: x.at[pl.ds(pl.multiple_of(t * rows, rows), rows)]

    def piece(t, u):
        return x.at[pl.ds(pl.multiple_of(t * rows + u * part, part), part)]

    def send_rows(t, u, i, j, when, twin=False, src=None):
        slot = t * pieces + u
        there = piece(t, u)
        s.start(there if src is None else src.at[pl.ds(u * part, part)], there, xin + slot, i, j, when, xtwin + slot if twin else None)

    def pass_rows(u, n, when, forward):
        t = p.near(n)
        s.arrive(piece(t, u), xin + t * pieces + u, when)
        if forward:
            send_rows(t, u, p.i, p.end, when)
        send_rows(t, u, p.twin, p.j, when, True)

    def edge_rows(u):
        for n in [*range(2, tensor), 1]:
            pass_rows(u, n, p.on & p.is_edge, p.half > 1 and n > 1)

    def end_rows(u):
        for n in range(1, tensor):
            pass_rows(u, n, p.on & jnp.logical_not(p.is_edge), False)
    locals_ = []

    def keep(src, dst, when=None):
        copy = pltpu.make_async_copy(src, dst, local.at[len(locals_)])
        copy.start() if when is None else pl.when(when)(copy.start)
        locals_.append((copy, when))
        return len(locals_) - 1

    def kept(k):
        copy, when = locals_[k]
        copy.wait() if when is None else pl.when(when)(copy.wait)
        locals_[k] = None

    mine = pl.ds(pl.multiple_of(p.i * shard, shard), shard)
    own = [keep(pack.at[k], w0.at[k, p.j, mine]) for k in range(2)]
    own += [keep(pack.at[2 + k], w1.at[k, p.j, mine]) for k in range(4)]
    own += [keep(small, sm.at[p.j, pl.ds(pl.multiple_of(p.i * small.shape[0], small.shape[0]), small.shape[0])])]
    own += [keep(tok, x_at(p.j), p.on), keep(cot, cot_out, p.on)]
    p.met()
    for g in now:
        g.first_line()
    for g in now:
        g.first_fan()
    for u in range(pieces):
        send_rows(p.j, u, p.i, p.edge, p.off, src=tok)
        if p.half > 1:
            send_rows(p.j, u, p.i, p.mate, p.on, src=tok)
        send_rows(p.j, u, p.twin, p.j, p.on, True, tok)
    for g in later:
        g.first_fan()
    stages = len(first)
    for step in range(1, tensor + stages - 1):
        if step < tensor:
            for g in now:
                g.line(step)
        for k in range(stages - 1):
            if 0 <= step - 1 - k < tensor:
                for g in now:
                    g.hop(k, step - 1 - k)
        if step - 1 < pieces:
            edge_rows(step - 1)
    for u in range(tensor + stages - 2, pieces):
        edge_rows(u)
    for u in range(pieces):
        end_rows(u)
    for g in later:
        g.first_line()
    for k in range(stages - 1):
        for g in later:
            g.hop(k, 0)
    s.start(cot, cot_out, cslot, p.twin, p.swap, p.off)
    for n in range(tensor):
        for g in now:
            g.hop(stages - 1, n)
    for t in range(tensor):
        for u in range(pieces):
            s.arrive(piece(t, u), xin + t * pieces + u, p.off)
    for k in own[:8]:
        kept(k)
    for t in range(tensor):
        total = sm[t, :small.shape[0], :]
        for i in range(1, fsdp):
            total += sm[t, i * small.shape[0]:(i + 1) * small.shape[0], :]
        smalls[t] = total
    keep(x_at(p.block), own_out)
    for t in range(tensor):
        keep(x_at(t), x_out.at[pl.ds(t * rows, rows)])
    for k in range(2):
        keep(w0.at[k], w0_out.at[k])
    fixed = len(locals_)
    sem = lambda k: local.at[fixed + k]

    def group(g, carry):
        def exp_copy(h, g):
            return pltpu.make_async_copy(exps.at[h], exp_out.at[g, h], sem(h))

        def before(h):
            pl.when(g > 0)(lambda: exp_copy(h, g - 1).wait())

        def after(h):
            exp_copy(h, g).start()
            point = {0: 0, heads // 2: 1, heads - 1: 2}.get(h)
            if point == 0:
                @pl.when(g >= 2)
                def _():
                    for st in later:
                        for k in range(1, stages - 1):
                            st.hop(k, g - 1)
            if point == 1:
                @pl.when(g >= 1)
                def _():
                    for st in later:
                        st.hop(0, g)
            if point == 2:
                @pl.when(g < tensor - 1)
                def _():
                    for st in later:
                        st.line(g + 1)

        attend_group(heads, g, x, pl.ds(pl.multiple_of(p.block * rows, rows), rows), w0.at[0], w0.at[1], smalls, kv, q, att, inv,
                     s_ref, exps, before, after)
        for k, (src, dst) in enumerate(((kv, kv_out), (q, q_out), (att, att_out))):
            pltpu.make_async_copy(src.at[g], dst.at[g], sem(heads + k * tensor + g)).start()
        return carry

    lax.fori_loop(0, tensor, group, 0)
    for k in range(1, stages - 1):
        for st in later:
            st.hop(k, tensor - 1)
    for n in range(tensor):
        for st in later:
            st.hop(stages - 1, n)
    for h in range(heads):
        pltpu.make_async_copy(exps.at[h], exp_out.at[0, h], sem(h)).wait()
    for k, (src, dst) in enumerate(((kv, kv_out), (q, q_out), (att, att_out))):
        for g in range(tensor):
            pltpu.make_async_copy(src.at[g], dst.at[g], sem(heads + k * tensor + g)).wait()
    s.arrive(cot_out, cslot, p.off)
    for k in range(len(locals_)):
        if locals_[k] is not None:
            kept(k)
    s.finish()
    for st in now + later:
        st.finish()


def first_part(fsdp, tensor, w_query, w_key, w_value, w_out, w_up, w_down, vectors, tok, cot):
    shard, width = w_query.shape[0], 2 * w_query.shape[1]
    rows, model = tok.shape
    heads, keys = width // 128, tensor * rows
    slots = 5 * (tensor + 1 + (fsdp - 1) * tensor) + 8 * tensor + 1
    return pl.pallas_call(
        functools.partial(first_kernel, fsdp, tensor),
        in_specs=[VM] * 9, out_specs=[ANY] * 9 + [VM] * 2,
        out_shape=[jax.ShapeDtypeStruct(s, d) for s, d in [
            ((2, tensor, model, width), BF16), ((4, tensor, model, width), BF16), ((keys, model), BF16), ((rows, model), BF16),
            ((rows, model), BF16), ((tensor, keys, width), BF16), ((tensor, rows, width), BF16), ((tensor, rows, width), BF16),
            ((tensor, heads, keys, rows), BF16), ((tensor, 8, rows), F32), ((tensor, 8, model), F32)]],
        scratch_shapes=[pltpu.VMEM(s, d) for s, d in [
            ((6, shard, width), BF16), ((8, model), F32),
            ((2, tensor, model, width), BF16), ((tensor, fsdp * 8, model), F32), ((keys, model), BF16),
            ((tensor, keys, width), BF16), ((tensor, rows, width), BF16), ((tensor, rows, width), BF16), ((keys, rows), F32),
            ((heads, keys, rows), BF16)]] + [pltpu.SemaphoreType.DMA((slots,)), pltpu.SemaphoreType.DMA((slots,)),
                                             pltpu.SemaphoreType.DMA((16 + 5 * tensor + heads,))],
        compiler_params=pltpu.CompilerParams(collective_id=0, has_side_effects=True, vmem_limit_bytes=VMEM_LIMIT),
    )(w_query, w_key, w_value, w_out, w_up, w_down, vectors, tok, cot)


class Fold:
    def __init__(self, sends, give, keep, lead, halves, inbox, order, out):
        self.s, self.p, self.give, self.keep, self.lead = sends, sends.place, give, keep, lead
        self.halves, self.inbox, self.order, self.out = halves, inbox, order[::-1], out
        n = self.p.tensor
        self.masks = [span(self.order[k + 1:]) for k in range(len(order))]
        self.slot = [[sends.slots(n) for _ in masks] for masks in self.masks]
        self.z = sends.slots(2 * n)

    def half(self, k, mask, t):
        return self.halves[k].at[(self.lead, self.masks[k].index(mask), t)]

    def first(self, n):
        t, bit = self.p.near(n), self.order[0]
        for k, m in enumerate(self.masks[0]):
            self.s.start(self.give(t, m | bit), self.half(0, m, t), self.slot[0][k] + t, flip(self.p.i, bit), self.p.j, note=False)

    def add(self, k, n):
        t = self.p.near(n)
        for at, m in enumerate(self.masks[k]):
            here = self.half(k, m, t)
            self.s.arrive(here, self.slot[k][at] + t)
            mine = self.keep(t, at) if k == 0 else self.half(k - 1, m, t)
            here[...] = (here[...].astype(F32) + mine[...].astype(F32)).astype(BF16)
        if k + 1 < len(self.order):
            bit = self.order[k + 1]
            for at, m in enumerate(self.masks[k + 1]):
                self.s.start(self.half(k, m | bit, t), self.half(k + 1, m, t), self.slot[k + 1][at] + t,
                             flip(self.p.i, bit), self.p.j, note=False)

    def total(self, t):
        return self.half(len(self.order) - 1, 0, t)

    def way(self, n):
        t = self.p.near(n)
        right = t > self.p.j
        there = self.p.j + jnp.where(right, 1, -1)
        before = self.p.j - jnp.where(right, 1, -1)
        side = jnp.where(right, 0, 1)
        has = (before >= 0) & (before < self.p.tensor)
        return t, there, has, self.inbox.at[(self.lead, side, t)], self.z + side * self.p.tensor + t

    def line_first(self, n):
        t, there, has, box, slot = self.way(n)
        self.s.start(self.total(t), box, slot, self.p.i, there, jnp.logical_not(has), note=False)

    def line_next(self, n):
        t, there, has, box, slot = self.way(n)
        total = self.total(t)

        @pl.when(has)
        def _():
            self.s.arrive(box, slot)
            box[...] = (box[...].astype(F32) + total[...].astype(F32)).astype(BF16)
            self.s.start(box, box, slot, self.p.i, there, note=False)

    def result(self):
        p = self.p
        self.out[...] = self.total(p.j)[...].astype(F32)
        for side, there in ((0, p.j > 0), (1, p.j < p.tensor - 1)):
            box = self.inbox.at[(self.lead, side, p.j)]

            @pl.when(there)
            def _(box=box, side=side):
                self.s.arrive(box, self.z + side * p.tensor + p.j)
                self.out[...] += box[...].astype(F32)

    def finish(self):
        here = self.half(0, self.masks[0][0], 0)
        for n in range(self.p.tensor):
            t = self.p.near(n)
            for slots in self.slot:
                for slot in slots:
                    self.s.left(here, slot + t)
            if n > 0:
                self.s.left(here, self.way(n)[4])

class Loads:
    def __init__(self, sems):
        self.sems, self.n = sems, 0

    def slots(self, n):
        self.n += n
        return self.n - n

    def load(self, src, dst):
        copy = pltpu.make_async_copy(src, dst, self.sems.at[self.slots(1)])
        copy.start()
        return copy

    def series(self, src, dst, n):
        first = self.slots(n)
        for k in range(n):
            pltpu.make_async_copy(src.at[k], dst.at[k], self.sems.at[first + k]).start()
        return lambda k: pltpu.make_async_copy(src.at[k], dst.at[k], self.sems.at[first + k]).wait()


def middle_kernel(groups, x_hbm, cot_hbm, att_hbm, w0_hbm, w1_hbm, smalls, inv,
                  out_ref, out_low, resid_ref, r_ref, datt_hbm, g_o_hbm, g_hbm, g_bup, g_vecs,
                  x_own, cot, att, w_qo, w1, datt, g_o, grads, act, slope, hid, n1_ref, acc, low, hl, sems):
    ld = Loads(sems)
    width = w_qo.shape[2]
    get_x = ld.load(x_hbm, x_own)
    get_att = ld.series(att_hbm, att, groups)
    get_qo = ld.series(w0_hbm.at[1], w_qo, groups)
    gets = [ld.series(w1_hbm.at[k], w1.at[k], groups) for k in range(4)]
    get_cot = ld.load(cot_hbm, cot)
    outs = [(grads.at[k], g_hbm.at[k], ld.slots(groups)) for k in range(4)]
    outs += [(datt, datt_hbm, ld.slots(groups)), (g_o, g_o_hbm, ld.slots(groups))]

    def put(k, g):
        src, dst, first = outs[k]
        return pltpu.make_async_copy(src.at[g], dst.at[g], sems.at[first + g])

    vec = lambda k: smalls[0, 2 + k:3 + k, :]
    get_x.wait()
    acc[...] = x_own[...].astype(F32) + vec(0)

    def branch(g, c):
        get_att(g)
        get_qo(g)
        acc[...] += dot(att[g], w_qo[g], NT)
        return c

    lax.fori_loop(0, groups, branch, 0)
    n1, inv1 = norm_forward(acc[...])
    n1_ref[...] = n1
    hidden = n1 * vec(2) + vec(3)
    hid[...] = hidden
    hl[...] = hidden.astype(BF16)
    acc[...] = hidden + vec(1)

    def forward(g, c):
        for get in gets:
            get(g)
        for k in range(2):
            pre = dot(hl[...], w1[2 * k, g], NN) + smalls[g, 1:2, k * width:(k + 1) * width]
            phi = 0.5 + 0.5 * lax.erf(pre * np.float32(0.5 ** 0.5))
            slope[g, k] = phi + pre * (jnp.exp(-0.5 * pre * pre) * np.float32((2 * np.pi) ** -0.5))
            act[g, k] = (pre * phi).astype(BF16)
            acc[...] += dot(act[g, k], w1[2 * k + 1, g], NT)
        return c

    lax.fori_loop(0, groups, forward, 0)
    n2, inv2 = norm_forward(acc[...])
    out = n2 * vec(4) + vec(5)
    out_ref[...] = out
    out_low[...] = out.astype(BF16)
    get_cot.wait()
    cott = cot[...].astype(F32)
    g_vecs[4:5] = colsum(cott * n2)
    g_vecs[5:6] = colsum(cott)
    resid = norm_backward(n2, inv2, cott * vec(4))
    acc[...] = resid
    low[...] = resid.astype(BF16)
    g_vecs[1:2] = colsum(low[...])

    def back(g, c):
        for k in range(2):
            grads[2 * k + 1, g] = dot(low[...], act[g, k], TN).astype(BF16)
            gp = (dot(low[...], w1[2 * k + 1, g], NN) * slope[g, k]).astype(BF16)
            act[g, k] = gp
            g_bup[g, :, k * width:(k + 1) * width] = colsum(gp)
            grads[2 * k, g] = dot(hl[...], gp, TN).astype(BF16)
            acc[...] += dot(act[g, k], w1[2 * k, g], NT)
        for k in range(4):
            put(k, g).start()
        return c

    lax.fori_loop(0, groups, back, 0)
    gh = acc[...]
    g_vecs[2:3] = colsum(gh * n1_ref[...])
    g_vecs[3:4] = colsum(gh)
    ga = norm_backward(n1_ref[...], inv1, gh * vec(2))
    resid_ref[...] = ga
    low[...] = ga.astype(BF16)
    g_vecs[0:1] = colsum(low[...])
    g_vecs[6:8] = jnp.zeros_like(g_vecs[6:8])

    def last(g, c):
        da = dot(low[...], w_qo[g], NN)
        da = jnp.where(lanes_from(da.shape, False), da, 0.0).T.astype(BF16).astype(F32)
        prod = da * att[g].T.astype(F32)
        for h in range(width // 128):
            cols = slice(h * 128, h * 128 + 128)
            scale = inv[g, h:h + 1]
            r_ref[g, h:h + 1] = jnp.sum(prod[cols], axis=0, keepdims=True) * scale
            datt[g, :, cols] = (da[cols] * scale).T.astype(BF16)
        g_o[g] = dot(low[...], att[g], TN).astype(BF16)
        put(4, g).start()
        put(5, g).start()
        return c

    lax.fori_loop(0, groups, last, 0)
    for k in range(6):
        for g in range(groups):
            put(k, g).wait()


def middle_part(x_own, cot, att, w0, w1, smalls, inv):
    _, groups, model, width = w0.shape
    rows = x_own.shape[0]
    wide, deep = ((groups, rows, width), BF16), ((groups, model, width), BF16)
    flat, low = ((rows, model), F32), ((rows, model), BF16)
    return pl.pallas_call(
        functools.partial(middle_kernel, groups),
        in_specs=[ANY] * 5 + [VM] * 2, out_specs=[VM] * 4 + [ANY, ANY, ANY, VM, VM],
        out_shape=[jax.ShapeDtypeStruct(s, d) for s, d in [
            flat, low, flat, ((groups, 8, rows), F32), wide, deep, ((4, groups, model, width), BF16), ((groups, 1, 2 * width), F32), ((8, model), F32)]],
        scratch_shapes=[pltpu.VMEM(s, d) for s, d in [
            low, low, wide, deep, ((4, groups, model, width), BF16), wide, deep, ((4, groups, model, width), BF16),
            ((groups, 2, rows, width), BF16), ((groups, 2, rows, width), F32), flat, flat, flat, low, low]]
        + [pltpu.SemaphoreType.DMA((12 * groups + 2,))],
        compiler_params=pltpu.CompilerParams(vmem_limit_bytes=VMEM_LIMIT),
    )(x_own, cot, att, w0, w1, smalls, inv)


def last_kernel(fsdp, tensor, x_hbm, w0_hbm, kv_hbm, q_hbm, do_hbm, g_o_hbm, g_hbm, e_hbm, resid_hbm, low_hbm, r, g_bup, g_vecs,
                shards, dx, tiny, swapped, *scratch):
    bits = fsdp.bit_length() - 1
    halves, scratch = scratch[:bits], scratch[bits:]
    (inbox, own_g, x, w0, kv, q, do, dqt, wacc, exps, gw, dkv, dxb, own, twin_in, mate_in, fin_in, tiny_in, send, recv, local) = scratch
    p = Place(fsdp, tensor)
    s, ld = Sends(p, send, recv), Loads(local)
    _, heads, rows, _ = exps.shape
    model, width = gw.shape[2:]
    shard = model // fsdp
    first, second = orders(fsdp)
    block_rows = lambda mask: pl.ds(pl.multiple_of(flips(p.i, mask) * shard, shard), shard)
    pair = lambda k: pl.ds(2 * k, 2)
    stay = [m for m in span(first[::-1][1:])]
    folds = []
    for k, order in enumerate((first, second)):
        masks = span(order[::-1][1:])
        folds.append(Fold(s, lambda t, m, k=k: g_hbm.at[pair(k), t, block_rows(m)],
                          lambda t, at, k=k, masks=masks: own_g.at[pair(k), t, stay.index(masks[at])],
                          pair(k + 1), halves, inbox, order, shards.at[pair(k + 1)]))
    tails = []
    for k, order in enumerate((first, second)):
        masks = span(order[::-1][1:])
        tails.append(Fold(s, lambda t, m, k=k: gw.at[pl.ds(k, 1), t, block_rows(m)],
                          lambda t, at, k=k, masks=masks: gw.at[pl.ds(k, 1), t, block_rows(masks[at])],
                          pl.ds(k, 1), halves, inbox, order, shards.at[pl.ds(k, 1)]))
    stages = bits

    steps = tensor * tensor
    step_sem, x_sem = ld.slots(4), ld.slots(2)

    def step_copies(step, slot):
        t, g = p.near(tensor - 1 - step // tensor), p.near(tensor - 1 - lax.rem(step, tensor))
        here = pl.ds(pl.multiple_of(t * rows, rows), rows)
        return (pltpu.make_async_copy(e_hbm.at[g, :, here], exps.at[slot], local.at[step_sem + slot]),
                pltpu.make_async_copy(kv_hbm.at[g, here], kv.at[slot], local.at[step_sem + 2 + slot]))

    def x_copy(it, slot):
        t = p.near(tensor - 1 - it)
        return pltpu.make_async_copy(x_hbm.at[pl.ds(pl.multiple_of(t * rows, rows), rows)], x.at[slot], local.at[x_sem + slot])

    for copy in step_copies(0, 0):
        copy.start()
    gets = [ld.load(do_hbm, do), ld.load(q_hbm, q)]
    x_copy(0, 0).start()
    gets.append(ld.load(w0_hbm.at[0], w0.at[0]))
    late = [ld.load(w0_hbm.at[1], w0.at[1])]
    own_gets = [ld.load(g_hbm.at[:, :, block_rows(m)], own_g.at[:, :, at]) for at, m in enumerate(stay)]
    late += [ld.load(g_o_hbm, gw.at[1]), ld.load(resid_hbm, own)]
    own_sem = ld.slots(1)
    tiny[:8] = g_vecs[...]
    for t in range(tensor):
        tiny[8 + t:9 + t] = g_bup[t]
    tiny[8 + tensor:] = jnp.zeros_like(tiny[8 + tensor:])
    p.greet()
    wacc[...] = jnp.zeros_like(wacc)
    dqt[...] = jnp.zeros_like(dqt)
    p.met()
    for n in range(tensor)[::-1]:
        for f in folds:
            f.first(n)
    swap_slot = s.slots(1)
    s.start(low_hbm, swapped, swap_slot, p.twin, p.swap, p.off)
    twin, mate, fin = s.slots(tensor), s.slots(tensor), s.slots(1)
    fin_send, own_slot = s.slots(tensor), s.slots(1)
    tiny_slots = s.slots((fsdp * tensor).bit_length() - 1)
    for copy in gets:
        copy.wait()

    def rows_to_twin(n, slot):
        t = p.near(n)
        s.start(dxb.at[slot], twin_in.at[t], twin + t, p.twin, p.j, p.off, note=False)

    def rows_from_twin(n, slot):
        t = p.near(n)

        @pl.when(p.on)
        def _():
            s.arrive(twin_in.at[t], twin + t)
            twin_in[t] = (twin_in[t].astype(F32) + dxb[slot].astype(F32)).astype(BF16)
        if p.half > 1:
            to_mate = p.on & ((n == 1) | ((n > 1) & p.is_end))
            s.start(twin_in.at[t], mate_in.at[t], mate + t, p.i, p.mate, to_mate, note=False)
        else:
            s.start(twin_in.at[t], fin_in, fin, p.i, t, p.on, fin_send + t, note=False)

    def rows_from_mate(n):
        t = p.near(n)
        here = p.on & p.is_edge

        @pl.when(here)
        def _():
            s.arrive(mate_in.at[t], mate + t)
            mate_in[t] = (mate_in[t].astype(F32) + twin_in[t].astype(F32)).astype(BF16)
        s.start(mate_in.at[t], fin_in, fin, p.i, t, here, fin_send + t, note=False)

    def one(it, gi):
        n = tensor - 1 - it
        t, g = p.near(n), p.near(tensor - 1 - gi)
        step = it * tensor + gi
        slot, x_slot = lax.rem(step, 2), lax.rem(it, 2)
        for copy in step_copies(step, slot):
            copy.wait()

        @pl.when(step + 1 < steps)
        def _():
            for copy in step_copies(step + 1, 1 - slot):
                copy.start()

        @pl.when(gi == 0)
        def _():
            x_copy(it, x_slot).wait()

            pl.when(it + 1 < tensor)(x_copy(it + 1, 1 - x_slot).start)
            dx[...] = jnp.zeros_like(dx)

            @pl.when(it + 1 == tensor)
            def _():
                copy = pltpu.make_async_copy(x_hbm.at[pl.ds(pl.multiple_of(p.block * rows, rows), rows)], x.at[1 - x_slot], local.at[own_sem])
                copy.start()
                copy.wait()

        for h in range(heads):
            cols = slice(h * 128, h * 128 + 128)
            k = kv[slot, :, cols]
            d = do[g, :, cols]
            e = exps[slot, h]
            ds = (e.astype(F32) * (dot(k, d, NT) - r[g, h:h + 1])).astype(BF16)
            dkv[:, cols] = (dot(ds, q[g, :, cols], NN) + dot(e, d, NN)).astype(BF16)
            dqt[g, h] += dot(k, ds, TN)
        dk = dkv[...]
        bias = pl.ds(8 + tensor + g, 1)
        tiny[bias, :width] += colsum(dk)
        dx[...] += dot(dk, w0[0, g], NT)
        wacc[g] += dot(x[x_slot], dk, TN)

        @pl.when(it == tensor - 1)
        def _():
            for h in range(heads):
                cols = slice(h * 128, h * 128 + 128)
                dq = dqt[g, h] * np.float32(HEAD ** -0.5)
                dq = jnp.where(lax.broadcasted_iota(jnp.int32, dq.shape, 0) < HEAD, dq, 0.0)
                dkv[:, cols] = dq.T.astype(BF16)
            dq = dkv[...]
            tiny[bias, width:] = colsum(dq)
            own[...] += dot(dq, w0[1, g], NT)
            gw[1, g] = (dot(x[1 - x_slot], dq, TN) + gw[1, g].astype(F32)).astype(BF16)
            gw[0, g] = wacc[g].astype(BF16)
            for f in tails:
                f.first(tensor - 1 - gi)

        @pl.when(step == 0)
        def _():
            for copy in own_gets + late:
                copy.wait()

        @pl.when((gi == 0) & (it >= 1))
        def _():
            for f in folds:
                for k in range(2, stages):
                    f.add(k, n + 1)
                f.line_first(n + 1)

        @pl.when((gi == 0) & (it >= 2))
        def _():
            if p.half > 1:
                rows_from_mate(n + 2)

        @pl.when(gi == 0)
        def _():
            for f in folds:
                f.add(0, n)

        @pl.when((gi == min(1, tensor - 1)) & (it >= 1))
        def _():
            rows_from_twin(n + 1, 1 - x_slot)

        @pl.when(gi == min(2, tensor - 1))
        def _():
            for f in folds:
                f.add(1, n)

        @pl.when((gi == tensor - 1) & (it >= 1))
        def _():
            for f in folds:
                f.line_next(n + 1)

        @pl.when((it == tensor - 1) & (gi >= 1))
        def _():
            for f in tails:
                f.add(0, tensor - gi)

        @pl.when((gi == tensor - 1) & (it < tensor - 1))
        def _():
            pl.when((it >= 2) & p.off)(lambda: s.left(dxb.at[x_slot], twin + p.near(n + 2)))
            dxb[x_slot] = dx[...].astype(BF16)
            rows_to_twin(n, x_slot)

    def body(step, carry):
        one(step // tensor, lax.rem(step, tensor))
        return carry

    lax.fori_loop(0, steps, body, 0)
    last_slot = (tensor - 1) % 2

    @pl.when(p.off)
    def _():
        if tensor > 2:
            s.left(dxb.at[last_slot], twin + p.near(2))
        dxb[last_slot] = dx[...].astype(BF16)
        mate_in[1] = own[...].astype(BF16)
    rows_to_twin(0, last_slot)
    s.start(mate_in.at[1], mate_in.at[0], own_slot, p.twin, p.swap, p.off)

    tiny_at = [0]

    def tiny_step(begin, end):
        k = tiny_at[0]
        if k == len(range((fsdp * tensor).bit_length() - 1)):
            return
        bit = 1 << k
        i, j = (flip(p.i, bit), p.j) if bit < fsdp else (p.i, flip(p.j, bit // fsdp))
        copy = s.copy(tiny, tiny_in.at[k], tiny_slots + k, i, j)
        if begin:
            copy.start()
        if end:
            copy.wait_recv()
            copy.wait_send()
            tiny[...] += tiny_in[k]
            tiny_at[0] += 1

    tiny_step(True, False)
    for f in folds:
        for k in range(2, stages):
            f.add(k, 0)
    for f in tails:
        f.add(0, 0)
    for n in range(tensor)[::-1]:
        for f in tails:
            f.add(1, n)
        if n < tensor - 1:
            for f in tails:
                for k in range(2, stages):
                    f.add(k, n + 1)
                f.line_first(n + 1)
        tiny_step(False, True)
        tiny_step(True, False)
    for f in folds:
        f.result()
    for f in tails:
        for k in range(2, stages):
            f.add(k, 0)
    for n in range(1, tensor)[::-1]:
        for f in tails:
            f.line_next(n)
        tiny_step(False, True)
        tiny_step(True, False)
    while tiny_at[0] < (fsdp * tensor).bit_length() - 1:
        tiny_step(False, True)
        tiny_step(True, False)

    @pl.when(p.on)
    def _():
        s.arrive(twin_in.at[p.j], twin + p.j)
        dx[...] += own[...] + twin_in[p.j].astype(F32)
        if p.half > 1:
            s.arrive(mate_in.at[p.j], mate + p.j)
            dx[...] += mate_in[p.j].astype(F32)

    @pl.when(p.off)
    def _():
        s.arrive(fin_in, fin)
        s.arrive(mate_in.at[0], own_slot)
        dx[...] = fin_in[...].astype(F32) + mate_in[0].astype(F32)
    s.arrive(swapped, swap_slot, p.off)
    for f in tails:
        f.result()
    for n in range(tensor):
        t = p.near(n)
        if n < 2:
            s.left(dxb.at[0], twin + t, p.off)
        if n > 0:
            if p.half > 1:
                s.left(dxb.at[0], mate + t, p.on & ((n == 1) | p.is_end))
                if n > 1:
                    s.left(dxb.at[0], fin_send + t, p.on & p.is_edge)
            else:
                s.left(dxb.at[0], fin_send + t, p.on)
    for f in folds + tails:
        f.finish()
    s.finish()


def last_part(fsdp, tensor, x, w0, kv, q, do, g_o, g, e, resid, low, r, g_bup, g_vecs):
    groups, heads, _, rows = e.shape
    model, width = w0.shape[2:]
    shard = model // fsdp
    bits = fsdp.bit_length() - 1
    vm = lambda d, *shape: pltpu.VMEM(shape, d)
    slots = 4 * ((fsdp - 1) * tensor + 2 * tensor) + 3 * tensor + 16
    scratch = [vm(BF16, 6, fsdp >> (k + 1), tensor, shard, width) for k in range(bits)]
    scratch += [vm(BF16, 6, 2, tensor, shard, width), vm(BF16, 4, tensor, fsdp // 2, shard, width), vm(BF16, 2, rows, model),
                vm(BF16, 2, tensor, model, width), vm(BF16, 2, rows, width), vm(BF16, tensor, rows, width), vm(BF16, tensor, rows, width),
                vm(F32, tensor, heads, 128, rows), vm(F32, tensor, model, width), vm(BF16, 2, heads, rows, rows),
                vm(BF16, 2, tensor, model, width), vm(BF16, rows, width), vm(BF16, 2, rows, model), vm(F32, rows, model), vm(BF16, tensor, rows, model),
                vm(BF16, tensor, rows, model), vm(BF16, rows, model), vm(F32, (fsdp * tensor).bit_length() - 1, 8 + 2 * tensor, model),
                pltpu.SemaphoreType.DMA((slots,)), pltpu.SemaphoreType.DMA((slots,)), pltpu.SemaphoreType.DMA((16 + fsdp,))]
    return pl.pallas_call(
        functools.partial(last_kernel, fsdp, tensor),
        in_specs=[ANY] * 10 + [VM] * 3, out_specs=[VM] * 3 + [ANY],
        out_shape=[jax.ShapeDtypeStruct(s, d) for s, d in [
            ((6, shard, width), F32), ((rows, model), F32), ((8 + 2 * tensor, model), F32), ((rows, model), BF16)]],
        scratch_shapes=scratch,
        compiler_params=pltpu.CompilerParams(collective_id=1, has_side_effects=True, vmem_limit_bytes=65400 * 1024),
    )(x, w0, kv, q, do, g_o, g, e, resid, low, r, g_bup, g_vecs)


def final_kernel(fsdp, tensor, shards, dx, tiny, out, swapped,
                 output, grad_tokens, g_query, g_key, g_value, g_out, g_up, g_down, b_query, b_value, b_up, *vectors):
    p = Place(fsdp, tensor)
    columns, width = g_query.shape[1], shards.shape[2]
    shard = shards.shape[1]
    grad_tokens[...] = dx[...]

    @pl.when(p.on)
    def _():
        output[...] = out[...]

    @pl.when(p.off)
    def _():
        output[...] = swapped[...].astype(F32)
    heads = [(h, slice(h * HEAD, h * HEAD + HEAD), slice(2 * h * HEAD, 2 * h * HEAD + 2 * HEAD)) for h in range(columns // HEAD)]
    out_rows = []
    for h, cols, both in heads:
        keys, query = shards[0, :, both], shards[1, :, both]
        g_key[:, cols], g_value[:, cols] = keys[:, :HEAD], keys[:, HEAD:]
        g_query[:, cols] = query[:, :HEAD]
        out_rows.append(query[:, HEAD:])
    g_out[...] = jnp.concatenate(out_rows, 1).T
    for k in range(2):
        cols = slice(k * width, k * width + width)
        g_up[:, cols] = shards[2 + 2 * k]
        g_down[:, cols] = shards[3 + 2 * k]

    def take(row, ones):
        return lax.dot_general(row, ones, ((NT[:1], NT[1:]), ((), ())), precision=lax.Precision.HIGHEST, preferred_element_type=F32)

    few, many = columns // fsdp, 2 * width // fsdp
    both = tiny[pl.ds(8 + tensor + p.j, 1), :]
    b_query[...] = take(both[:, width:], spread(head_lanes(False), few, p.i, 0, width))
    b_value[...] = take(both[:, :width], spread(head_lanes(True), few, p.i, 0, width))
    b_up[...] = take(tiny[pl.ds(8 + p.j, 1), :], spread(lambda lane: lane, many, p.i, 0, 2 * width))
    rows = take(tiny[:8], spread(lambda lane: lane, shard, p.i, 0, shard * fsdp))
    for k, vector in enumerate(vectors):
        vector[...] = rows[k:k + 1]


def final_part(fsdp, tensor, shards, dx, tiny, out, swapped):
    _, shard, width = shards.shape
    rows, model = dx.shape
    columns = width // 2
    flat, square = (rows, model), (shard, columns)
    results = pl.pallas_call(
        functools.partial(final_kernel, fsdp, tensor),
        in_specs=[VM] * 5, out_specs=[VM] * 17,
        out_shape=[jax.ShapeDtypeStruct(s, F32) for s in [
            flat, flat, square, square, square, (columns, shard), (shard, 2 * width), (shard, 2 * width),
            (1, columns // fsdp), (1, columns // fsdp), (1, 2 * width // fsdp)] + [(1, shard)] * 6],
        compiler_params=pltpu.CompilerParams(vmem_limit_bytes=VMEM_LIMIT),
    )(shards, dx, tiny, out, swapped)
    return (*results[:7], results[7].T, *[r.reshape(-1) for r in results[8:]])


def normalize(values, gain, shift):
    average = jnp.mean(values, -1, keepdims=True)
    centered = values - average
    inverse = lax.rsqrt(jnp.mean(centered * centered, -1, keepdims=True) + EPSILON)
    return centered * inverse * gain + shift


def exact_gelu(values):
    return jax.nn.gelu(values, approximate=False)


def outer_sum(left, right):
    return dot(left, right, TN)


def times_transposed(left, right):
    return dot(left, right, NT)


def plain(
    tokens,
    cotangent,
    w_query,
    w_key,
    w_value,
    w_out,
    w_up,
    w_down,
    b_query,
    b_value,
    b_up,
    b_out,
    b_down,
    gain_attn,
    shift_attn,
    gain_ffn,
    shift_ffn,
):
    gathered = (
        lax.all_gather(w_query, "fsdp", axis=0, tiled=True),
        lax.all_gather(w_key, "fsdp", axis=0, tiled=True),
        lax.all_gather(w_value, "fsdp", axis=0, tiled=True),
        lax.all_gather(w_out, "fsdp", axis=1, tiled=True),
        lax.all_gather(w_up, "fsdp", axis=0, tiled=True),
        lax.all_gather(w_down, "fsdp", axis=1, tiled=True),
        lax.all_gather(b_query, "fsdp", axis=0, tiled=True),
        lax.all_gather(b_value, "fsdp", axis=0, tiled=True),
        lax.all_gather(b_up, "fsdp", axis=0, tiled=True),
        lax.all_gather(b_out, "fsdp", axis=0, tiled=True),
        lax.all_gather(b_down, "fsdp", axis=0, tiled=True),
        lax.all_gather(gain_attn, "fsdp", axis=0, tiled=True),
        lax.all_gather(shift_attn, "fsdp", axis=0, tiled=True),
        lax.all_gather(gain_ffn, "fsdp", axis=0, tiled=True),
        lax.all_gather(shift_ffn, "fsdp", axis=0, tiled=True),
    )
    (
        query_weight,
        key_weight,
        value_weight,
        out_weight,
        up_weight,
        down_weight,
        query_bias,
        value_bias,
        up_bias,
        out_bias,
        down_bias,
        attn_gain,
        attn_shift,
        ffn_gain,
        ffn_shift,
    ) = gathered
    own_rows = tokens.shape[0]
    seq_len = own_rows * lax.axis_size("tensor")
    heads = query_weight.shape[1] // HEAD
    span = min(512, seq_len)
    blocks = seq_len // span
    scale = HEAD ** (-0.5)
    full_tokens = lax.all_gather(tokens, "tensor", axis=0, tiled=True)
    query = (
        jnp.dot(full_tokens, query_weight, preferred_element_type=jnp.float32)
        + query_bias.astype(jnp.float32)
    ).astype(jnp.bfloat16)
    keys = jnp.dot(full_tokens, key_weight, preferred_element_type=jnp.float32).astype(jnp.bfloat16)
    values = (
        jnp.dot(full_tokens, value_weight, preferred_element_type=jnp.float32)
        + value_bias.astype(jnp.float32)
    ).astype(jnp.bfloat16)
    query_blocks = query.reshape(blocks, span, heads, HEAD)
    key_heads = keys.reshape(seq_len, heads, HEAD)
    value_heads = values.reshape(seq_len, heads, HEAD)

    def scores_of(piece):
        return (
            jnp.einsum("qhd,khd->hqk", piece, key_heads, preferred_element_type=jnp.float32) * scale
        )

    def forward_block(piece):
        scores = scores_of(piece)
        largest = jnp.max(scores, -1, keepdims=True)
        exponent = jnp.exp(scores - largest)
        total = jnp.sum(exponent, -1, keepdims=True)
        soft_low = (exponent / total).astype(jnp.bfloat16)
        result = jnp.einsum(
            "hqk,khd->qhd", soft_low, value_heads, preferred_element_type=jnp.float32
        )
        return (result.astype(jnp.bfloat16), largest, total)

    attended, largest_all, total_all = lax.map(forward_block, query_blocks)
    attended = attended.reshape(seq_len, heads * HEAD)
    attn_part = lax.psum_scatter(
        jnp.dot(attended, out_weight, preferred_element_type=jnp.float32).astype(jnp.bfloat16),
        "tensor",
        scatter_dimension=0,
        tiled=True,
    ).astype(jnp.float32)
    resid_attn = tokens.astype(jnp.float32) + (attn_part + out_bias.astype(jnp.float32))
    hidden, attn_norm_back = jax.vjp(
        normalize, resid_attn, attn_gain.astype(jnp.float32), attn_shift.astype(jnp.float32)
    )
    full_hidden = lax.all_gather(hidden.astype(jnp.bfloat16), "tensor", axis=0, tiled=True)
    pre_act = jnp.dot(full_hidden, up_weight, preferred_element_type=jnp.float32) + up_bias.astype(
        jnp.float32
    )
    activ, gelu_back = jax.vjp(exact_gelu, pre_act)
    activ_low = activ.astype(jnp.bfloat16)
    ffn_part = lax.psum_scatter(
        jnp.dot(activ_low, down_weight, preferred_element_type=jnp.float32).astype(jnp.bfloat16),
        "tensor",
        scatter_dimension=0,
        tiled=True,
    ).astype(jnp.float32)
    resid_ffn = hidden + (ffn_part + down_bias.astype(jnp.float32))
    output, ffn_norm_back = jax.vjp(
        normalize, resid_ffn, ffn_gain.astype(jnp.float32), ffn_shift.astype(jnp.float32)
    )
    matrices = (
        lax.all_gather(w_query, "fsdp", axis=0, tiled=True),
        lax.all_gather(w_key, "fsdp", axis=0, tiled=True),
        lax.all_gather(w_value, "fsdp", axis=0, tiled=True),
        lax.all_gather(w_out, "fsdp", axis=1, tiled=True),
        lax.all_gather(w_up, "fsdp", axis=0, tiled=True),
        lax.all_gather(w_down, "fsdp", axis=1, tiled=True),
    )
    back_query, back_key, back_value, back_out, back_up, back_down = matrices
    grad_resid_ffn, grad_gain_ffn, grad_shift_ffn = ffn_norm_back(cotangent.astype(jnp.float32))
    grad_ffn_full = lax.all_gather(
        grad_resid_ffn.astype(jnp.bfloat16), "tensor", axis=0, tiled=True
    )
    grad_down_bias = jnp.sum(grad_ffn_full, 0, dtype=jnp.float32)
    grad_down_weight = outer_sum(activ_low, grad_ffn_full)
    grad_activ = times_transposed(grad_ffn_full, back_down)
    grad_pre = gelu_back(grad_activ)[0].astype(jnp.bfloat16)
    grad_up_bias = jnp.sum(grad_pre, 0, dtype=jnp.float32)
    grad_up_weight = outer_sum(full_hidden, grad_pre)
    grad_hidden = grad_resid_ffn + lax.psum_scatter(
        times_transposed(grad_pre, back_up).astype(jnp.bfloat16),
        "tensor",
        scatter_dimension=0,
        tiled=True,
    ).astype(jnp.float32)
    grad_resid_attn, grad_gain_attn, grad_shift_attn = attn_norm_back(grad_hidden)
    grad_attn_full = lax.all_gather(
        grad_resid_attn.astype(jnp.bfloat16), "tensor", axis=0, tiled=True
    )
    grad_out_bias = jnp.sum(grad_attn_full, 0, dtype=jnp.float32)
    grad_out_weight = outer_sum(attended, grad_attn_full)
    grad_attended = times_transposed(grad_attn_full, back_out).astype(jnp.bfloat16)
    grad_blocks = grad_attended.reshape(blocks, span, heads, HEAD)

    def backward_block(carry, item):
        piece, grad_piece, largest, total = item
        soft = jnp.exp(scores_of(piece) - largest) / total
        soft_low = soft.astype(jnp.bfloat16)
        grad_soft = jnp.einsum(
            "qhd,khd->hqk", grad_piece, value_heads, preferred_element_type=jnp.float32
        )
        inner = jnp.sum(soft * grad_soft, -1, keepdims=True)
        grad_scores = (soft * (grad_soft - inner)).astype(jnp.bfloat16)
        grad_query_block = (
            jnp.einsum("hqk,khd->qhd", grad_scores, key_heads, preferred_element_type=jnp.float32)
            * scale
        )
        grad_key_sum = (
            carry[0]
            + jnp.einsum("hqk,qhd->khd", grad_scores, piece, preferred_element_type=jnp.float32)
            * scale
        )
        grad_value_sum = carry[1] + jnp.einsum(
            "hqk,qhd->khd", soft_low, grad_piece, preferred_element_type=jnp.float32
        )
        return ((grad_key_sum, grad_value_sum), grad_query_block.astype(jnp.bfloat16))

    zeros = jnp.zeros((seq_len, heads, HEAD), jnp.float32)
    (grad_key_sum, grad_value_sum), grad_query = lax.scan(
        backward_block, (zeros, zeros), (query_blocks, grad_blocks, largest_all, total_all)
    )
    grad_query = grad_query.reshape(seq_len, heads * HEAD)
    grad_keys = grad_key_sum.reshape(seq_len, heads * HEAD).astype(jnp.bfloat16)
    grad_values = grad_value_sum.reshape(seq_len, heads * HEAD).astype(jnp.bfloat16)
    grad_query_bias = jnp.sum(grad_query, 0, dtype=jnp.float32)
    grad_value_bias = jnp.sum(grad_values, 0, dtype=jnp.float32)
    grad_query_weight = outer_sum(full_tokens, grad_query)
    grad_key_weight = outer_sum(full_tokens, grad_keys)
    grad_value_weight = outer_sum(full_tokens, grad_values)
    token_terms = (
        times_transposed(grad_query, back_query)
        + times_transposed(grad_keys, back_key)
        + times_transposed(grad_values, back_value)
    )
    norm_terms = jnp.tile(
        jnp.stack([grad_gain_attn, grad_shift_attn, grad_gain_ffn, grad_shift_ffn]),
        (lax.axis_size("tensor"), 1),
    )
    token_part, norm_sums = (
        lax.psum_scatter(
            token_terms.astype(jnp.bfloat16), "tensor", scatter_dimension=0, tiled=True
        ).astype(jnp.float32),
        lax.psum_scatter(
            norm_terms.astype(jnp.bfloat16), "tensor", scatter_dimension=0, tiled=True
        ).astype(jnp.float32),
    )
    grad_tokens = grad_resid_attn + token_part
    shards = (
        lax.psum_scatter(grad_query_weight, "fsdp", scatter_dimension=0, tiled=True),
        lax.psum_scatter(grad_key_weight, "fsdp", scatter_dimension=0, tiled=True),
        lax.psum_scatter(grad_value_weight, "fsdp", scatter_dimension=0, tiled=True),
        lax.psum_scatter(grad_out_weight, "fsdp", scatter_dimension=1, tiled=True),
        lax.psum_scatter(grad_up_weight, "fsdp", scatter_dimension=0, tiled=True),
        lax.psum_scatter(grad_down_weight, "fsdp", scatter_dimension=1, tiled=True),
        lax.psum_scatter(grad_query_bias, "fsdp", scatter_dimension=0, tiled=True),
        lax.psum_scatter(grad_value_bias, "fsdp", scatter_dimension=0, tiled=True),
        lax.psum_scatter(grad_up_bias, "fsdp", scatter_dimension=0, tiled=True),
        lax.psum_scatter(grad_out_bias, "fsdp", scatter_dimension=0, tiled=True),
        lax.psum_scatter(grad_down_bias, "fsdp", scatter_dimension=0, tiled=True),
        lax.psum_scatter(norm_sums[0], "fsdp", scatter_dimension=0, tiled=True),
        lax.psum_scatter(norm_sums[1], "fsdp", scatter_dimension=0, tiled=True),
        lax.psum_scatter(norm_sums[2], "fsdp", scatter_dimension=0, tiled=True),
        lax.psum_scatter(norm_sums[3], "fsdp", scatter_dimension=0, tiled=True),
    )
    return (
        output,
        grad_tokens,
        shards[0],
        shards[1],
        shards[2],
        shards[3],
        shards[4],
        shards[5],
        shards[6],
        shards[7],
        shards[8],
        shards[9],
        shards[10],
        shards[11],
        shards[12],
        shards[13],
        shards[14],
    )


def fits(tokens, w_query, w_up):
    fsdp, tensor = lax.axis_size("fsdp"), lax.axis_size("tensor")
    shard, columns = w_query.shape
    return (tensor == 4 and fsdp >= 4 and fsdp & (fsdp - 1) == 0 and shard % 16 == 0 and 4 * columns == tokens.shape[1] and columns >= 3 * HEAD and columns % HEAD == 0
            and w_up.shape[1] == 4 * columns and tokens.shape[0] % 128 == 0)


def layer(tokens, cotangent, w_query, w_key, w_value, w_out, w_up, w_down, b_query, b_value, b_up, b_out, b_down,
          gain_attn, shift_attn, gain_ffn, shift_ffn):
    if not fits(tokens, w_query, w_up):
        return plain(tokens, cotangent, w_query, w_key, w_value, w_out, w_up, w_down, b_query, b_value, b_up, b_out, b_down,
                     gain_attn, shift_attn, gain_ffn, shift_ffn)
    fsdp, tensor = lax.axis_size("fsdp"), lax.axis_size("tensor")
    pieces = (b_query, b_value, b_up, b_out, b_down, gain_attn, shift_attn, gain_ffn, shift_ffn)
    total, at, vectors = sum(piece.size for piece in pieces), 0, 0.0
    for piece in pieces:
        vectors += jnp.pad(piece.reshape(1, -1), ((0, 0), (at, total - at - piece.size)))
        at += piece.size
    w0, w1, x, x_own, cot, kv, q, att, exps, inv, smalls = first_part(
        fsdp, tensor, w_query, w_key, w_value, w_out, w_up, w_down.T, vectors, tokens, cotangent)
    out, low, resid, r, do, g_o, g, g_bup, g_vecs = middle_part(x_own, cot, att, w0, w1, smalls, inv)
    shards, grad_tokens, tiny, swapped = last_part(fsdp, tensor, x, w0, kv, q, do, g_o, g, exps, resid, low, r, g_bup, g_vecs)
    return final_part(fsdp, tensor, shards, grad_tokens, tiny, out, swapped)


def solution(mesh):
    return jax.shard_map(
        layer,
        mesh=mesh,
        in_specs=(
            P(("fsdp", "tensor"), None),
            P(("fsdp", "tensor"), None),
            P("fsdp", "tensor"),
            P("fsdp", "tensor"),
            P("fsdp", "tensor"),
            P("tensor", "fsdp"),
            P("fsdp", "tensor"),
            P("tensor", "fsdp"),
            P(("tensor", "fsdp")),
            P(("tensor", "fsdp")),
            P(("tensor", "fsdp")),
            P("fsdp"),
            P("fsdp"),
            P("fsdp"),
            P("fsdp"),
            P("fsdp"),
            P("fsdp"),
        ),
        out_specs=(
            P(("fsdp", "tensor"), None),
            P(("fsdp", "tensor"), None),
            P("fsdp", "tensor"),
            P("fsdp", "tensor"),
            P("fsdp", "tensor"),
            P("tensor", "fsdp"),
            P("fsdp", "tensor"),
            P("tensor", "fsdp"),
            P(("tensor", "fsdp")),
            P(("tensor", "fsdp")),
            P(("tensor", "fsdp")),
            P("fsdp"),
            P("fsdp"),
            P("fsdp"),
            P("fsdp"),
            P("fsdp"),
            P("fsdp"),
        ),
        check_vma=False,
    )
```

```python
import functools

import jax
import jax.numpy as jnp
import numpy as np
from jax import lax
from jax.experimental import pallas as pl
from jax.experimental.pallas import tpu as pltpu
from jax.sharding import PartitionSpec as P

F32, BF16 = jnp.float32, jnp.bfloat16
HEAD = 64
EPSILON = 1e-12
VMEM_LIMIT = 64000 * 1024


def dot(left, right, contract):
    return lax.dot_general(left, right, ((contract[:1], contract[1:]), ((), ())), preferred_element_type=F32)

NN, NT, TN = (1, 0), (1, 1), (0, 0)


def lanes_from(shape, low):
    return lax.broadcasted_iota(jnp.int32, shape, len(shape) - 1) % (2 * HEAD) >= HEAD if not low else \
        lax.broadcasted_iota(jnp.int32, shape, len(shape) - 1) % (2 * HEAD) < HEAD


def project_keys(x, w, bias):
    return (dot(x, w, NN) + bias).astype(BF16)


def project_query(x, w, bias):
    out = dot(x, w, NN) + bias
    return jnp.where(lanes_from(out.shape, True), out.astype(BF16) * BF16(HEAD ** -0.5), BF16(0))


def norm_forward(z):
    mean = jnp.mean(z, -1, keepdims=True)
    centered = z - mean
    inv = lax.rsqrt(jnp.mean(centered * centered, -1, keepdims=True) + EPSILON)
    return centered * inv, inv


def norm_backward(n, inv, dn):
    return inv * (dn - jnp.mean(dn, -1, keepdims=True) - n * jnp.mean(dn * n, -1, keepdims=True))


def colsum(x):
    return jnp.sum(x.astype(F32), axis=0, keepdims=True)


MESH = pl.DeviceIdType.MESH
ANY = pl.BlockSpec(memory_space=pl.ANY)
VM = pl.BlockSpec(memory_space=pltpu.VMEM)


def flip(index, bit):
    return index + bit - 2 * bit * lax.rem(index // bit, 2)


def flips(index, mask):
    bit = 1
    while bit <= mask:
        if mask & bit:
            index = flip(index, bit)
        bit *= 2
    return index


def span(bits):
    masks = [0]
    for bit in bits:
        masks += [m | bit for m in masks]
    return masks


def orders(fsdp):
    bits = [1 << k for k in range(fsdp.bit_length() - 1)]
    return bits[1:] + bits[:1], bits[:0:-1] + bits[:1]


class Place:
    def __init__(self, fsdp, tensor):
        self.fsdp, self.tensor = fsdp, tensor
        self.i, self.j = lax.axis_index("fsdp"), lax.axis_index("tensor")
        self.half = tensor // 2
        self.c = lax.rem(self.i, 2)
        self.h = self.j // self.half
        self.on = self.c == self.h
        self.off = self.c != self.h
        self.twin = flip(self.i, 1)
        self.swap = lax.rem(self.j + self.half, tensor)
        self.block = jnp.where(self.on, self.j, self.swap)
        self.edge = self.half - 1 + self.c
        self.end = self.c * (tensor - 1)
        self.mate = self.h * tensor + 1 - self.j
        self.is_edge = self.j == self.edge
        self.is_end = self.j == self.end

    def other(self, k):
        return (1 - self.c) * (self.half + k) + self.c * (self.half - 1 - k)

    def near(self, n):
        low = jnp.where(self.h == 0, self.j, self.tensor - 1 - self.j)
        if isinstance(n, int):
            place = low if n == 0 else 1 - low if n == 1 else n
        else:
            place = jnp.where(n == 0, low, jnp.where(n == 1, 1 - low, n))
        return jnp.where(self.h == 0, place, self.tensor - 1 - place)

    def barrier(self):
        self.greet()
        self.met()

    def met(self):
        pl.semaphore_wait(pltpu.get_barrier_semaphore(), self.tensor + self.fsdp.bit_length() - 1)

    def greet(self):
        sem = pltpu.get_barrier_semaphore()
        others = [(self.i, lax.rem(self.j + k, self.tensor)) for k in range(1, self.tensor)]
        bit = 1
        while bit < self.fsdp:
            others.append((flip(self.i, bit), self.j))
            bit *= 2
        others.append((self.twin, self.swap))
        for i, j in others:
            pl.semaphore_signal(sem, inc=1, device_id=(i, j), device_id_type=MESH)


class Sends:
    def __init__(self, place, send, recv):
        self.place, self.send, self.recv, self.n, self.started = place, send, recv, 0, []

    def slots(self, n):
        self.n += n
        return self.n - n

    def slot(self):
        return self.slots(1)

    def copy(self, src, dst, slot, i, j, back=None):
        return pltpu.make_async_remote_copy(src_ref=src, dst_ref=dst, send_sem=self.send.at[slot if back is None else back],
                                            recv_sem=self.recv.at[slot], device_id=(i, j), device_id_type=MESH)

    def start(self, src, dst, slot, i, j, when=None, back=None, note=True):
        copy = self.copy(src, dst, slot, i, j, back)
        copy.start() if when is None else pl.when(when)(copy.start)
        if note:
            self.started.append((copy, when))

    def arrive(self, dst, slot, when=None):
        copy = self.copy(dst, dst, slot, self.place.i, self.place.j)
        copy.wait_recv() if when is None else pl.when(when)(copy.wait_recv)

    def left(self, src, slot, when=None):
        copy = self.copy(src, src, slot, self.place.i, self.place.j)
        copy.wait_send() if when is None else pl.when(when)(copy.wait_send)

    def finish(self):
        for copy, when in self.started:
            copy.wait_send() if when is None else pl.when(when)(copy.wait_send)
        self.started = []


def transposed(value):
    return value.astype(F32).T.astype(value.dtype)


def spread(lanes, n, place, first, width):
    at = lanes(lax.broadcasted_iota(jnp.int32, (n, width), 1))
    return jnp.where(at == lax.broadcasted_iota(jnp.int32, (n, width), 0) + place * n, 1.0, 0.0)


def head_lanes(second):
    def lanes(lane):
        inside = lane % 128
        if second:
            return jnp.where(inside >= HEAD, lane // 128 * HEAD + inside - HEAD, -1)
        return jnp.where(inside < HEAD, lane // 128 * HEAD + inside, -1)
    return lanes


def pack_own(p, w_query, w_key, w_value, w_out, w_up, w_down, vectors, pack, small):
    shard, columns = w_query.shape
    width = 2 * columns
    out = transposed(w_out[...])
    for k, (first, second) in enumerate(((w_key[...], w_value[...]), (w_query[...], out))):
        for h in range(columns // HEAD):
            cols = slice(h * HEAD, h * HEAD + HEAD)
            pack[k, :, 2 * h * HEAD:2 * h * HEAD + 2 * HEAD] = jnp.concatenate([first[:, cols], second[:, cols]], 1)
    for k in range(2):
        cols = slice(k * width, k * width + width)
        pack[2 + 2 * k] = w_up[:, cols]
        pack[3 + 2 * k] = w_down[:, cols]
    few, many = columns // p.fsdp, 2 * width // p.fsdp
    take = lambda at, n: vectors[:, at:at + n].astype(BF16)
    put = lambda value, ones: dot(value, ones.astype(BF16), NN)
    small[0:1, width:] = put(take(0, few), spread(head_lanes(False), few, p.i, 0, width))
    small[0:1, :width] = put(take(few, few), spread(head_lanes(True), few, p.i, 0, width))
    small[1:2] = put(take(2 * few, many), spread(lambda lane: lane, many, p.i, 0, 2 * width))
    ones = spread(lambda lane: lane, shard, p.i, 0, shard * p.fsdp)
    for k in range(6):
        small[2 + k:3 + k] = put(take(2 * few + many + k * shard, shard), ones)


class Stream:
    def __init__(self, sends, array, lead, shard, order, own):
        self.s, self.p, self.a, self.lead, self.shard, self.order, self.own = sends, sends.place, array, lead, shard, order, own
        n = self.p.tensor
        self.z, self.back = sends.slots(n), sends.slots(1)
        self.hops = [{m: sends.slots(n) for m in span(order[:k])} for k in range(len(order))]

    def block(self, t, mask):
        rows = pl.ds(pl.multiple_of(flips(self.p.i, mask) * self.shard, self.shard), self.shard)
        return self.a.at[(*self.lead, t, rows)]

    def first_line(self):
        s, p = self.s, self.p
        there = self.block(p.j, 0)
        s.start(self.own, there, self.z + p.j, p.i, p.j + 1, p.j + 1 < p.tensor, note=False)
        s.start(self.own, there, self.z + p.j, p.i, p.j - 1, p.j > 0, self.back, note=False)

    def first_fan(self):
        self.fan(0, 0, self.p.j, self.own)

    def fan(self, mask, k, t, src=None):
        for n in range(k, len(self.order)):
            there = self.block(t, mask)
            self.s.start(there if src is None else src, there, self.hops[n][mask] + t, flip(self.p.i, self.order[n]), self.p.j, note=False)

    def line(self, n):
        s, p = self.s, self.p
        t = p.near(n)
        there = self.block(t, 0)
        s.arrive(there, self.z + t)
        ahead = p.j + jnp.where(t < p.j, 1, -1)
        s.start(there, there, self.z + t, p.i, ahead, (ahead >= 0) & (ahead < p.tensor), note=False)
        self.fan(0, 0, t)

    def finish(self):
        s, p = self.s, self.p
        here = self.block(p.j, 0)
        s.left(here, self.z + p.j, p.j + 1 < p.tensor)
        s.left(here, self.back, p.j > 0)
        for n in range(p.tensor):
            t = p.near(n)
            if n > 0:
                ahead = p.j + jnp.where(t < p.j, 1, -1)
                s.left(here, self.z + t, (ahead >= 0) & (ahead < p.tensor))
            for hops in self.hops:
                for slot in hops.values():
                    s.left(here, slot + t)

    def hop(self, k, n):
        t = self.p.near(n)
        for m in self.hops[k]:
            mask = m | self.order[k]
            self.s.arrive(self.block(t, mask), self.hops[k][m] + t)
            self.fan(mask, k + 1, t)


def attend_group(heads, g, x, own_rows, w_kv, w_qo, smalls, kv, q, att, inv, s_ref, exps, before, after):
    width = heads * 128
    kv[g] = project_keys(x[...], w_kv[g], smalls[g, 0:1, :width])
    q[g] = project_query(x[own_rows, :], w_qo[g], smalls[g, 0:1, width:])
    for h in range(heads):
        cols = slice(h * 128, h * 128 + 128)
        keys = kv[g, :, cols]
        s_ref[...] = dot(keys, q[g, :, cols], NT)
        top = jnp.max(s_ref[...], axis=0, keepdims=True)
        e = jnp.exp(s_ref[...] - top)
        scale = 1.0 / jnp.sum(e, axis=0, keepdims=True)
        before(h)
        exps[h] = e.astype(BF16)
        out = dot(keys, exps[h], TN) * scale
        out = jnp.where(lax.broadcasted_iota(jnp.int32, out.shape, 0) >= HEAD, out, 0.0)
        att[g, :, cols] = out.T.astype(BF16)
        inv[g, h:h + 1] = scale
        after(h)


def first_kernel(fsdp, tensor, w_query, w_key, w_value, w_out, w_up, w_down, vectors, tok, cot, w0_out, w1, x_out, own_out, cot_out, kv_out, q_out, att_out, exp_out,
                 inv, smalls, pack, small, w0, sm, x, kv, q, att, s_ref, exps, send, recv, local):
    p = Place(fsdp, tensor)
    s = Sends(p, send, recv)
    p.greet()
    pack_own(p, w_query, w_key, w_value, w_out, w_up, w_down, vectors, pack, small)
    rows, model = tok.shape
    shard = pack.shape[1]
    heads = exps.shape[0]
    first, second = orders(fsdp)
    kvw = Stream(s, w0, (0,), shard, first, pack.at[0])
    qow = Stream(s, w0, (1,), shard, second, pack.at[1])
    tiny = Stream(s, sm, (), small.shape[0], first, small)
    upper = Stream(s, w1, (pl.ds(0, 2),), shard, first, pack.at[pl.ds(2, 2)])
    lower = Stream(s, w1, (pl.ds(2, 2),), shard, second, pack.at[pl.ds(4, 2)])
    now, later = (kvw, qow, tiny), (upper, lower)
    pieces = 4 if rows % 64 == 0 else 1
    part = rows // pieces
    xin, xtwin, cslot = s.slots(tensor * pieces), s.slots(tensor * pieces), s.slots(1)
    x_at = lambda t: x.at[pl.ds(pl.multiple_of(t * rows, rows), rows)]

    def piece(t, u):
        return x.at[pl.ds(pl.multiple_of(t * rows + u * part, part), part)]

    def send_rows(t, u, i, j, when, twin=False, src=None):
        slot = t * pieces + u
        there = piece(t, u)
        s.start(there if src is None else src.at[pl.ds(u * part, part)], there, xin + slot, i, j, when, xtwin + slot if twin else None)

    def pass_rows(u, n, when, forward):
        t = p.near(n)
        s.arrive(piece(t, u), xin + t * pieces + u, when)
        if forward:
            send_rows(t, u, p.i, p.end, when)
        send_rows(t, u, p.twin, p.j, when, True)

    def edge_rows(u):
        for n in [*range(2, tensor), 1]:
            pass_rows(u, n, p.on & p.is_edge, p.half > 1 and n > 1)

    def end_rows(u):
        for n in range(1, tensor):
            pass_rows(u, n, p.on & jnp.logical_not(p.is_edge), False)
    locals_ = []

    def keep(src, dst, when=None):
        copy = pltpu.make_async_copy(src, dst, local.at[len(locals_)])
        copy.start() if when is None else pl.when(when)(copy.start)
        locals_.append((copy, when))
        return len(locals_) - 1

    def kept(k):
        copy, when = locals_[k]
        copy.wait() if when is None else pl.when(when)(copy.wait)
        locals_[k] = None

    mine = pl.ds(pl.multiple_of(p.i * shard, shard), shard)
    own = [keep(pack.at[k], w0.at[k, p.j, mine]) for k in range(2)]
    own += [keep(pack.at[2 + k], w1.at[k, p.j, mine]) for k in range(4)]
    own += [keep(small, sm.at[p.j, pl.ds(pl.multiple_of(p.i * small.shape[0], small.shape[0]), small.shape[0])])]
    own += [keep(tok, x_at(p.j), p.on), keep(cot, cot_out, p.on)]
    p.met()
    for g in now:
        g.first_line()
    for g in now:
        g.first_fan()
    for u in range(pieces):
        send_rows(p.j, u, p.i, p.edge, p.off, src=tok)
        if p.half > 1:
            send_rows(p.j, u, p.i, p.mate, p.on, src=tok)
        send_rows(p.j, u, p.twin, p.j, p.on, True, tok)
    for g in later:
        g.first_fan()
    stages = len(first)
    for step in range(1, tensor + stages - 1):
        if step < tensor:
            for g in now:
                g.line(step)
        for k in range(stages - 1):
            if 0 <= step - 1 - k < tensor:
                for g in now:
                    g.hop(k, step - 1 - k)
        if step - 1 < pieces:
            edge_rows(step - 1)
    for u in range(tensor + stages - 2, pieces):
        edge_rows(u)
    for u in range(pieces):
        end_rows(u)
    for g in later:
        g.first_line()
    for k in range(stages - 1):
        for g in later:
            g.hop(k, 0)
    s.start(cot, cot_out, cslot, p.twin, p.swap, p.off)
    for n in range(tensor):
        for g in now:
            g.hop(stages - 1, n)
    for t in range(tensor):
        for u in range(pieces):
            s.arrive(piece(t, u), xin + t * pieces + u, p.off)
    for k in own[:8]:
        kept(k)
    for t in range(tensor):
        total = sm[t, :small.shape[0], :]
        for i in range(1, fsdp):
            total += sm[t, i * small.shape[0]:(i + 1) * small.shape[0], :]
        smalls[t] = total
    keep(x_at(p.block), own_out)
    for t in range(tensor):
        keep(x_at(t), x_out.at[pl.ds(t * rows, rows)])
    for k in range(2):
        keep(w0.at[k], w0_out.at[k])
    fixed = len(locals_)
    sem = lambda k: local.at[fixed + k]

    def group(g, carry):
        def exp_copy(h, g):
            return pltpu.make_async_copy(exps.at[h], exp_out.at[g, h], sem(h))

        def before(h):
            pl.when(g > 0)(lambda: exp_copy(h, g - 1).wait())

        def after(h):
            exp_copy(h, g).start()
            point = {0: 0, heads // 2: 1, heads - 1: 2}.get(h)
            if point == 0:
                @pl.when(g >= 2)
                def _():
                    for st in later:
                        for k in range(1, stages - 1):
                            st.hop(k, g - 1)
            if point == 1:
                @pl.when(g >= 1)
                def _():
                    for st in later:
                        st.hop(0, g)
            if point == 2:
                @pl.when(g < tensor - 1)
                def _():
                    for st in later:
                        st.line(g + 1)

        attend_group(heads, g, x, pl.ds(pl.multiple_of(p.block * rows, rows), rows), w0.at[0], w0.at[1], smalls, kv, q, att, inv,
                     s_ref, exps, before, after)
        for k, (src, dst) in enumerate(((kv, kv_out), (q, q_out), (att, att_out))):
            pltpu.make_async_copy(src.at[g], dst.at[g], sem(heads + k * tensor + g)).start()
        return carry

    lax.fori_loop(0, tensor, group, 0)
    for k in range(1, stages - 1):
        for st in later:
            st.hop(k, tensor - 1)
    for n in range(tensor):
        for st in later:
            st.hop(stages - 1, n)
    for h in range(heads):
        pltpu.make_async_copy(exps.at[h], exp_out.at[0, h], sem(h)).wait()
    for k, (src, dst) in enumerate(((kv, kv_out), (q, q_out), (att, att_out))):
        for g in range(tensor):
            pltpu.make_async_copy(src.at[g], dst.at[g], sem(heads + k * tensor + g)).wait()
    s.arrive(cot_out, cslot, p.off)
    for k in range(len(locals_)):
        if locals_[k] is not None:
            kept(k)
    s.finish()
    for st in now + later:
        st.finish()


def first_part(fsdp, tensor, w_query, w_key, w_value, w_out, w_up, w_down, vectors, tok, cot):
    shard, width = w_query.shape[0], 2 * w_query.shape[1]
    rows, model = tok.shape
    heads, keys = width // 128, tensor * rows
    slots = 5 * (tensor + 1 + (fsdp - 1) * tensor) + 8 * tensor + 1
    return pl.pallas_call(
        functools.partial(first_kernel, fsdp, tensor),
        in_specs=[VM] * 9, out_specs=[ANY] * 9 + [VM] * 2,
        out_shape=[jax.ShapeDtypeStruct(s, d) for s, d in [
            ((2, tensor, model, width), BF16), ((4, tensor, model, width), BF16), ((keys, model), BF16), ((rows, model), BF16),
            ((rows, model), BF16), ((tensor, keys, width), BF16), ((tensor, rows, width), BF16), ((tensor, rows, width), BF16),
            ((tensor, heads, keys, rows), BF16), ((tensor, 8, rows), F32), ((tensor, 8, model), F32)]],
        scratch_shapes=[pltpu.VMEM(s, d) for s, d in [
            ((6, shard, width), BF16), ((8, model), F32),
            ((2, tensor, model, width), BF16), ((tensor, fsdp * 8, model), F32), ((keys, model), BF16),
            ((tensor, keys, width), BF16), ((tensor, rows, width), BF16), ((tensor, rows, width), BF16), ((keys, rows), F32),
            ((heads, keys, rows), BF16)]] + [pltpu.SemaphoreType.DMA((slots,)), pltpu.SemaphoreType.DMA((slots,)),
                                             pltpu.SemaphoreType.DMA((16 + 5 * tensor + heads,))],
        compiler_params=pltpu.CompilerParams(collective_id=0, has_side_effects=True, vmem_limit_bytes=VMEM_LIMIT),
    )(w_query, w_key, w_value, w_out, w_up, w_down, vectors, tok, cot)


class Fold:
    def __init__(self, sends, give, keep, lead, halves, inbox, order, out):
        self.s, self.p, self.give, self.keep, self.lead = sends, sends.place, give, keep, lead
        self.halves, self.inbox, self.order, self.out = halves, inbox, order[::-1], out
        n = self.p.tensor
        self.masks = [span(self.order[k + 1:]) for k in range(len(order))]
        self.slot = [[sends.slots(n) for _ in masks] for masks in self.masks]
        self.z = sends.slots(2 * n)

    def half(self, k, mask, t):
        return self.halves[k].at[(self.lead, self.masks[k].index(mask), t)]

    def first(self, n):
        t, bit = self.p.near(n), self.order[0]
        for k, m in enumerate(self.masks[0]):
            self.s.start(self.give(t, m | bit), self.half(0, m, t), self.slot[0][k] + t, flip(self.p.i, bit), self.p.j, note=False)

    def add(self, k, n):
        t = self.p.near(n)
        for at, m in enumerate(self.masks[k]):
            here = self.half(k, m, t)
            self.s.arrive(here, self.slot[k][at] + t)
            mine = self.keep(t, at) if k == 0 else self.half(k - 1, m, t)
            here[...] = (here[...].astype(F32) + mine[...].astype(F32)).astype(BF16)
        if k + 1 < len(self.order):
            bit = self.order[k + 1]
            for at, m in enumerate(self.masks[k + 1]):
                self.s.start(self.half(k, m | bit, t), self.half(k + 1, m, t), self.slot[k + 1][at] + t,
                             flip(self.p.i, bit), self.p.j, note=False)

    def total(self, t):
        return self.half(len(self.order) - 1, 0, t)

    def way(self, n):
        t = self.p.near(n)
        right = t > self.p.j
        there = self.p.j + jnp.where(right, 1, -1)
        before = self.p.j - jnp.where(right, 1, -1)
        side = jnp.where(right, 0, 1)
        has = (before >= 0) & (before < self.p.tensor)
        return t, there, has, self.inbox.at[(self.lead, side, t)], self.z + side * self.p.tensor + t

    def line_first(self, n):
        t, there, has, box, slot = self.way(n)
        self.s.start(self.total(t), box, slot, self.p.i, there, jnp.logical_not(has), note=False)

    def line_next(self, n):
        t, there, has, box, slot = self.way(n)
        total = self.total(t)

        @pl.when(has)
        def _():
            self.s.arrive(box, slot)
            box[...] = (box[...].astype(F32) + total[...].astype(F32)).astype(BF16)
            self.s.start(box, box, slot, self.p.i, there, note=False)

    def result(self):
        p = self.p
        self.out[...] = self.total(p.j)[...].astype(F32)
        for side, there in ((0, p.j > 0), (1, p.j < p.tensor - 1)):
            box = self.inbox.at[(self.lead, side, p.j)]

            @pl.when(there)
            def _(box=box, side=side):
                self.s.arrive(box, self.z + side * p.tensor + p.j)
                self.out[...] += box[...].astype(F32)

    def finish(self):
        here = self.half(0, self.masks[0][0], 0)
        for n in range(self.p.tensor):
            t = self.p.near(n)
            for slots in self.slot:
                for slot in slots:
                    self.s.left(here, slot + t)
            if n > 0:
                self.s.left(here, self.way(n)[4])

class Loads:
    def __init__(self, sems):
        self.sems, self.n = sems, 0

    def slots(self, n):
        self.n += n
        return self.n - n

    def load(self, src, dst):
        copy = pltpu.make_async_copy(src, dst, self.sems.at[self.slots(1)])
        copy.start()
        return copy

    def series(self, src, dst, n):
        first = self.slots(n)
        for k in range(n):
            pltpu.make_async_copy(src.at[k], dst.at[k], self.sems.at[first + k]).start()
        return lambda k: pltpu.make_async_copy(src.at[k], dst.at[k], self.sems.at[first + k]).wait()


def middle_kernel(groups, x_hbm, cot_hbm, att_hbm, w0_hbm, w1_hbm, smalls, inv,
                  out_ref, out_low, resid_ref, r_ref, datt_hbm, g_o_hbm, g_hbm, g_bup, g_vecs,
                  x_own, cot, att, w_qo, w1, datt, g_o, grads, act, slope, hid, n1_ref, acc, low, hl, sems):
    ld = Loads(sems)
    width = w_qo.shape[2]
    get_x = ld.load(x_hbm, x_own)
    get_att = ld.series(att_hbm, att, groups)
    get_qo = ld.series(w0_hbm.at[1], w_qo, groups)
    gets = [ld.series(w1_hbm.at[k], w1.at[k], groups) for k in range(4)]
    get_cot = ld.load(cot_hbm, cot)
    outs = [(grads.at[k], g_hbm.at[k], ld.slots(groups)) for k in range(4)]
    outs += [(datt, datt_hbm, ld.slots(groups)), (g_o, g_o_hbm, ld.slots(groups))]

    def put(k, g):
        src, dst, first = outs[k]
        return pltpu.make_async_copy(src.at[g], dst.at[g], sems.at[first + g])

    vec = lambda k: smalls[0, 2 + k:3 + k, :]
    get_x.wait()
    acc[...] = x_own[...].astype(F32) + vec(0)

    def branch(g, c):
        get_att(g)
        get_qo(g)
        acc[...] += dot(att[g], w_qo[g], NT)
        return c

    lax.fori_loop(0, groups, branch, 0)
    n1, inv1 = norm_forward(acc[...])
    n1_ref[...] = n1
    hidden = n1 * vec(2) + vec(3)
    hid[...] = hidden
    hl[...] = hidden.astype(BF16)
    acc[...] = hidden + vec(1)

    def forward(g, c):
        for get in gets:
            get(g)
        for k in range(2):
            pre = dot(hl[...], w1[2 * k, g], NN) + smalls[g, 1:2, k * width:(k + 1) * width]
            phi = 0.5 + 0.5 * lax.erf(pre * np.float32(0.5 ** 0.5))
            slope[g, k] = phi + pre * (jnp.exp(-0.5 * pre * pre) * np.float32((2 * np.pi) ** -0.5))
            act[g, k] = (pre * phi).astype(BF16)
            acc[...] += dot(act[g, k], w1[2 * k + 1, g], NT)
        return c

    lax.fori_loop(0, groups, forward, 0)
    n2, inv2 = norm_forward(acc[...])
    out = n2 * vec(4) + vec(5)
    out_ref[...] = out
    out_low[...] = out.astype(BF16)
    get_cot.wait()
    cott = cot[...].astype(F32)
    g_vecs[4:5] = colsum(cott * n2)
    g_vecs[5:6] = colsum(cott)
    resid = norm_backward(n2, inv2, cott * vec(4))
    acc[...] = resid
    low[...] = resid.astype(BF16)
    g_vecs[1:2] = colsum(low[...])

    def back(g, c):
        for k in range(2):
            grads[2 * k + 1, g] = dot(low[...], act[g, k], TN).astype(BF16)
            gp = (dot(low[...], w1[2 * k + 1, g], NN) * slope[g, k]).astype(BF16)
            act[g, k] = gp
            g_bup[g, :, k * width:(k + 1) * width] = colsum(gp)
            grads[2 * k, g] = dot(hl[...], gp, TN).astype(BF16)
            acc[...] += dot(act[g, k], w1[2 * k, g], NT)
        for k in range(4):
            put(k, g).start()
        return c

    lax.fori_loop(0, groups, back, 0)
    gh = acc[...]
    g_vecs[2:3] = colsum(gh * n1_ref[...])
    g_vecs[3:4] = colsum(gh)
    ga = norm_backward(n1_ref[...], inv1, gh * vec(2))
    resid_ref[...] = ga
    low[...] = ga.astype(BF16)
    g_vecs[0:1] = colsum(low[...])
    g_vecs[6:8] = jnp.zeros_like(g_vecs[6:8])

    def last(g, c):
        da = dot(low[...], w_qo[g], NN)
        da = jnp.where(lanes_from(da.shape, False), da, 0.0).T.astype(BF16).astype(F32)
        prod = da * att[g].T.astype(F32)
        for h in range(width // 128):
            cols = slice(h * 128, h * 128 + 128)
            scale = inv[g, h:h + 1]
            r_ref[g, h:h + 1] = jnp.sum(prod[cols], axis=0, keepdims=True) * scale
            datt[g, :, cols] = (da[cols] * scale).T.astype(BF16)
        g_o[g] = dot(low[...], att[g], TN).astype(BF16)
        put(4, g).start()
        put(5, g).start()
        return c

    lax.fori_loop(0, groups, last, 0)
    for k in range(6):
        for g in range(groups):
            put(k, g).wait()


def middle_part(x_own, cot, att, w0, w1, smalls, inv):
    _, groups, model, width = w0.shape
    rows = x_own.shape[0]
    wide, deep = ((groups, rows, width), BF16), ((groups, model, width), BF16)
    flat, low = ((rows, model), F32), ((rows, model), BF16)
    return pl.pallas_call(
        functools.partial(middle_kernel, groups),
        in_specs=[ANY] * 5 + [VM] * 2, out_specs=[VM] * 4 + [ANY, ANY, ANY, VM, VM],
        out_shape=[jax.ShapeDtypeStruct(s, d) for s, d in [
            flat, low, flat, ((groups, 8, rows), F32), wide, deep, ((4, groups, model, width), BF16), ((groups, 1, 2 * width), F32), ((8, model), F32)]],
        scratch_shapes=[pltpu.VMEM(s, d) for s, d in [
            low, low, wide, deep, ((4, groups, model, width), BF16), wide, deep, ((4, groups, model, width), BF16),
            ((groups, 2, rows, width), BF16), ((groups, 2, rows, width), F32), flat, flat, flat, low, low]]
        + [pltpu.SemaphoreType.DMA((12 * groups + 2,))],
        compiler_params=pltpu.CompilerParams(vmem_limit_bytes=VMEM_LIMIT),
    )(x_own, cot, att, w0, w1, smalls, inv)


def last_kernel(fsdp, tensor, x_hbm, w0_hbm, kv_hbm, q_hbm, do_hbm, g_o_hbm, g_hbm, e_hbm, resid_hbm, low_hbm, r, g_bup, g_vecs,
                shards, dx, tiny, swapped, *scratch):
    bits = fsdp.bit_length() - 1
    halves, scratch = scratch[:bits], scratch[bits:]
    (inbox, own_g, x, w0, kv, q, do, dqt, wacc, exps, gw, dkv, dxb, own, twin_in, mate_in, fin_in, tiny_in, send, recv, local) = scratch
    p = Place(fsdp, tensor)
    s, ld = Sends(p, send, recv), Loads(local)
    _, heads, rows, _ = exps.shape
    model, width = gw.shape[2:]
    shard = model // fsdp
    first, second = orders(fsdp)
    block_rows = lambda mask: pl.ds(pl.multiple_of(flips(p.i, mask) * shard, shard), shard)
    pair = lambda k: pl.ds(2 * k, 2)
    stay = [m for m in span(first[::-1][1:])]
    folds = []
    for k, order in enumerate((first, second)):
        masks = span(order[::-1][1:])
        folds.append(Fold(s, lambda t, m, k=k: g_hbm.at[pair(k), t, block_rows(m)],
                          lambda t, at, k=k, masks=masks: own_g.at[pair(k), t, stay.index(masks[at])],
                          pair(k + 1), halves, inbox, order, shards.at[pair(k + 1)]))
    tails = []
    for k, order in enumerate((first, second)):
        masks = span(order[::-1][1:])
        tails.append(Fold(s, lambda t, m, k=k: gw.at[pl.ds(k, 1), t, block_rows(m)],
                          lambda t, at, k=k, masks=masks: gw.at[pl.ds(k, 1), t, block_rows(masks[at])],
                          pl.ds(k, 1), halves, inbox, order, shards.at[pl.ds(k, 1)]))
    stages = bits

    steps = tensor * tensor
    step_sem, x_sem = ld.slots(4), ld.slots(2)

    def step_copies(step, slot):
        t, g = p.near(tensor - 1 - step // tensor), p.near(tensor - 1 - lax.rem(step, tensor))
        here = pl.ds(pl.multiple_of(t * rows, rows), rows)
        return (pltpu.make_async_copy(e_hbm.at[g, :, here], exps.at[slot], local.at[step_sem + slot]),
                pltpu.make_async_copy(kv_hbm.at[g, here], kv.at[slot], local.at[step_sem + 2 + slot]))

    def x_copy(it, slot):
        t = p.near(tensor - 1 - it)
        return pltpu.make_async_copy(x_hbm.at[pl.ds(pl.multiple_of(t * rows, rows), rows)], x.at[slot], local.at[x_sem + slot])

    for copy in step_copies(0, 0):
        copy.start()
    gets = [ld.load(do_hbm, do), ld.load(q_hbm, q)]
    x_copy(0, 0).start()
    gets.append(ld.load(w0_hbm.at[0], w0.at[0]))
    late = [ld.load(w0_hbm.at[1], w0.at[1])]
    own_gets = [ld.load(g_hbm.at[:, :, block_rows(m)], own_g.at[:, :, at]) for at, m in enumerate(stay)]
    late += [ld.load(g_o_hbm, gw.at[1]), ld.load(resid_hbm, own)]
    own_sem = ld.slots(1)
    tiny[:8] = g_vecs[...]
    for t in range(tensor):
        tiny[8 + t:9 + t] = g_bup[t]
    tiny[8 + tensor:] = jnp.zeros_like(tiny[8 + tensor:])
    p.greet()
    wacc[...] = jnp.zeros_like(wacc)
    dqt[...] = jnp.zeros_like(dqt)
    p.met()
    for n in range(tensor)[::-1]:
        for f in folds:
            f.first(n)
    swap_slot = s.slots(1)
    s.start(low_hbm, swapped, swap_slot, p.twin, p.swap, p.off)
    twin, mate, fin = s.slots(tensor), s.slots(tensor), s.slots(1)
    fin_send, own_slot = s.slots(tensor), s.slots(1)
    tiny_slots = s.slots((fsdp * tensor).bit_length() - 1)
    for copy in gets:
        copy.wait()

    def rows_to_twin(n, slot):
        t = p.near(n)
        s.start(dxb.at[slot], twin_in.at[t], twin + t, p.twin, p.j, p.off, note=False)

    def rows_from_twin(n, slot):
        t = p.near(n)

        @pl.when(p.on)
        def _():
            s.arrive(twin_in.at[t], twin + t)
            twin_in[t] = (twin_in[t].astype(F32) + dxb[slot].astype(F32)).astype(BF16)
        if p.half > 1:
            to_mate = p.on & ((n == 1) | ((n > 1) & p.is_end))
            s.start(twin_in.at[t], mate_in.at[t], mate + t, p.i, p.mate, to_mate, note=False)
        else:
            s.start(twin_in.at[t], fin_in, fin, p.i, t, p.on, fin_send + t, note=False)

    def rows_from_mate(n):
        t = p.near(n)
        here = p.on & p.is_edge

        @pl.when(here)
        def _():
            s.arrive(mate_in.at[t], mate + t)
            mate_in[t] = (mate_in[t].astype(F32) + twin_in[t].astype(F32)).astype(BF16)
        s.start(mate_in.at[t], fin_in, fin, p.i, t, here, fin_send + t, note=False)

    def one(it, gi):
        n = tensor - 1 - it
        t, g = p.near(n), p.near(tensor - 1 - gi)
        step = it * tensor + gi
        slot, x_slot = lax.rem(step, 2), lax.rem(it, 2)
        for copy in step_copies(step, slot):
            copy.wait()

        @pl.when(step + 1 < steps)
        def _():
            for copy in step_copies(step + 1, 1 - slot):
                copy.start()

        @pl.when(gi == 0)
        def _():
            x_copy(it, x_slot).wait()

            pl.when(it + 1 < tensor)(x_copy(it + 1, 1 - x_slot).start)
            dx[...] = jnp.zeros_like(dx)

            @pl.when(it + 1 == tensor)
            def _():
                copy = pltpu.make_async_copy(x_hbm.at[pl.ds(pl.multiple_of(p.block * rows, rows), rows)], x.at[1 - x_slot], local.at[own_sem])
                copy.start()
                copy.wait()

        for h in range(heads):
            cols = slice(h * 128, h * 128 + 128)
            k = kv[slot, :, cols]
            d = do[g, :, cols]
            e = exps[slot, h]
            ds = (e.astype(F32) * (dot(k, d, NT) - r[g, h:h + 1])).astype(BF16)
            dkv[:, cols] = (dot(ds, q[g, :, cols], NN) + dot(e, d, NN)).astype(BF16)
            dqt[g, h] += dot(k, ds, TN)
        dk = dkv[...]
        bias = pl.ds(8 + tensor + g, 1)
        tiny[bias, :width] += colsum(dk)
        dx[...] += dot(dk, w0[0, g], NT)
        wacc[g] += dot(x[x_slot], dk, TN)

        @pl.when(it == tensor - 1)
        def _():
            for h in range(heads):
                cols = slice(h * 128, h * 128 + 128)
                dq = dqt[g, h] * np.float32(HEAD ** -0.5)
                dq = jnp.where(lax.broadcasted_iota(jnp.int32, dq.shape, 0) < HEAD, dq, 0.0)
                dkv[:, cols] = dq.T.astype(BF16)
            dq = dkv[...]
            tiny[bias, width:] = colsum(dq)
            own[...] += dot(dq, w0[1, g], NT)
            gw[1, g] = (dot(x[1 - x_slot], dq, TN) + gw[1, g].astype(F32)).astype(BF16)
            gw[0, g] = wacc[g].astype(BF16)
            for f in tails:
                f.first(tensor - 1 - gi)

        @pl.when(step == 0)
        def _():
            for copy in own_gets + late:
                copy.wait()

        @pl.when((gi == 0) & (it >= 1))
        def _():
            for f in folds:
                for k in range(2, stages):
                    f.add(k, n + 1)
                f.line_first(n + 1)

        @pl.when((gi == 0) & (it >= 2))
        def _():
            if p.half > 1:
                rows_from_mate(n + 2)

        @pl.when(gi == 0)
        def _():
            for f in folds:
                f.add(0, n)

        @pl.when((gi == min(1, tensor - 1)) & (it >= 1))
        def _():
            rows_from_twin(n + 1, 1 - x_slot)

        @pl.when(gi == tensor - 1)
        def _():
            for f in folds:
                f.add(1, n)

        @pl.when((gi == tensor - 1) & (it >= 1))
        def _():
            for f in folds:
                f.line_next(n + 1)

        @pl.when((it == tensor - 1) & (gi >= 1))
        def _():
            for f in tails:
                f.add(0, tensor - gi)

        @pl.when((gi == tensor - 1) & (it < tensor - 1))
        def _():
            pl.when((it >= 2) & p.off)(lambda: s.left(dxb.at[x_slot], twin + p.near(n + 2)))
            dxb[x_slot] = dx[...].astype(BF16)
            rows_to_twin(n, x_slot)

    def body(step, carry):
        one(step // tensor, lax.rem(step, tensor))
        return carry

    lax.fori_loop(0, steps, body, 0)
    last_slot = (tensor - 1) % 2

    @pl.when(p.off)
    def _():
        if tensor > 2:
            s.left(dxb.at[last_slot], twin + p.near(2))
        dxb[last_slot] = dx[...].astype(BF16)
        mate_in[1] = own[...].astype(BF16)
    rows_to_twin(0, last_slot)
    s.start(mate_in.at[1], mate_in.at[0], own_slot, p.twin, p.swap, p.off)

    tiny_at = [0]

    def tiny_step(begin, end):
        k = tiny_at[0]
        if k == len(range((fsdp * tensor).bit_length() - 1)):
            return
        bit = 1 << k
        i, j = (flip(p.i, bit), p.j) if bit < fsdp else (p.i, flip(p.j, bit // fsdp))
        copy = s.copy(tiny, tiny_in.at[k], tiny_slots + k, i, j)
        if begin:
            copy.start()
        if end:
            copy.wait_recv()
            copy.wait_send()
            tiny[...] += tiny_in[k]
            tiny_at[0] += 1

    tiny_step(True, False)
    for f in folds:
        for k in range(2, stages):
            f.add(k, 0)
    for f in tails:
        f.add(0, 0)
    for n in range(tensor)[::-1]:
        for f in tails:
            f.add(1, n)
        if n < tensor - 1:
            for f in tails:
                for k in range(2, stages):
                    f.add(k, n + 1)
                f.line_first(n + 1)
        tiny_step(False, True)
        tiny_step(True, False)
    for f in folds:
        f.result()
    for f in tails:
        for k in range(2, stages):
            f.add(k, 0)
    for n in range(1, tensor)[::-1]:
        for f in tails:
            f.line_next(n)
        tiny_step(False, True)
        tiny_step(True, False)
    while tiny_at[0] < (fsdp * tensor).bit_length() - 1:
        tiny_step(False, True)
        tiny_step(True, False)

    @pl.when(p.on)
    def _():
        s.arrive(twin_in.at[p.j], twin + p.j)
        dx[...] += own[...] + twin_in[p.j].astype(F32)
        if p.half > 1:
            s.arrive(mate_in.at[p.j], mate + p.j)
            dx[...] += mate_in[p.j].astype(F32)

    @pl.when(p.off)
    def _():
        s.arrive(fin_in, fin)
        s.arrive(mate_in.at[0], own_slot)
        dx[...] = fin_in[...].astype(F32) + mate_in[0].astype(F32)
    s.arrive(swapped, swap_slot, p.off)
    for f in tails:
        f.result()
    for n in range(tensor):
        t = p.near(n)
        if n < 2:
            s.left(dxb.at[0], twin + t, p.off)
        if n > 0:
            if p.half > 1:
                s.left(dxb.at[0], mate + t, p.on & ((n == 1) | p.is_end))
                if n > 1:
                    s.left(dxb.at[0], fin_send + t, p.on & p.is_edge)
            else:
                s.left(dxb.at[0], fin_send + t, p.on)
    for f in folds + tails:
        f.finish()
    s.finish()


def last_part(fsdp, tensor, x, w0, kv, q, do, g_o, g, e, resid, low, r, g_bup, g_vecs):
    groups, heads, _, rows = e.shape
    model, width = w0.shape[2:]
    shard = model // fsdp
    bits = fsdp.bit_length() - 1
    vm = lambda d, *shape: pltpu.VMEM(shape, d)
    slots = 4 * ((fsdp - 1) * tensor + 2 * tensor) + 3 * tensor + 16
    scratch = [vm(BF16, 6, fsdp >> (k + 1), tensor, shard, width) for k in range(bits)]
    scratch += [vm(BF16, 6, 2, tensor, shard, width), vm(BF16, 4, tensor, fsdp // 2, shard, width), vm(BF16, 2, rows, model),
                vm(BF16, 2, tensor, model, width), vm(BF16, 2, rows, width), vm(BF16, tensor, rows, width), vm(BF16, tensor, rows, width),
                vm(F32, tensor, heads, 128, rows), vm(F32, tensor, model, width), vm(BF16, 2, heads, rows, rows),
                vm(BF16, 2, tensor, model, width), vm(BF16, rows, width), vm(BF16, 2, rows, model), vm(F32, rows, model), vm(BF16, tensor, rows, model),
                vm(BF16, tensor, rows, model), vm(BF16, rows, model), vm(F32, (fsdp * tensor).bit_length() - 1, 8 + 2 * tensor, model),
                pltpu.SemaphoreType.DMA((slots,)), pltpu.SemaphoreType.DMA((slots,)), pltpu.SemaphoreType.DMA((16 + fsdp,))]
    return pl.pallas_call(
        functools.partial(last_kernel, fsdp, tensor),
        in_specs=[ANY] * 10 + [VM] * 3, out_specs=[VM] * 3 + [ANY],
        out_shape=[jax.ShapeDtypeStruct(s, d) for s, d in [
            ((6, shard, width), F32), ((rows, model), F32), ((8 + 2 * tensor, model), F32), ((rows, model), BF16)]],
        scratch_shapes=scratch,
        compiler_params=pltpu.CompilerParams(collective_id=1, has_side_effects=True, vmem_limit_bytes=65400 * 1024),
    )(x, w0, kv, q, do, g_o, g, e, resid, low, r, g_bup, g_vecs)


def final_kernel(fsdp, tensor, shards, dx, tiny, out, swapped,
                 output, grad_tokens, g_query, g_key, g_value, g_out, g_up, g_down, b_query, b_value, b_up, *vectors):
    p = Place(fsdp, tensor)
    columns, width = g_query.shape[1], shards.shape[2]
    shard = shards.shape[1]
    grad_tokens[...] = dx[...]

    @pl.when(p.on)
    def _():
        output[...] = out[...]

    @pl.when(p.off)
    def _():
        output[...] = swapped[...].astype(F32)
    heads = [(h, slice(h * HEAD, h * HEAD + HEAD), slice(2 * h * HEAD, 2 * h * HEAD + 2 * HEAD)) for h in range(columns // HEAD)]
    out_rows = []
    for h, cols, both in heads:
        keys, query = shards[0, :, both], shards[1, :, both]
        g_key[:, cols], g_value[:, cols] = keys[:, :HEAD], keys[:, HEAD:]
        g_query[:, cols] = query[:, :HEAD]
        out_rows.append(query[:, HEAD:])
    g_out[...] = jnp.concatenate(out_rows, 1).T
    for k in range(2):
        cols = slice(k * width, k * width + width)
        g_up[:, cols] = shards[2 + 2 * k]
        g_down[:, cols] = shards[3 + 2 * k]

    def take(row, ones):
        return lax.dot_general(row, ones, ((NT[:1], NT[1:]), ((), ())), precision=lax.Precision.HIGHEST, preferred_element_type=F32)

    few, many = columns // fsdp, 2 * width // fsdp
    both = tiny[pl.ds(8 + tensor + p.j, 1), :]
    b_query[...] = take(both[:, width:], spread(head_lanes(False), few, p.i, 0, width))
    b_value[...] = take(both[:, :width], spread(head_lanes(True), few, p.i, 0, width))
    b_up[...] = take(tiny[pl.ds(8 + p.j, 1), :], spread(lambda lane: lane, many, p.i, 0, 2 * width))
    rows = take(tiny[:8], spread(lambda lane: lane, shard, p.i, 0, shard * fsdp))
    for k, vector in enumerate(vectors):
        vector[...] = rows[k:k + 1]


def final_part(fsdp, tensor, shards, dx, tiny, out, swapped):
    _, shard, width = shards.shape
    rows, model = dx.shape
    columns = width // 2
    flat, square = (rows, model), (shard, columns)
    results = pl.pallas_call(
        functools.partial(final_kernel, fsdp, tensor),
        in_specs=[VM] * 5, out_specs=[VM] * 17,
        out_shape=[jax.ShapeDtypeStruct(s, F32) for s in [
            flat, flat, square, square, square, (columns, shard), (shard, 2 * width), (shard, 2 * width),
            (1, columns // fsdp), (1, columns // fsdp), (1, 2 * width // fsdp)] + [(1, shard)] * 6],
        compiler_params=pltpu.CompilerParams(vmem_limit_bytes=VMEM_LIMIT),
    )(shards, dx, tiny, out, swapped)
    return (*results[:7], results[7].T, *[r.reshape(-1) for r in results[8:]])


def normalize(values, gain, shift):
    average = jnp.mean(values, -1, keepdims=True)
    centered = values - average
    inverse = lax.rsqrt(jnp.mean(centered * centered, -1, keepdims=True) + EPSILON)
    return centered * inverse * gain + shift


def exact_gelu(values):
    return jax.nn.gelu(values, approximate=False)


def outer_sum(left, right):
    return dot(left, right, TN)


def times_transposed(left, right):
    return dot(left, right, NT)


def plain(
    tokens,
    cotangent,
    w_query,
    w_key,
    w_value,
    w_out,
    w_up,
    w_down,
    b_query,
    b_value,
    b_up,
    b_out,
    b_down,
    gain_attn,
    shift_attn,
    gain_ffn,
    shift_ffn,
):
    gathered = (
        lax.all_gather(w_query, "fsdp", axis=0, tiled=True),
        lax.all_gather(w_key, "fsdp", axis=0, tiled=True),
        lax.all_gather(w_value, "fsdp", axis=0, tiled=True),
        lax.all_gather(w_out, "fsdp", axis=1, tiled=True),
        lax.all_gather(w_up, "fsdp", axis=0, tiled=True),
        lax.all_gather(w_down, "fsdp", axis=1, tiled=True),
        lax.all_gather(b_query, "fsdp", axis=0, tiled=True),
        lax.all_gather(b_value, "fsdp", axis=0, tiled=True),
        lax.all_gather(b_up, "fsdp", axis=0, tiled=True),
        lax.all_gather(b_out, "fsdp", axis=0, tiled=True),
        lax.all_gather(b_down, "fsdp", axis=0, tiled=True),
        lax.all_gather(gain_attn, "fsdp", axis=0, tiled=True),
        lax.all_gather(shift_attn, "fsdp", axis=0, tiled=True),
        lax.all_gather(gain_ffn, "fsdp", axis=0, tiled=True),
        lax.all_gather(shift_ffn, "fsdp", axis=0, tiled=True),
    )
    (
        query_weight,
        key_weight,
        value_weight,
        out_weight,
        up_weight,
        down_weight,
        query_bias,
        value_bias,
        up_bias,
        out_bias,
        down_bias,
        attn_gain,
        attn_shift,
        ffn_gain,
        ffn_shift,
    ) = gathered
    own_rows = tokens.shape[0]
    seq_len = own_rows * lax.axis_size("tensor")
    heads = query_weight.shape[1] // HEAD
    span = min(512, seq_len)
    blocks = seq_len // span
    scale = HEAD ** (-0.5)
    full_tokens = lax.all_gather(tokens, "tensor", axis=0, tiled=True)
    query = (
        jnp.dot(full_tokens, query_weight, preferred_element_type=jnp.float32)
        + query_bias.astype(jnp.float32)
    ).astype(jnp.bfloat16)
    keys = jnp.dot(full_tokens, key_weight, preferred_element_type=jnp.float32).astype(jnp.bfloat16)
    values = (
        jnp.dot(full_tokens, value_weight, preferred_element_type=jnp.float32)
        + value_bias.astype(jnp.float32)
    ).astype(jnp.bfloat16)
    query_blocks = query.reshape(blocks, span, heads, HEAD)
    key_heads = keys.reshape(seq_len, heads, HEAD)
    value_heads = values.reshape(seq_len, heads, HEAD)

    def scores_of(piece):
        return (
            jnp.einsum("qhd,khd->hqk", piece, key_heads, preferred_element_type=jnp.float32) * scale
        )

    def forward_block(piece):
        scores = scores_of(piece)
        largest = jnp.max(scores, -1, keepdims=True)
        exponent = jnp.exp(scores - largest)
        total = jnp.sum(exponent, -1, keepdims=True)
        soft_low = (exponent / total).astype(jnp.bfloat16)
        result = jnp.einsum(
            "hqk,khd->qhd", soft_low, value_heads, preferred_element_type=jnp.float32
        )
        return (result.astype(jnp.bfloat16), largest, total)

    attended, largest_all, total_all = lax.map(forward_block, query_blocks)
    attended = attended.reshape(seq_len, heads * HEAD)
    attn_part = lax.psum_scatter(
        jnp.dot(attended, out_weight, preferred_element_type=jnp.float32).astype(jnp.bfloat16),
        "tensor",
        scatter_dimension=0,
        tiled=True,
    ).astype(jnp.float32)
    resid_attn = tokens.astype(jnp.float32) + (attn_part + out_bias.astype(jnp.float32))
    hidden, attn_norm_back = jax.vjp(
        normalize, resid_attn, attn_gain.astype(jnp.float32), attn_shift.astype(jnp.float32)
    )
    full_hidden = lax.all_gather(hidden.astype(jnp.bfloat16), "tensor", axis=0, tiled=True)
    pre_act = jnp.dot(full_hidden, up_weight, preferred_element_type=jnp.float32) + up_bias.astype(
        jnp.float32
    )
    activ, gelu_back = jax.vjp(exact_gelu, pre_act)
    activ_low = activ.astype(jnp.bfloat16)
    ffn_part = lax.psum_scatter(
        jnp.dot(activ_low, down_weight, preferred_element_type=jnp.float32).astype(jnp.bfloat16),
        "tensor",
        scatter_dimension=0,
        tiled=True,
    ).astype(jnp.float32)
    resid_ffn = hidden + (ffn_part + down_bias.astype(jnp.float32))
    output, ffn_norm_back = jax.vjp(
        normalize, resid_ffn, ffn_gain.astype(jnp.float32), ffn_shift.astype(jnp.float32)
    )
    matrices = (
        lax.all_gather(w_query, "fsdp", axis=0, tiled=True),
        lax.all_gather(w_key, "fsdp", axis=0, tiled=True),
        lax.all_gather(w_value, "fsdp", axis=0, tiled=True),
        lax.all_gather(w_out, "fsdp", axis=1, tiled=True),
        lax.all_gather(w_up, "fsdp", axis=0, tiled=True),
        lax.all_gather(w_down, "fsdp", axis=1, tiled=True),
    )
    back_query, back_key, back_value, back_out, back_up, back_down = matrices
    grad_resid_ffn, grad_gain_ffn, grad_shift_ffn = ffn_norm_back(cotangent.astype(jnp.float32))
    grad_ffn_full = lax.all_gather(
        grad_resid_ffn.astype(jnp.bfloat16), "tensor", axis=0, tiled=True
    )
    grad_down_bias = jnp.sum(grad_ffn_full, 0, dtype=jnp.float32)
    grad_down_weight = outer_sum(activ_low, grad_ffn_full)
    grad_activ = times_transposed(grad_ffn_full, back_down)
    grad_pre = gelu_back(grad_activ)[0].astype(jnp.bfloat16)
    grad_up_bias = jnp.sum(grad_pre, 0, dtype=jnp.float32)
    grad_up_weight = outer_sum(full_hidden, grad_pre)
    grad_hidden = grad_resid_ffn + lax.psum_scatter(
        times_transposed(grad_pre, back_up).astype(jnp.bfloat16),
        "tensor",
        scatter_dimension=0,
        tiled=True,
    ).astype(jnp.float32)
    grad_resid_attn, grad_gain_attn, grad_shift_attn = attn_norm_back(grad_hidden)
    grad_attn_full = lax.all_gather(
        grad_resid_attn.astype(jnp.bfloat16), "tensor", axis=0, tiled=True
    )
    grad_out_bias = jnp.sum(grad_attn_full, 0, dtype=jnp.float32)
    grad_out_weight = outer_sum(attended, grad_attn_full)
    grad_attended = times_transposed(grad_attn_full, back_out).astype(jnp.bfloat16)
    grad_blocks = grad_attended.reshape(blocks, span, heads, HEAD)

    def backward_block(carry, item):
        piece, grad_piece, largest, total = item
        soft = jnp.exp(scores_of(piece) - largest) / total
        soft_low = soft.astype(jnp.bfloat16)
        grad_soft = jnp.einsum(
            "qhd,khd->hqk", grad_piece, value_heads, preferred_element_type=jnp.float32
        )
        inner = jnp.sum(soft * grad_soft, -1, keepdims=True)
        grad_scores = (soft * (grad_soft - inner)).astype(jnp.bfloat16)
        grad_query_block = (
            jnp.einsum("hqk,khd->qhd", grad_scores, key_heads, preferred_element_type=jnp.float32)
            * scale
        )
        grad_key_sum = (
            carry[0]
            + jnp.einsum("hqk,qhd->khd", grad_scores, piece, preferred_element_type=jnp.float32)
            * scale
        )
        grad_value_sum = carry[1] + jnp.einsum(
            "hqk,qhd->khd", soft_low, grad_piece, preferred_element_type=jnp.float32
        )
        return ((grad_key_sum, grad_value_sum), grad_query_block.astype(jnp.bfloat16))

    zeros = jnp.zeros((seq_len, heads, HEAD), jnp.float32)
    (grad_key_sum, grad_value_sum), grad_query = lax.scan(
        backward_block, (zeros, zeros), (query_blocks, grad_blocks, largest_all, total_all)
    )
    grad_query = grad_query.reshape(seq_len, heads * HEAD)
    grad_keys = grad_key_sum.reshape(seq_len, heads * HEAD).astype(jnp.bfloat16)
    grad_values = grad_value_sum.reshape(seq_len, heads * HEAD).astype(jnp.bfloat16)
    grad_query_bias = jnp.sum(grad_query, 0, dtype=jnp.float32)
    grad_value_bias = jnp.sum(grad_values, 0, dtype=jnp.float32)
    grad_query_weight = outer_sum(full_tokens, grad_query)
    grad_key_weight = outer_sum(full_tokens, grad_keys)
    grad_value_weight = outer_sum(full_tokens, grad_values)
    token_terms = (
        times_transposed(grad_query, back_query)
        + times_transposed(grad_keys, back_key)
        + times_transposed(grad_values, back_value)
    )
    norm_terms = jnp.tile(
        jnp.stack([grad_gain_attn, grad_shift_attn, grad_gain_ffn, grad_shift_ffn]),
        (lax.axis_size("tensor"), 1),
    )
    token_part, norm_sums = (
        lax.psum_scatter(
            token_terms.astype(jnp.bfloat16), "tensor", scatter_dimension=0, tiled=True
        ).astype(jnp.float32),
        lax.psum_scatter(
            norm_terms.astype(jnp.bfloat16), "tensor", scatter_dimension=0, tiled=True
        ).astype(jnp.float32),
    )
    grad_tokens = grad_resid_attn + token_part
    shards = (
        lax.psum_scatter(grad_query_weight, "fsdp", scatter_dimension=0, tiled=True),
        lax.psum_scatter(grad_key_weight, "fsdp", scatter_dimension=0, tiled=True),
        lax.psum_scatter(grad_value_weight, "fsdp", scatter_dimension=0, tiled=True),
        lax.psum_scatter(grad_out_weight, "fsdp", scatter_dimension=1, tiled=True),
        lax.psum_scatter(grad_up_weight, "fsdp", scatter_dimension=0, tiled=True),
        lax.psum_scatter(grad_down_weight, "fsdp", scatter_dimension=1, tiled=True),
        lax.psum_scatter(grad_query_bias, "fsdp", scatter_dimension=0, tiled=True),
        lax.psum_scatter(grad_value_bias, "fsdp", scatter_dimension=0, tiled=True),
        lax.psum_scatter(grad_up_bias, "fsdp", scatter_dimension=0, tiled=True),
        lax.psum_scatter(grad_out_bias, "fsdp", scatter_dimension=0, tiled=True),
        lax.psum_scatter(grad_down_bias, "fsdp", scatter_dimension=0, tiled=True),
        lax.psum_scatter(norm_sums[0], "fsdp", scatter_dimension=0, tiled=True),
        lax.psum_scatter(norm_sums[1], "fsdp", scatter_dimension=0, tiled=True),
        lax.psum_scatter(norm_sums[2], "fsdp", scatter_dimension=0, tiled=True),
        lax.psum_scatter(norm_sums[3], "fsdp", scatter_dimension=0, tiled=True),
    )
    return (
        output,
        grad_tokens,
        shards[0],
        shards[1],
        shards[2],
        shards[3],
        shards[4],
        shards[5],
        shards[6],
        shards[7],
        shards[8],
        shards[9],
        shards[10],
        shards[11],
        shards[12],
        shards[13],
        shards[14],
    )


def fits(tokens, w_query, w_up):
    fsdp, tensor = lax.axis_size("fsdp"), lax.axis_size("tensor")
    shard, columns = w_query.shape
    return (tensor == 4 and fsdp >= 4 and fsdp & (fsdp - 1) == 0 and shard % 16 == 0 and 4 * columns == tokens.shape[1] and columns >= 3 * HEAD and columns % HEAD == 0
            and w_up.shape[1] == 4 * columns and tokens.shape[0] % 128 == 0)


def layer(tokens, cotangent, w_query, w_key, w_value, w_out, w_up, w_down, b_query, b_value, b_up, b_out, b_down,
          gain_attn, shift_attn, gain_ffn, shift_ffn):
    if not fits(tokens, w_query, w_up):
        return plain(tokens, cotangent, w_query, w_key, w_value, w_out, w_up, w_down, b_query, b_value, b_up, b_out, b_down,
                     gain_attn, shift_attn, gain_ffn, shift_ffn)
    fsdp, tensor = lax.axis_size("fsdp"), lax.axis_size("tensor")
    pieces = (b_query, b_value, b_up, b_out, b_down, gain_attn, shift_attn, gain_ffn, shift_ffn)
    total, at, vectors = sum(piece.size for piece in pieces), 0, 0.0
    for piece in pieces:
        vectors += jnp.pad(piece.reshape(1, -1), ((0, 0), (at, total - at - piece.size)))
        at += piece.size
    w0, w1, x, x_own, cot, kv, q, att, exps, inv, smalls = first_part(
        fsdp, tensor, w_query, w_key, w_value, w_out, w_up, w_down.T, vectors, tokens, cotangent)
    out, low, resid, r, do, g_o, g, g_bup, g_vecs = middle_part(x_own, cot, att, w0, w1, smalls, inv)
    shards, grad_tokens, tiny, swapped = last_part(fsdp, tensor, x, w0, kv, q, do, g_o, g, exps, resid, low, r, g_bup, g_vecs)
    return final_part(fsdp, tensor, shards, grad_tokens, tiny, out, swapped)


def solution(mesh):
    return jax.shard_map(
        layer,
        mesh=mesh,
        in_specs=(
            P(("fsdp", "tensor"), None),
            P(("fsdp", "tensor"), None),
            P("fsdp", "tensor"),
            P("fsdp", "tensor"),
            P("fsdp", "tensor"),
            P("tensor", "fsdp"),
            P("fsdp", "tensor"),
            P("tensor", "fsdp"),
            P(("tensor", "fsdp")),
            P(("tensor", "fsdp")),
            P(("tensor", "fsdp")),
            P("fsdp"),
            P("fsdp"),
            P("fsdp"),
            P("fsdp"),
            P("fsdp"),
            P("fsdp"),
        ),
        out_specs=(
            P(("fsdp", "tensor"), None),
            P(("fsdp", "tensor"), None),
            P("fsdp", "tensor"),
            P("fsdp", "tensor"),
            P("fsdp", "tensor"),
            P("tensor", "fsdp"),
            P("fsdp", "tensor"),
            P("tensor", "fsdp"),
            P(("tensor", "fsdp")),
            P(("tensor", "fsdp")),
            P(("tensor", "fsdp")),
            P("fsdp"),
            P("fsdp"),
            P("fsdp"),
            P("fsdp"),
            P("fsdp"),
            P("fsdp"),
        ),
        check_vma=False,
    )
```
